32 devices in a mesh: box: 8 (over z, y), col: 4 (over x, core).
Axes of the slice: x: 2, y: 2, z: 4, core: 2. Of those that a mesh axis runs over, the one named last changes fastest.
Arguments:
- box_points: float32 [16, 3, 512], P('box'), may hold values from 0 to 1
- proxy_directions: float32 [3, 1024], P(None, 'col'), may hold values from -1 to 1, as said below
- point_order: int32 [16, 512], P('box'), may hold values from 0 to 511, each once within a row
- neighbour_boxes: int32 [16, 8], P('box'), may hold values from 0 to 15, as said below
- neighbour_places: int32 [16, 8], P('box'), may hold values from 0 to 25
- pivot_inverse: float32 [16, 2, 256], P('box', None, 'col'), may hold values from -6 to 6
Outputs:
- interpolation: float32 [16, 2, 256, 256], P('box', None, None, 'col')
- skeleton_update: float32 [16, 2, 256, 256], P('box', None, 'col')
The draws below stay inside these ranges and needn't reach their ends.
Inputs may be any that keep to these rules, and one draw needn't show every extreme that they name: `neighbour_boxes`: box g is held by index g // 2 of the box axis. Every entry names a box of the same index or of the index just before or just after it, cyclically. Of the 16 entries of one index's boxes exactly half name boxes of that same index, never the listing box itself; a box may be listed twice in one row. `proxy_directions`: unit vectors.
All inputs are finite; a program needn't handle non-finite values.
Results may differ from the reference program's by a relative error of at most 0.0038.
Values sent between devices are 32-bit elements; how exact they have to be, the bound alone decides.
A program may use at most 64 MiB of HBM per device.

```python
import math
import jax
import jax.numpy as jnp
from jax import lax

P_SIZE = 512
S = 256
PROXY = 1024
NB = 8
BOX_DEV = 2
R = 256
BOXES = 16


def draw_proxy_directions(key, part):
    samples = jax.random.normal(key, (3, PROXY), jnp.float32)
    length = jnp.sqrt(jnp.sum(samples * samples, axis=0, keepdims=True)) + 1e-06
    return samples / length


def draw_neighbour_boxes(key, part):
    device_count = BOXES // BOX_DEV
    entries = BOX_DEV * NB
    key_list = jax.random.split(jax.random.fold_in(key, 17), 4)
    places = jax.vmap(lambda one_key: jax.random.permutation(one_key, entries))(jax.random.split(key_list[0], device_count))
    side_sign = 2 * jax.random.randint(key_list[1], (device_count, entries), 0, 2) - 1
    entry_rank = jnp.arange(entries, dtype=jnp.int32)[None, :]
    own_side = entry_rank < entries // 2
    device_step = jnp.where(own_side, 0, side_sign)
    home_box = places // NB
    own_slot = (home_box + 1 + jax.random.randint(key_list[2], (device_count, entries), 0, BOX_DEV - 1)) % BOX_DEV
    far_slot = jax.random.randint(key_list[3], (device_count, entries), 0, BOX_DEV)
    chosen_slot = jnp.where(own_side, own_slot, far_slot)
    device_rank = jnp.arange(device_count, dtype=jnp.int32)[:, None]
    target = (device_rank + device_step) % device_count * BOX_DEV + chosen_slot
    neighbour_table = jnp.zeros((device_count, entries), jnp.int32).at[device_rank, places].set(target.astype(jnp.int32))
    return neighbour_table.reshape(BOXES, NB)


def place_ends(values, rng, smallest, high):
    longest = values.shape.index(max(values.shape))
    spots = []
    for shift in (0, 1):
        where = [jax.random.randint(jax.random.fold_in(rng, axis), (), 0, length) for axis, length in enumerate(values.shape)]
        where[longest] = (where[longest] + shift) % values.shape[longest]
        spots.append(tuple(where))
    return values.at[spots[0]].set(smallest).at[spots[1]].set(high)


def steps_of(stream_key, dims, shards, least, high):
    level = 1.0
    for position, parts in shards:
        steps = jax.random.uniform(jax.random.fold_in(jax.random.fold_in(stream_key, 6), position), (parts,), jnp.float32, least / len(shards), high / len(shards))
        level = level * jnp.repeat(jnp.exp(steps), dims[position] // parts).reshape((-1,) + (1,) * (len(dims) - 1 - position))
    return level


def noise(rng, shape, scale, limit, pieces=(), kind=jnp.bfloat16):
    array = jax.random.normal(rng, shape, jnp.float32) * scale
    if len(pieces) > 0:
        array = steps_of(rng, shape, pieces, -0.22, 0.18) * array
    return jnp.clip(array, min=-limit, max=limit).astype(kind)


def setup_inputs(seed: int = 0) -> dict:
    key_of = jax.random.split(jax.random.key(seed), 7)
    box_points = jnp.clip(1.0 * jax.random.uniform(key_of[0], (BOXES, 3, P_SIZE), jnp.float32) ** steps_of(key_of[0], (BOXES, 3, P_SIZE), ((0, 8),), -0.2, 0.2), 0.0, 1.0)
    proxy_directions = draw_proxy_directions(jax.random.fold_in(key_of[6], 71), 0)
    point_order = jax.vmap(lambda own: jax.random.permutation(own, P_SIZE))(jax.random.split(key_of[2], BOXES)).reshape((BOXES, P_SIZE)).astype(jnp.int32)
    neighbour_boxes = draw_neighbour_boxes(jax.random.fold_in(key_of[6], 71), 0)
    neighbour_places = place_ends(jax.random.randint(key_of[4], (BOXES, NB), 0, 26), jax.random.fold_in(key_of[4], 1), 0, 25).astype(jnp.int32)
    pivot_inverse = noise(key_of[5], (BOXES, 2, R), 1.0, 6.0, ((0, 8), (2, 4)), jnp.float32)
    return {"box_points": box_points, "proxy_directions": proxy_directions, "point_order": point_order, "neighbour_boxes": neighbour_boxes, "neighbour_places": neighbour_places, "pivot_inverse": pivot_inverse}


wavenumber = 4.0 * math.pi
softening = 0.05
proxy_radius = 1.5
ridge_share = 0.05
highest = lax.Precision.HIGHEST

def helmholtz(targets, sources):
    distance_sq = jnp.zeros((targets.shape[1], sources.shape[1]), targets.dtype)
    for axis_id in range(3):
        difference = targets[axis_id][:, None] - sources[axis_id][None, :]
        distance_sq = distance_sq + difference * difference
    radius = jnp.sqrt(distance_sq + softening * softening)
    amplitude = 1.0 / (4.0 * math.pi * radius)
    return (amplitude * jnp.cos(wavenumber * radius), amplitude * jnp.sin(wavenumber * radius))

def decode(place_codes):
    full_code = place_codes + (place_codes >= 13).astype(jnp.int32)
    return jnp.stack([full_code // 9 - 1, full_code // 3 % 3 - 1, full_code % 3 - 1], axis=-1).astype(jnp.float32)

def cross_products(real_tile, imag_tile, skel_count):
    stacked = jnp.concatenate([real_tile, imag_tile], axis=0)
    flipped = jnp.concatenate([imag_tile, -real_tile], axis=0)
    left_cols = stacked[:, :skel_count]
    contract = (((0,), (0,)), ((), ()))
    real_cross = lax.dot_general(left_cols.astype(jnp.float32), stacked.astype(jnp.float32), contract, preferred_element_type=jnp.float32)
    imag_cross = lax.dot_general(left_cols.astype(jnp.float32), flipped.astype(jnp.float32), contract, preferred_element_type=jnp.float32)
    return jnp.stack([real_cross, imag_cross])

def factor(gram_block):
    real_gram = gram_block[0]
    imag_gram = gram_block[1]
    skel_count = real_gram.shape[0]
    ridge_value = ridge_share * jnp.trace(real_gram) / skel_count
    real_gram = real_gram + ridge_value * jnp.eye(skel_count, dtype=real_gram.dtype)
    upper_half = jnp.concatenate([real_gram, -imag_gram], axis=1)
    lower_half = jnp.concatenate([imag_gram, real_gram], axis=1)
    return jnp.linalg.cholesky(jnp.concatenate([upper_half, lower_half], axis=0))

def apply_inverse(cholesky_factor, right_side):
    stacked = right_side.reshape(2 * right_side.shape[1], right_side.shape[2])
    forward = lax.linalg.triangular_solve(cholesky_factor, stacked, left_side=True, lower=True)
    backward = lax.linalg.triangular_solve(cholesky_factor, forward, left_side=True, lower=True, transpose_a=True)
    return backward.reshape(right_side.shape)

def pair_update(near_points, own_columns, coefficients, pivot_row):
    skel_count = coefficients.shape[1]
    real_kernel, imag_kernel = helmholtz(near_points, own_columns)
    real_skel = real_kernel[:, :skel_count]
    imag_skel = imag_kernel[:, :skel_count]
    real_rest = real_kernel[:, skel_count:]
    imag_rest = imag_kernel[:, skel_count:]
    matmul_dims = (((1,), (0,)), ((), ()))
    outer_dims = (((1,), (1,)), ((), ()))

    def product(left_side, right_side):
        return lax.dot_general(left_side.astype(jnp.float32), right_side.astype(jnp.float32), matmul_dims, precision=highest, preferred_element_type=jnp.float32)

    def outer_product(left_side, right_side):
        return lax.dot_general(left_side.astype(jnp.float32), right_side.astype(jnp.float32), outer_dims, precision=highest, preferred_element_type=jnp.float32)
    real_block = real_rest - (product(real_skel, coefficients[0]) - product(imag_skel, coefficients[1]))
    imag_block = imag_rest - (product(real_skel, coefficients[1]) + product(imag_skel, coefficients[0]))
    real_weighted = real_block * pivot_row[0][None, :] - imag_block * pivot_row[1][None, :]
    imag_weighted = real_block * pivot_row[1][None, :] + imag_block * pivot_row[0][None, :]
    real_update = outer_product(real_weighted, real_block) - outer_product(imag_weighted, imag_block)
    imag_update = outer_product(real_weighted, imag_block) + outer_product(imag_weighted, real_block)
    return -jnp.stack([real_update, imag_update])

def reference(box_points, proxy_directions, point_order, neighbour_boxes, neighbour_places, pivot_inverse):
    ordered = jnp.take_along_axis(box_points, jnp.broadcast_to(point_order[:, None, :], box_points.shape), axis=2)
    shift_table = decode(neighbour_places)
    proxies = 0.5 + proxy_radius * proxy_directions

    def interp_one(which_box):
        own_points = ordered[which_box]
        near_points = ordered[neighbour_boxes[which_box]] + shift_table[which_box][:, :, None]
        near_points = jnp.transpose(near_points, (1, 0, 2)).reshape(3, NB * P_SIZE)
        targets = jnp.concatenate([proxies, near_points], axis=1)
        real_tile, imag_tile = helmholtz(targets, own_points)
        cross_terms = cross_products(real_tile.astype(jnp.bfloat16), imag_tile.astype(jnp.bfloat16), S)
        cholesky_factor = factor(cross_terms[:, :, :S])
        return apply_inverse(cholesky_factor, cross_terms[:, :, S:])
    interpolation = lax.map(interp_one, jnp.arange(BOXES, dtype=jnp.int32))

    def schur_box(which_box, running):
        own_points = ordered[which_box]
        near_points = ordered[neighbour_boxes[which_box]][:, :, :S] + shift_table[which_box][:, :, None]
        coefficients = interpolation[which_box]
        pivot_row = pivot_inverse[which_box]
        updates = jax.vmap(lambda points_one: pair_update(points_one, own_points, coefficients, pivot_row))(near_points)
        return running.at[neighbour_boxes[which_box]].add(updates)
    skeleton_update = lax.fori_loop(0, BOXES, schur_box, jnp.zeros((BOXES, 2, S, S), jnp.float32))
    return (interpolation, skeleton_update)
```

```python
import functools
import math

import jax
import jax.numpy as jnp
from jax import lax
from jax.experimental import pallas as pl
from jax.experimental.pallas import tpu as pltpu
from jax.sharding import PartitionSpec as P

softening = 0.05
proxy_radius = 1.5
ridge_share = 0.05
highest = lax.Precision.HIGHEST
NBLK = 32
BLOCK = 256
ROWS = 16
DEPTH = 64

SIN = (4.44287959, -7.30781805, 3.59778873, -0.79123822)
COS_TILE = (1.41420408, -6.97764206, 5.7152384, -1.72834866)
COS = (1.4142135381698608, -6.978850841522217, 5.739460468292236, -1.883557915687561, 0.3106880187988281)

HBM = pl.BlockSpec(memory_space=pltpu.HBM)
VMEM = pl.BlockSpec(memory_space=pltpu.VMEM)
SMEM = pl.BlockSpec(memory_space=pltpu.SMEM)
MESH = pl.DeviceIdType.MESH
F32 = jnp.float32
BF16 = jnp.bfloat16


def params(**more):
    return pltpu.CompilerParams(vmem_limit_bytes=24 * 1024 * 1024, **more)


def horner(coefficients, z):
    total = coefficients[-1] * z + coefficients[-2]
    for one in coefficients[-3::-1]:
        total = total * z + one
    return total


def kernel_values(square, cosine):
    inverse = lax.rsqrt(square)
    turns = square * inverse
    part = turns - jnp.floor(turns + 0.5)
    z = part * part
    amplitude = inverse * (1.0 / (2.0 * math.pi))
    sine = part * horner(SIN, z)
    scaled = amplitude * sine
    return amplitude - scaled * sine, scaled * horner(cosine, z)


def three(x):
    high = x.astype(BF16).astype(F32)
    rest = x - high
    mid = rest.astype(BF16).astype(F32)
    return high, mid, rest - mid


def row_three(block, row):
    third = lax.broadcasted_iota(jnp.int32, block.shape, 0) == 3
    return jnp.where(third, row, block)


def norm_of(points):
    return jnp.sum(points * points, axis=0, keepdims=True)


def stacked(groups):
    zero = jnp.zeros_like(groups[0])
    return jnp.concatenate(groups + [zero] * (DEPTH // 8 - len(groups)), axis=0).astype(BF16)


def target_rows(points):
    high, mid, low = three(points)
    n_high, n_mid, n_low = three(norm_of(points))
    return stacked([row_three(high, n_high), row_three(high, n_mid), row_three(mid, n_low),
                    row_three(high, 1.0), row_three(mid, 1.0), row_three(low, 1.0)])


def source_rows(points):
    high, mid, low = three(points)
    norm = norm_of(points) + 4.0 * softening * softening
    n_high, n_mid, n_low = three(norm)
    return stacked([row_three(-2.0 * high, 1.0), row_three(-2.0 * mid, 1.0),
                    row_three(-2.0 * high, 1.0), row_three(-2.0 * low, n_high),
                    row_three(-2.0 * mid, n_mid), row_three(-2.0 * high, n_low)])


def three_rows(points):
    rows = lax.broadcasted_iota(jnp.int32, points.shape, 0)
    return jnp.where(rows < 3, points, 0.0)


def shifted(points, code):
    code = jnp.where(code >= 13, code + 1, code)
    axis_row = lax.broadcasted_iota(jnp.int32, points.shape, 0)
    move = jnp.where(
        axis_row == 0,
        (code // 9 - 1).astype(F32),
        jnp.where(axis_row == 1, ((code // 3) % 3 - 1).astype(F32), (code % 3 - 1).astype(F32)),
    )
    return three_rows(2.0 * (points + (move - 0.5)))


def centred(points):
    return three_rows(2.0 * (points - 0.5))


def slot_of(nb_ref, row, entry, box_count, box_total):
    owner_box = nb_ref[row, entry]
    step = owner_box // box_count - lax.axis_index("box") + 1
    step = jnp.where(step < 0, step + box_total, step)
    step = jnp.where(step >= box_total, step - box_total, step)
    return step * box_count + owner_box % box_count


def dot_tn(a, b):
    return lax.dot_general(a, b, (((0,), (0,)), ((), ())), preferred_element_type=F32)


def meet(peers):
    barrier = pltpu.get_barrier_semaphore()
    for peer in peers:
        pl.semaphore_signal(barrier, inc=1, device_id=peer, device_id_type=MESH)
    return lambda: pl.semaphore_wait(barrier, len(peers))


def send(source, target, sends, recvs, index, peer):
    one = pltpu.make_async_remote_copy(
        src_ref=source, dst_ref=target, send_sem=sends.at[index], recv_sem=recvs.at[index],
        device_id=peer, device_id_type=MESH)
    one.start()
    return one


def exchange_kernel(box_total, col_count, group, skeleton, points_ref, order_ref, proxy_ref,
                    pivot_ref, points_out, proxy_out, pivot_out, points, order, sends, recvs,
                    local):
    me = lax.axis_index("col")
    place = lax.axis_index("box")
    box_count, _, count = points_ref.shape
    after = {"box": lax.rem(place + 1, box_total)}
    before = {"box": lax.rem(place + box_total - 1, box_total)}
    across = {"col": lax.rem(me + group, col_count)}
    mine = me // group
    own = ((points_ref, points), (order_ref, order), (proxy_ref, proxy_out.at[0]),
           (pivot_ref, pivot_out.at[mine]))
    loads = []
    for i, (source, target) in enumerate(own):
        copy = pltpu.make_async_copy(source, target, local.at[i])
        copy.start()
        loads.append(copy)
    arrived = meet([before, after, across])
    for copy in loads:
        copy.wait()
    width = (count - skeleton) // col_count
    for box in range(box_count):
        row = order[box:box + 1, :]
        strips = [row[:, skeleton + s * width:skeleton + (s + 1) * width]
                  for c in range(group) for s in range(c, col_count, group)]
        row = jnp.concatenate([row[:, 0:skeleton]] + strips, axis=1)
        one_hot = (lax.broadcasted_iota(jnp.int32, (count, count), 0) == row).astype(F32)
        whole = jnp.concatenate([points[box], jnp.zeros((5, count), F32)], axis=0)
        rows = jnp.concatenate(list(three(whole)) + [jnp.zeros_like(whole)], axis=0)
        picked = jnp.dot(rows.astype(BF16), one_hot.astype(BF16), preferred_element_type=F32)
        points_out[1, box] = (picked[0:8] + picked[8:16]) + picked[16:24]
    arrived()
    jobs = [
        send(points_out.at[1], points_out.at[0], sends, recvs, 0, after),
        send(points_out.at[1], points_out.at[2], sends, recvs, 1, before),
        send(proxy_ref, proxy_out.at[1], sends, recvs, 2, across),
        send(pivot_ref, pivot_out.at[mine], sends, recvs, 3, across),
    ]
    for copy in jobs:
        copy.wait()


def tile_kernel(box_total, entries, group, skeleton, nb_hbm, place_hbm, points_ref, proxy_ref,
                gram_ref, rest_ref, nb_ref, place_ref, targets, sources, tiles, total, local):
    count = points_ref.shape[3]
    box_count, _, share = proxy_ref.shape
    proxies = box_count * share
    me = lax.axis_index("col")
    box = me // group
    first = lax.rem(me, group) * entries
    loads = [pltpu.make_async_copy(nb_hbm, nb_ref, local.at[0]),
             pltpu.make_async_copy(place_hbm, place_ref, local.at[1])]
    for copy in loads:
        copy.start()
    sources[...] = source_rows(centred(points_ref[1, box]))
    for d in range(box_count):
        directions = jnp.concatenate([proxy_ref[d], jnp.zeros((5, share), F32)], axis=0)
        targets[:, d * share:(d + 1) * share] = target_rows((2.0 * proxy_radius) * directions)
    for copy in loads:
        copy.wait()
    for k in range(entries):
        slot = slot_of(nb_ref, box, first + k, box_count, box_total)
        here = shifted(points_ref[slot // box_count, slot % box_count], place_ref[box, first + k])
        targets[:, proxies + k * count:proxies + (k + 1) * count] = target_rows(here)
    block = tiles.shape[1] // 2

    def evaluate(base, slot):
        squares = dot_tn(targets[:, pl.ds(pl.multiple_of(base, block), block)], sources[...])
        for i in range(block // ROWS):
            inner = slice(i * ROWS, (i + 1) * ROWS)
            lower = slice(block + i * ROWS, block + (i + 1) * ROWS)
            for c in range(0, count, 256):
                here = slice(c, c + 256)
                there = slice(count + c, count + c + 256)
                real, imag = kernel_values(squares[inner, here], COS_TILE)
                real = real.astype(BF16)
                imag = imag.astype(BF16)
                tiles[slot, inner, here] = real
                tiles[slot, inner, there] = imag
                tiles[slot, lower, here] = imag
                tiles[slot, lower, there] = -real

    def gather(slot):
        total[...] += dot_tn(tiles[slot, :, 0:skeleton], tiles[slot])

    total[...] = jnp.zeros_like(total)
    evaluate(0, 0)
    for i in range(1, proxies // block):
        gather((i + 1) % 2)
        evaluate(i * block, i % 2)
    parity = (proxies // block) % 2
    per = count // block

    @pl.loop(0, entries)
    def _(k):
        base = proxies + k * count
        for i in range(per):
            gather((parity + i + 1) % 2)
            evaluate(base + i * block, (parity + i) % 2)

    gather((parity + per - 1) % 2)
    half = (count - skeleton) // group
    for p in range(2):
        gram_ref[p] = total[:, p * count:p * count + skeleton]
        for c in range(group):
            start = p * count + skeleton + c * half
            rest_ref[c, p] = total[:, start:start + half]


def swap_kernel(gram_ref, rest_ref, gram_out, rest_out, sends, recvs):
    me = lax.axis_index("col")
    side = lax.rem(me, 2)
    peer = {"col": me + 1 - 2 * side}
    meet([peer])()
    copies = []
    for i in range(2):
        copies.append(send(gram_ref.at[i], gram_out.at[i], sends, recvs, i, peer))
    for i in range(2):
        copies.append(send(rest_ref.at[1 - side, i], rest_out.at[i], sends, recvs, 2 + i, peer))
    for copy in copies:
        copy.wait()


def exact(a, b, dims=((1,), (0,))):
    return lax.dot_general(a, b, (dims, ((), ())), precision=highest,
                           preferred_element_type=F32)


def solve_kernel(group, gram_ref, rest_ref, gram_in, rest_in, x_ref, mat, low, high):
    n = x_ref.shape[1]
    wide = mat.shape[2]
    nb = NBLK
    side = lax.rem(lax.axis_index("col"), group)
    mat[:, :, 0:n] = gram_ref[...] + gram_in[...]
    mat[:, :, n:] = rest_ref[side] + rest_in[...]
    diagonal = lax.broadcasted_iota(jnp.int32, (n, n), 0) == lax.broadcasted_iota(
        jnp.int32, (n, n), 1
    )
    gram = mat[0, :, 0:n]
    ridge = ridge_share * jnp.sum(jnp.where(diagonal, gram, 0.0)) / n
    mat[0, :, 0:n] = gram + jnp.where(diagonal, ridge, 0.0)
    low[...] = jnp.zeros_like(low)
    high[...] = jnp.zeros_like(high)
    lane = lax.broadcasted_iota(jnp.int32, (nb, 128), 1)
    sub = lax.broadcasted_iota(jnp.int32, (nb, 128), 0)
    lane_all = lax.broadcasted_iota(jnp.int32, (n, 128), 1)

    def turned(block, shift):
        return pltpu.roll(block, shift, 1) if shift else block

    def inverse(block_re, block_im, back):
        re0, im0 = turned(block_re, back), turned(block_im, back)
        re1, im1 = turned(block_re, (back + nb) % 128), turned(block_im, (back + nb) % 128)
        zero = jnp.zeros_like(re0)
        m = jnp.where(lane < nb, re0, jnp.where(lane < 2 * nb, im1,
                                                jnp.where(lane - 2 * nb == sub, 1.0, zero)))
        w = jnp.where(lane < nb, -im0, jnp.where(lane < 2 * nb, re1,
                                                 jnp.where(lane - 3 * nb == sub, 1.0, zero)))

        def spread(block, k):
            return jnp.broadcast_to(block[:, k:k + 1], (nb, 128))

        for k in range(0, nb, 2):
            p0, p1 = spread(m, k), spread(m, k + 1)
            s0, s1 = spread(m, nb + k), spread(m, nb + k + 1)
            a, d = p0[k:k + 1], p1[k + 1:k + 2]
            br, bi = p1[k:k + 1], s1[k:k + 1]
            scale = 1.0 / (a * d - (br * br + bi * bi))
            m0, m1, w0, w1 = m[k:k + 1], m[k + 1:k + 2], w[k:k + 1], w[k + 1:k + 2]
            row_m0 = (d * m0 - (br * m1 + bi * w1)) * scale
            row_w0 = (d * w0 - (br * w1 - bi * m1)) * scale
            row_m1 = (a * m1 - (br * m0 - bi * w0)) * scale
            row_w1 = (a * w1 - (br * w0 + bi * m0)) * scale
            new_m = m - ((p0 * row_m0 + s0 * row_w0) + (p1 * row_m1 + s1 * row_w1))
            new_w = w - ((p0 * row_w0 - s0 * row_m0) + (p1 * row_w1 - s1 * row_m1))
            m = jnp.where(sub == k, row_m0, jnp.where(sub == k + 1, row_m1, new_m))
            w = jnp.where(sub == k, row_w0, jnp.where(sub == k + 1, row_w1, new_w))
        return m

    m = inverse(mat[0, 0:nb, 0:128], mat[1, 0:nb, 0:128], 0)
    for j in range(n // nb):
        rows = slice(j * nb, (j + 1) * nb)
        after = slice((j + 1) * nb, (j + 2) * nb)
        q = (j * nb) // 128 * 128
        back = (128 - (j * nb) % 128) % 128
        start = (j + 1) * nb // 128 * 128
        span = wide - start
        panel_re = mat[0, rows, start:]
        panel_im = mat[1, rows, start:]
        high[2 * nb:3 * nb, 0:span] = panel_re
        high[2 * nb:3 * nb, span:2 * span] = panel_im
        high[3 * nb:4 * nb, 0:span] = -panel_im
        high[3 * nb:4 * nb, span:2 * span] = panel_re
        solved = exact(m, high[:, 0:2 * span])
        low[0:nb, 0:2 * span] = solved
        low[nb:2 * nb, 0:span] = -solved[:, span:]
        low[nb:2 * nb, span:2 * span] = solved[:, 0:span]
        left = jnp.where(
            lane_all < nb,
            turned(mat[0, :, q:q + 128], back),
            jnp.where(lane_all < 2 * nb, turned(mat[1, :, q:q + 128], (back + nb) % 128), 0.0),
        )
        if (j + 1) * nb < n:
            ahead = left[after]
            next_re = mat[0, after, start:start + 128] - exact(ahead, low[:, 0:128])
            next_im = mat[1, after, start:start + 128] - exact(ahead, low[:, span:span + 128])
            m = inverse(next_re, next_im, (128 - ((j + 1) * nb) % 128) % 128)
        change = exact(left, low[:, 0:2 * span])
        mat[0, :, start:] = mat[0, :, start:] - change[:, 0:span]
        mat[1, :, start:] = mat[1, :, start:] - change[:, span:]
        mat[0, rows, start:] = solved[:, 0:span]
        mat[1, rows, start:] = solved[:, span:]
    x_ref[...] = mat[:, :, n:]


def split(x):
    high = x.astype(BF16)
    return high, (x - high.astype(F32)).astype(BF16)


def threefold(a, b, dims=((1,), (0,))):
    def one(x, y):
        return lax.dot_general(x, y, (dims, ((), ())), preferred_element_type=F32)

    return one(a[0], b[0]) + (one(a[0], b[1]) + one(a[1], b[0]))


def right_side(x):
    xr, xi = x[0], x[1]
    return split(jnp.concatenate(
        [jnp.concatenate([xr, xi], axis=1), jnp.concatenate([-xi, xr], axis=1)], axis=0))


def pivot_rows(pivot_ref, box):
    pieces = range(pivot_ref.shape[0])
    return [jnp.concatenate([pivot_ref[c, box, p:p + 1, :] for c in pieces], axis=1)
            for p in range(2)]


def fold(left, rest, right, pivots, rows, weighted, out_ref, slot):
    qr, qi = pivots
    width = qr.shape[1]
    held = weighted.shape[1] // 2
    both = rest - threefold(left, right)
    br, bi = both[:, 0:width], both[:, width:]
    wr = br * qr - bi * qi
    wi = br * qi + bi * qr
    weighted[0] = jnp.concatenate([wr, -wi], axis=1)
    weighted[1] = jnp.concatenate([wi, wr], axis=1)
    upper = jnp.concatenate([weighted[0, rows, :], weighted[1, rows, :]], axis=0)
    update = threefold(split(upper), split(both), ((1,), (1,)))
    half = update.shape[0] // 2
    out_ref[slot, 0] = out_ref[slot, 0] - update[0:half]
    out_ref[slot, 1] = out_ref[slot, 1] - update[half:]


def row_half(col_count, group, n):
    count = n // (col_count // group)
    me = lax.axis_index("col")
    return pl.ds(pl.multiple_of((me // group) * count, count), count)


def spread(squares, keep):
    for i in range(0, squares.shape[0], ROWS):
        inner = slice(i, i + ROWS)
        for c in range(0, squares.shape[1], 128):
            real, imag = kernel_values(squares[inner, c:c + 128], COS)
            keep(inner, c, real, imag)


def near_kernel(box_total, col_count, group, nb_ref, place_ref, points_ref, x_ref, pivot_ref,
                out_ref, high_ref, low_ref, rest_ref, sources, left, rest, weighted):
    n = x_ref.shape[1]
    width = x_ref.shape[2]
    box_count, _, count = points_ref.shape[1:]
    entries = nb_ref.shape[1]
    me = lax.axis_index("col")
    side = lax.rem(me, group)
    box = me // group
    fed = 1 - box
    out_ref[...] = jnp.zeros_like(out_ref)
    for i, which in enumerate((box, fed)):
        whole = source_rows(centred(points_ref[1, which]))
        half = whole[:, n:n + width]
        for c in range(1, group):
            half = jnp.where(side == c, whole[:, n + c * width:n + (c + 1) * width], half)
        sources[i, :, 0:n] = whole[:, 0:n]
        sources[i, :, n:] = half
    right = right_side(x_ref)
    pivots = pivot_rows(pivot_ref, box)
    rows = row_half(col_count, group, n)

    def evaluate(i, which, k, high, low, rest_at):
        slot = slot_of(nb_ref, which, k, box_count, box_total)
        here = shifted(points_ref[slot // box_count, slot % box_count], place_ref[which, k])
        squares = dot_tn(target_rows(here[:, 0:n]), sources[i])

        def keep(inner, c, real, imag):
            for p, value in enumerate((real, imag)):
                if c < n:
                    top, bottom = split(value)
                    high[inner, p * n + c:p * n + c + 128] = top
                    low[inner, p * n + c:p * n + c + 128] = bottom
                else:
                    rest_at[inner, p * width + c - n:p * width + c - n + 128] = value

        spread(squares, keep)

    def own(k, slot):
        evaluate(0, box, k, left.at[slot, 0], left.at[slot, 1], rest.at[slot])

    def other(k):
        evaluate(1, fed, k, high_ref.at[k], low_ref.at[k], rest_ref.at[k])

    def use(k, slot):
        to = slot_of(nb_ref, box, k, box_count, box_total)
        fold((left[slot, 0], left[slot, 1]), rest[slot], right, pivots, rows, weighted, out_ref,
             to)

    own(0, 0)

    @pl.loop(0, entries // 2)
    def _(pair):
        k = 2 * pair
        own(k + 1, 1)
        other(k)
        use(k, 0)
        own(jnp.minimum(k + 2, entries - 1), 0)
        other(k + 1)
        use(k + 1, 1)


def far_kernel(box_total, col_count, group, nb_ref, buf_ref, high_ref, low_ref, rest_ref, x_ref,
               mine_ref, pivot_ref, out_ref, inter_ref, weighted):
    n = x_ref.shape[1]
    entries, _, _ = rest_ref.shape
    me = lax.axis_index("col")
    box = me // group
    fed = 1 - box
    box_count = pivot_ref.shape[1]
    out_ref[...] = buf_ref[...]
    right = right_side(x_ref)
    pivots = pivot_rows(pivot_ref, fed)
    rows = row_half(col_count, group, n)
    strip = inter_ref.shape[2]
    for p in range(2):
        for ref, where in ((mine_ref, box), (x_ref, fed)):
            block = jnp.transpose(ref[p])
            piece = block[0:strip]
            for c in range(1, block.shape[0] // strip):
                piece = jnp.where(box == c, block[c * strip:(c + 1) * strip], piece)
            inter_ref[where, p] = piece

    @pl.loop(0, entries // 2)
    def _(pair):
        for i in range(2):
            k = 2 * pair + i
            to = slot_of(nb_ref, fed, k, box_count, box_total)
            fold((high_ref[k], low_ref[k]), rest_ref[k], right, pivots, rows, weighted.at[i],
                 out_ref, to)


def reduce_kernel(box_total, buf_ref, out_ref, pair_in, line_out, line_in, side_out, side_in,
                  held, sends, recvs):
    me = lax.axis_index("col")
    place = lax.axis_index("box")
    side = lax.rem(me, 2)
    odd = lax.rem(place, 2)
    near = {"col": me + 1 - 2 * side}
    relay = {"box": lax.rem(place + box_total + 4 * odd - 2, box_total)}
    source = {"box": lax.rem(place + box_total + 2 - 4 * odd, box_total)}
    twin = {"box": place + 1 - 2 * odd}
    meet([near, relay, source, twin])()
    box_count = out_ref.shape[0]
    order = (2 * odd, 2 - 2 * odd, 1)
    chunks = [(d, p) for d in range(box_count) for p in range(2)]
    pairs = {}
    for g, at in enumerate(order):
        for i, (d, p) in enumerate(chunks):
            pairs[g, i] = send(buf_ref.at[at * box_count + d, p, 1 - side], pair_in.at[g, d, p],
                               sends, recvs, len(chunks) * g + i, near)
    base = 3 * len(chunks)
    lines, sides = [], []
    for i, (d, p) in enumerate(chunks):
        pairs[0, i].wait()
        line_out[d, p] = buf_ref[order[0] * box_count + d, p, side] + pair_in[0, d, p]
        lines.append(send(line_out.at[d, p], line_in.at[d, p], sends, recvs, base + i, relay))
    for i, (d, p) in enumerate(chunks):
        pairs[1, i].wait()
        held[d, p] = buf_ref[order[1] * box_count + d, p, side] + pair_in[1, d, p]
    for i, (d, p) in enumerate(chunks):
        lines[i].wait()
        side_out[d, p] = held[d, p] + line_in[d, p]
        sides.append(send(side_out.at[d, p], side_in.at[d, p], sends, recvs,
                          base + len(chunks) + i, twin))
    for i, (d, p) in enumerate(chunks):
        pairs[2, i].wait()
        held[d, p] = buf_ref[box_count + d, p, side] + pair_in[2, d, p]
    for i, (d, p) in enumerate(chunks):
        sides[i].wait()
        out_ref[d, p] = held[d, p] + side_in[d, p]


def ring(count, step):
    return [(i, (i + step) % count) for i in range(count)]


def on_device(
    box_points, proxy_directions, point_order, neighbour_boxes, neighbour_places, pivot_inverse
):
    box_count, _, point_count = box_points.shape
    col_count = lax.axis_size("col")
    box_total = lax.axis_size("box")
    group = col_count // box_count
    listed = neighbour_boxes.shape[1]
    entries = listed // group
    width = pivot_inverse.shape[2]
    rest = width * col_count
    skeleton = point_count - rest
    half = rest // group
    share = proxy_directions.shape[1]
    dma = pltpu.SemaphoreType.DMA

    points, proxies, pivots = pl.pallas_call(
        functools.partial(exchange_kernel, box_total, col_count, group, skeleton),
        out_shape=(
            jax.ShapeDtypeStruct((3, box_count, 8, point_count), F32),
            jax.ShapeDtypeStruct((box_count,) + proxy_directions.shape, F32),
            jax.ShapeDtypeStruct((box_count,) + pivot_inverse.shape, F32),
        ),
        in_specs=[HBM] * 4,
        out_specs=(VMEM,) * 3,
        scratch_shapes=[pltpu.VMEM(box_points.shape, F32),
                        pltpu.VMEM(point_order.shape, jnp.int32),
                        dma((4,)), dma((4,)), dma((4,))],
        compiler_params=params(collective_id=0, has_side_effects=True),
    )(box_points, point_order, proxy_directions, pivot_inverse)

    rows = box_count * share + entries * point_count
    gram, right = pl.pallas_call(
        functools.partial(tile_kernel, box_total, entries, group, skeleton),
        out_shape=(
            jax.ShapeDtypeStruct((2, skeleton, skeleton), F32),
            jax.ShapeDtypeStruct((group, 2, skeleton, half), F32),
        ),
        in_specs=[HBM, HBM, VMEM, VMEM],
        out_specs=(VMEM, VMEM),
        scratch_shapes=[
            pltpu.SMEM(neighbour_boxes.shape, jnp.int32),
            pltpu.SMEM(neighbour_places.shape, jnp.int32),
            pltpu.VMEM((DEPTH, rows), BF16),
            pltpu.VMEM((DEPTH, point_count), BF16),
            pltpu.VMEM((2, 2 * BLOCK, 2 * point_count), BF16),
            pltpu.VMEM((skeleton, 2 * point_count), F32),
            dma((2,)),
        ],
        compiler_params=params(),
    )(neighbour_boxes, neighbour_places, points, proxies)

    gram_in, right_in = pl.pallas_call(
        swap_kernel,
        out_shape=(jax.ShapeDtypeStruct(gram.shape, F32),
                   jax.ShapeDtypeStruct(right.shape[1:], F32)),
        in_specs=[VMEM, VMEM],
        out_specs=(VMEM, VMEM),
        scratch_shapes=[dma((4,)), dma((4,))],
        compiler_params=params(collective_id=2, has_side_effects=True),
    )(gram, right)
    solved = pl.pallas_call(
        functools.partial(solve_kernel, group),
        out_shape=jax.ShapeDtypeStruct((2, skeleton, half), F32),
        in_specs=[VMEM] * 4,
        out_specs=VMEM,
        scratch_shapes=[
            pltpu.VMEM((2, skeleton, skeleton + half), F32),
            pltpu.VMEM((128, 2 * (skeleton + half)), F32),
            pltpu.VMEM((128, 2 * (skeleton + half)), F32),
        ],
        compiler_params=params(),
    )(gram, right, gram_in, right_in)
    arrived = lax.ppermute(solved, "col", ring(col_count, group))

    strips = skeleton // box_count
    buffer, high, low, kept = pl.pallas_call(
        functools.partial(near_kernel, box_total, col_count, group),
        out_shape=(
            jax.ShapeDtypeStruct((3 * box_count, 2, strips, skeleton), F32),
            jax.ShapeDtypeStruct((listed, skeleton, 2 * skeleton), BF16),
            jax.ShapeDtypeStruct((listed, skeleton, 2 * skeleton), BF16),
            jax.ShapeDtypeStruct((listed, skeleton, 2 * half), F32),
        ),
        in_specs=[SMEM, SMEM, VMEM, VMEM, VMEM],
        out_specs=(VMEM,) * 4,
        scratch_shapes=[
            pltpu.VMEM((box_count, DEPTH, skeleton + half), BF16),
            pltpu.VMEM((2, 2, skeleton, 2 * skeleton), BF16),
            pltpu.VMEM((2, skeleton, 2 * half), F32),
            pltpu.VMEM((2, skeleton, 2 * half), F32),
        ],
        compiler_params=params(),
        cost_estimate=pl.CostEstimate(flops=4 * 10**9, bytes_accessed=8 * 10**6,
                                      transcendentals=0),
    )(neighbour_boxes, neighbour_places, points, solved, pivots)

    buffer, inter = pl.pallas_call(
        functools.partial(far_kernel, box_total, col_count, group),
        out_shape=(
            jax.ShapeDtypeStruct(buffer.shape, F32),
            jax.ShapeDtypeStruct((box_count, 2, width, skeleton), F32),
        ),
        in_specs=[SMEM] + [VMEM] * 7,
        out_specs=(VMEM, VMEM),
        scratch_shapes=[pltpu.VMEM((2, 2, skeleton, 2 * half), F32)],
        compiler_params=params(),
    )(neighbour_boxes, buffer, high, low, kept, arrived, solved, pivots)
    interpolation = jnp.swapaxes(inter, 2, 3)

    strip = skeleton // col_count
    block = (box_count, 2, strip, skeleton)
    jobs = 5 * 2 * box_count
    skeleton_update = pl.pallas_call(
        functools.partial(reduce_kernel, box_total),
        out_shape=jax.ShapeDtypeStruct(block, F32),
        in_specs=[VMEM],
        out_specs=VMEM,
        scratch_shapes=[
            pltpu.VMEM((3,) + block, F32),
            pltpu.VMEM(block, F32),
            pltpu.VMEM(block, F32),
            pltpu.VMEM(block, F32),
            pltpu.VMEM(block, F32),
            pltpu.VMEM(block, F32),
            dma((jobs,)),
            dma((jobs,)),
        ],
        compiler_params=params(collective_id=1, has_side_effects=True),
    )(buffer.reshape(3 * box_count, 2, group, strip, skeleton))
    return (interpolation, skeleton_update)


def solution(mesh):
    placed = (
        P("box", None, None),
        P(None, "col"),
        P("box", None),
        P("box", None),
        P("box", None),
        P("box", None, "col"),
    )
    return jax.shard_map(
        on_device,
        mesh=mesh,
        in_specs=placed,
        out_specs=(P("box", None, None, "col"), P("box", None, "col", None)),
        check_vma=False,
    )
```

```python
import functools
import math

import jax
import jax.numpy as jnp
from jax import lax
from jax.experimental import pallas as pl
from jax.experimental.pallas import tpu as pltpu
from jax.sharding import PartitionSpec as P

softening = 0.05
proxy_radius = 1.5
ridge_share = 0.05
NBLK = 32
BLOCK = 256
ROWS = 16
DEPTH = 64

SIN = (4.44287959, -7.30781805, 3.59778873, -0.79123822)
COS_TILE = (1.41420408, -6.97764206, 5.7152384, -1.72834866)
COS = (1.4142135381698608, -6.978850841522217, 5.739460468292236, -1.883557915687561, 0.3106880187988281)

HBM = pl.BlockSpec(memory_space=pltpu.HBM)
VMEM = pl.BlockSpec(memory_space=pltpu.VMEM)
SMEM = pl.BlockSpec(memory_space=pltpu.SMEM)
MESH = pl.DeviceIdType.MESH
F32 = jnp.float32
BF16 = jnp.bfloat16


def params(**more):
    return pltpu.CompilerParams(vmem_limit_bytes=24 * 1024 * 1024, **more)


def horner(coefficients, z):
    total = coefficients[-1] * z + coefficients[-2]
    for one in coefficients[-3::-1]:
        total = total * z + one
    return total


def kernel_values(square, cosine):
    inverse = lax.rsqrt(square)
    turns = square * inverse
    part = turns - jnp.floor(turns + 0.5)
    z = part * part
    amplitude = inverse * (1.0 / (2.0 * math.pi))
    sine = part * horner(SIN, z)
    scaled = amplitude * sine
    return amplitude - scaled * sine, scaled * horner(cosine, z)


def three(x):
    high = x.astype(BF16).astype(F32)
    rest = x - high
    mid = rest.astype(BF16).astype(F32)
    return high, mid, rest - mid


def row_three(block, row):
    third = lax.broadcasted_iota(jnp.int32, block.shape, 0) == 3
    return jnp.where(third, row, block)


def norm_of(points):
    return jnp.sum(points * points, axis=0, keepdims=True)


def stacked(groups):
    zero = jnp.zeros_like(groups[0])
    return jnp.concatenate(groups + [zero] * (DEPTH // 8 - len(groups)), axis=0).astype(BF16)


def target_rows(points):
    high, mid, low = three(points)
    n_high, n_mid, n_low = three(norm_of(points))
    return stacked([row_three(high, n_high), row_three(high, n_mid), row_three(mid, n_low),
                    row_three(high, 1.0), row_three(mid, 1.0), row_three(low, 1.0)])


def source_rows(points):
    high, mid, low = three(points)
    norm = norm_of(points) + 4.0 * softening * softening
    n_high, n_mid, n_low = three(norm)
    return stacked([row_three(-2.0 * high, 1.0), row_three(-2.0 * mid, 1.0),
                    row_three(-2.0 * high, 1.0), row_three(-2.0 * low, n_high),
                    row_three(-2.0 * mid, n_mid), row_three(-2.0 * high, n_low)])


def three_rows(points):
    rows = lax.broadcasted_iota(jnp.int32, points.shape, 0)
    return jnp.where(rows < 3, points, 0.0)


def shifted(points, code):
    code = jnp.where(code >= 13, code + 1, code)
    axis_row = lax.broadcasted_iota(jnp.int32, points.shape, 0)
    move = jnp.where(
        axis_row == 0,
        (code // 9 - 1).astype(F32),
        jnp.where(axis_row == 1, ((code // 3) % 3 - 1).astype(F32), (code % 3 - 1).astype(F32)),
    )
    return three_rows(2.0 * (points + (move - 0.5)))


def centred(points):
    return three_rows(2.0 * (points - 0.5))


def slot_of(nb_ref, row, entry, box_count, box_total):
    owner_box = nb_ref[row, entry]
    step = owner_box // box_count - lax.axis_index("box") + 1
    step = jnp.where(step < 0, step + box_total, step)
    step = jnp.where(step >= box_total, step - box_total, step)
    return step * box_count + owner_box % box_count


def dot_tn(a, b):
    return lax.dot_general(a, b, (((0,), (0,)), ((), ())), preferred_element_type=F32)


def meet(peers):
    barrier = pltpu.get_barrier_semaphore()
    for peer in peers:
        pl.semaphore_signal(barrier, inc=1, device_id=peer, device_id_type=MESH)
    return lambda: pl.semaphore_wait(barrier, len(peers))


def send(source, target, sends, recvs, index, peer):
    one = pltpu.make_async_remote_copy(
        src_ref=source, dst_ref=target, send_sem=sends.at[index], recv_sem=recvs.at[index],
        device_id=peer, device_id_type=MESH)
    one.start()
    return one


def exchange_kernel(box_total, col_count, group, skeleton, points_ref, order_ref, proxy_ref,
                    pivot_ref, points_out, proxy_out, pivot_out, points, order, sends, recvs,
                    local):
    me = lax.axis_index("col")
    place = lax.axis_index("box")
    box_count, _, count = points_ref.shape
    after = {"box": lax.rem(place + 1, box_total)}
    before = {"box": lax.rem(place + box_total - 1, box_total)}
    across = {"col": lax.rem(me + group, col_count)}
    mine = me // group
    own = ((points_ref, points), (order_ref, order), (proxy_ref, proxy_out.at[0]),
           (pivot_ref, pivot_out.at[mine]))
    loads = []
    for i, (source, target) in enumerate(own):
        copy = pltpu.make_async_copy(source, target, local.at[i])
        copy.start()
        loads.append(copy)
    arrived = meet([before, after, across])
    for copy in loads:
        copy.wait()
    width = (count - skeleton) // col_count
    for box in range(box_count):
        row = order[box:box + 1, :]
        strips = [row[:, skeleton + s * width:skeleton + (s + 1) * width]
                  for c in range(group) for s in range(c, col_count, group)]
        row = jnp.concatenate([row[:, 0:skeleton]] + strips, axis=1)
        one_hot = (lax.broadcasted_iota(jnp.int32, (count, count), 0) == row).astype(F32)
        whole = jnp.concatenate([points[box], jnp.zeros((5, count), F32)], axis=0)
        rows = jnp.concatenate(list(three(whole)) + [jnp.zeros_like(whole)], axis=0)
        picked = jnp.dot(rows.astype(BF16), one_hot.astype(BF16), preferred_element_type=F32)
        points_out[1, box] = (picked[0:8] + picked[8:16]) + picked[16:24]
    arrived()
    jobs = [
        send(points_out.at[1], points_out.at[0], sends, recvs, 0, after),
        send(points_out.at[1], points_out.at[2], sends, recvs, 1, before),
        send(proxy_ref, proxy_out.at[1], sends, recvs, 2, across),
        send(pivot_ref, pivot_out.at[mine], sends, recvs, 3, across),
    ]
    for copy in jobs:
        copy.wait()


def tile_kernel(box_total, entries, group, skeleton, nb_hbm, place_hbm, points_ref, proxy_ref,
                gram_ref, rest_ref, nb_ref, place_ref, targets, sources, tiles, total, local):
    count = points_ref.shape[3]
    box_count, _, share = proxy_ref.shape
    proxies = box_count * share
    me = lax.axis_index("col")
    box = me // group
    first = lax.rem(me, group) * entries
    loads = [pltpu.make_async_copy(nb_hbm, nb_ref, local.at[0]),
             pltpu.make_async_copy(place_hbm, place_ref, local.at[1])]
    for copy in loads:
        copy.start()
    sources[...] = source_rows(centred(points_ref[1, box]))
    for d in range(box_count):
        directions = jnp.concatenate([proxy_ref[d], jnp.zeros((5, share), F32)], axis=0)
        targets[:, d * share:(d + 1) * share] = target_rows((2.0 * proxy_radius) * directions)
    for copy in loads:
        copy.wait()
    for k in range(entries):
        slot = slot_of(nb_ref, box, first + k, box_count, box_total)
        here = shifted(points_ref[slot // box_count, slot % box_count], place_ref[box, first + k])
        targets[:, proxies + k * count:proxies + (k + 1) * count] = target_rows(here)
    block = tiles.shape[1] // 2

    def evaluate(base, slot):
        squares = dot_tn(targets[:, pl.ds(pl.multiple_of(base, block), block)], sources[...])
        for i in range(block // ROWS):
            inner = slice(i * ROWS, (i + 1) * ROWS)
            lower = slice(block + i * ROWS, block + (i + 1) * ROWS)
            for c in range(0, count, 256):
                here = slice(c, c + 256)
                there = slice(count + c, count + c + 256)
                real, imag = kernel_values(squares[inner, here], COS_TILE)
                real = real.astype(BF16)
                imag = imag.astype(BF16)
                tiles[slot, inner, here] = real
                tiles[slot, inner, there] = imag
                tiles[slot, lower, here] = imag
                tiles[slot, lower, there] = -real

    def gather(slot):
        total[...] += dot_tn(tiles[slot, :, 0:skeleton], tiles[slot])

    total[...] = jnp.zeros_like(total)
    evaluate(0, 0)
    for i in range(1, proxies // block):
        gather((i + 1) % 2)
        evaluate(i * block, i % 2)
    parity = (proxies // block) % 2
    per = count // block

    @pl.loop(0, entries)
    def _(k):
        base = proxies + k * count
        for i in range(per):
            gather((parity + i + 1) % 2)
            evaluate(base + i * block, (parity + i) % 2)

    gather((parity + per - 1) % 2)
    half = (count - skeleton) // group
    for p in range(2):
        gram_ref[p] = total[:, p * count:p * count + skeleton]
        for c in range(group):
            start = p * count + skeleton + c * half
            rest_ref[c, p] = total[:, start:start + half]


def swap_kernel(gram_ref, rest_ref, gram_out, rest_out, sends, recvs):
    me = lax.axis_index("col")
    side = lax.rem(me, 2)
    peer = {"col": me + 1 - 2 * side}
    meet([peer])()
    copies = []
    for i in range(2):
        copies.append(send(gram_ref.at[i], gram_out.at[i], sends, recvs, i, peer))
    for i in range(2):
        copies.append(send(rest_ref.at[1 - side, i], rest_out.at[i], sends, recvs, 2 + i, peer))
    for copy in copies:
        copy.wait()


def solve_kernel(group, gram_ref, rest_ref, gram_in, rest_in, x_ref, mat, head, tail):
    n = x_ref.shape[1]
    nb = NBLK
    side = lax.rem(lax.axis_index("col"), group)
    mat[:, :, n:] = rest_ref[side] + rest_in[...]
    ridge = 0.0
    diagonal = lax.broadcasted_iota(jnp.int32, (128, 128), 0) == lax.broadcasted_iota(
        jnp.int32, (128, 128), 1
    )
    gram = gram_ref[...] + gram_in[...]
    for c in range(0, n, 128):
        ridge = ridge + jnp.sum(jnp.where(diagonal, gram[0, c:c + 128, c:c + 128], 0.0))
    ridge = ridge_share * ridge / n
    mat[:, :, 0:n] = gram
    for c in range(0, n, 128):
        here = slice(c, c + 128)
        mat[0, here, here] = gram[0, here, here] + jnp.where(diagonal, ridge, 0.0)
    head[6 * nb:, :] = jnp.zeros_like(head[6 * nb:, :])
    tail[6 * nb:, :] = jnp.zeros_like(tail[6 * nb:, :])
    lane = lax.broadcasted_iota(jnp.int32, (nb, 128), 1)
    sub = lax.broadcasted_iota(jnp.int32, (nb, 128), 0)
    lane_all = lax.broadcasted_iota(jnp.int32, (n, 128), 1)

    def turned(block, shift):
        shift = shift % 128
        return pltpu.roll(block, shift, 1) if shift else block

    def inverse(block_re, block_im, back):
        re0, im0 = turned(block_re, back), turned(block_im, back)
        re1, im1 = turned(block_re, back + nb), turned(block_im, back + nb)
        zero = jnp.zeros_like(re0)
        m = jnp.where(lane < nb, re0, jnp.where(lane < 2 * nb, im1,
                                                jnp.where(lane - 2 * nb == sub, 1.0, zero)))
        w = jnp.where(lane < nb, -im0, jnp.where(lane < 2 * nb, re1,
                                                 jnp.where(lane - 3 * nb == sub, 1.0, zero)))

        def spread(block, k):
            return jnp.broadcast_to(block[:, k:k + 1], (nb, 128))

        for k in range(0, nb, 2):
            p0, p1 = spread(m, k), spread(m, k + 1)
            s0, s1 = spread(m, nb + k), spread(m, nb + k + 1)
            a, d = p0[k:k + 1], p1[k + 1:k + 2]
            br, bi = p1[k:k + 1], s1[k:k + 1]
            scale = 1.0 / (a * d - (br * br + bi * bi))
            m0, m1, w0, w1 = m[k:k + 1], m[k + 1:k + 2], w[k:k + 1], w[k + 1:k + 2]
            row_m0 = (d * m0 - (br * m1 + bi * w1)) * scale
            row_w0 = (d * w0 - (br * w1 - bi * m1)) * scale
            row_m1 = (a * m1 - (br * m0 - bi * w0)) * scale
            row_w1 = (a * w1 - (br * w0 + bi * m0)) * scale
            new_m = m - ((p0 * row_m0 + s0 * row_w0) + (p1 * row_m1 + s1 * row_w1))
            new_w = w - ((p0 * row_w0 - s0 * row_m0) + (p1 * row_w1 - s1 * row_m1))
            m = jnp.where(sub == k, row_m0, jnp.where(sub == k + 1, row_m1, new_m))
            w = jnp.where(sub == k, row_w0, jnp.where(sub == k + 1, row_w1, new_w))
            yield m

    def tripled(block):
        high = block.astype(BF16)
        return jnp.concatenate([high, (block - high.astype(F32)).astype(BF16)], axis=1)

    def put(ref, w, re, im):
        block = jnp.concatenate([jnp.concatenate([re, im], axis=1),
                                 jnp.concatenate([-im, re], axis=1)], axis=0)
        high, rest = split(block)
        where = slice(256 * w, 256 * w + 256)
        ref[0:2 * nb, where] = high
        ref[2 * nb:4 * nb, where] = rest
        ref[4 * nb:6 * nb, where] = high

    def plain(a, b):
        return jnp.dot(a, b, preferred_element_type=F32)

    for m in inverse(mat[0, 0:nb, 0:128], mat[1, 0:nb, 0:128], 0):
        pass
    for j in range(n // nb):
        rows = slice(j * nb, (j + 1) * nb)
        after = slice((j + 1) * nb, (j + 2) * nb)
        q = (j * nb) // 128 * 128
        back = -(j * nb)
        windows = list(range((j + 1) * nb // 128, mat.shape[2] // 128))
        window_re, window_im = mat[0, :, q:q + 128], mat[1, :, q:q + 128]
        left = tripled(jnp.where(
            lane_all < nb, turned(window_re, back),
            jnp.where(lane_all < 2 * nb, turned(window_im, back + nb),
                      jnp.where(lane_all < 3 * nb, turned(window_re, back + 2 * nb),
                                turned(window_im, back + 3 * nb)))))
        factor = tripled(jnp.where(lane < 2 * nb, turned(m, 64), m))
        held = {}

        def solve(w):
            here = slice(128 * w, 128 * w + 128)
            put(head, w, mat[0, rows, here], mat[1, rows, here])
            held[w] = plain(factor, head[:, 256 * w:256 * w + 256])
            put(tail, w, held[w][:, 0:128], held[w][:, 128:])

        def change(w, part):
            here = slice(128 * w, 128 * w + 128)
            some = slice(part * 128, (part + 1) * 128)
            less = plain(left[some], tail[:, 256 * w:256 * w + 256])
            mat[0, some, here] = mat[0, some, here] - less[:, 0:128]
            mat[1, some, here] = mat[1, some, here] - less[:, 128:]

        def place(w):
            here = slice(128 * w, 128 * w + 128)
            mat[0, rows, here] = held[w][:, 0:128]
            mat[1, rows, here] = held[w][:, 128:]

        first = windows[0]
        solve(first)
        pivots = iter(())
        if (j + 1) * nb < n:
            here = slice(128 * first, 128 * first + 128)
            less = plain(left[after], tail[:, 256 * first:256 * first + 256])
            pivots = inverse(mat[0, after, here] - less[:, 0:128],
                             mat[1, after, here] - less[:, 128:], -((j + 1) * nb))
        tasks = [functools.partial(solve, w) for w in windows[1:]]
        for w in windows:
            tasks += [functools.partial(change, w, part) for part in range(n // 128)]
            tasks.append(functools.partial(place, w))
        steps = nb // 2
        done = 0
        for i, task in enumerate(tasks):
            task()
            upto = (i + 1) * steps // len(tasks)
            for _ in range(upto - done):
                m = next(pivots, m)
            done = upto
        for m in pivots:
            pass
    x_ref[...] = mat[:, :, n:]


def split(x):
    high = x.astype(BF16)
    return high, (x - high.astype(F32)).astype(BF16)


def threefold(a, b, dims=((1,), (0,))):
    def one(x, y):
        return lax.dot_general(x, y, (dims, ((), ())), preferred_element_type=F32)

    return one(a[0], b[0]) + (one(a[0], b[1]) + one(a[1], b[0]))


def right_side(x):
    xr, xi = x[0], x[1]
    return split(jnp.concatenate(
        [jnp.concatenate([xr, xi], axis=1), jnp.concatenate([-xi, xr], axis=1)], axis=0))


def pivot_rows(pivot_ref, box):
    pieces = range(pivot_ref.shape[0])
    return [jnp.concatenate([pivot_ref[c, box, p:p + 1, :] for c in pieces], axis=1)
            for p in range(2)]


def fold(left, rest, right, pivots, rows, weighted, out_ref, slot):
    qr, qi = pivots
    width = qr.shape[1]
    held = weighted.shape[1] // 2
    both = rest - threefold(left, right)
    br, bi = both[:, 0:width], both[:, width:]
    wr = br * qr - bi * qi
    wi = br * qi + bi * qr
    weighted[0] = jnp.concatenate([wr, -wi], axis=1)
    weighted[1] = jnp.concatenate([wi, wr], axis=1)
    upper = jnp.concatenate([weighted[0, rows, :], weighted[1, rows, :]], axis=0)
    update = threefold(split(upper), split(both), ((1,), (1,)))
    half = update.shape[0] // 2
    out_ref[slot, 0] = out_ref[slot, 0] - update[0:half]
    out_ref[slot, 1] = out_ref[slot, 1] - update[half:]


def row_half(col_count, group, n):
    count = n // (col_count // group)
    me = lax.axis_index("col")
    return pl.ds(pl.multiple_of((me // group) * count, count), count)


def spread(squares, keep):
    for i in range(0, squares.shape[0], ROWS):
        inner = slice(i, i + ROWS)
        for c in range(0, squares.shape[1], 128):
            real, imag = kernel_values(squares[inner, c:c + 128], COS)
            keep(inner, c, real, imag)


def near_kernel(box_total, col_count, group, nb_ref, place_ref, points_ref, x_ref, pivot_ref,
                out_ref, high_ref, low_ref, rest_ref, sources, left, rest, weighted):
    n = x_ref.shape[1]
    width = x_ref.shape[2]
    box_count, _, count = points_ref.shape[1:]
    entries = nb_ref.shape[1]
    me = lax.axis_index("col")
    side = lax.rem(me, group)
    box = me // group
    fed = 1 - box
    out_ref[...] = jnp.zeros_like(out_ref)
    for i, which in enumerate((box, fed)):
        whole = source_rows(centred(points_ref[1, which]))
        half = whole[:, n:n + width]
        for c in range(1, group):
            half = jnp.where(side == c, whole[:, n + c * width:n + (c + 1) * width], half)
        sources[i, :, 0:n] = whole[:, 0:n]
        sources[i, :, n:] = half
    right = right_side(x_ref)
    pivots = pivot_rows(pivot_ref, box)
    rows = row_half(col_count, group, n)

    def evaluate(i, which, k, high, low, rest_at):
        slot = slot_of(nb_ref, which, k, box_count, box_total)
        here = shifted(points_ref[slot // box_count, slot % box_count], place_ref[which, k])
        squares = dot_tn(target_rows(here[:, 0:n]), sources[i])

        def keep(inner, c, real, imag):
            for p, value in enumerate((real, imag)):
                if c < n:
                    top, bottom = split(value)
                    high[inner, p * n + c:p * n + c + 128] = top
                    low[inner, p * n + c:p * n + c + 128] = bottom
                else:
                    rest_at[inner, p * width + c - n:p * width + c - n + 128] = value

        spread(squares, keep)

    def own(k, slot):
        evaluate(0, box, k, left.at[slot, 0], left.at[slot, 1], rest.at[slot])

    def other(k):
        evaluate(1, fed, k, high_ref.at[k], low_ref.at[k], rest_ref.at[k])

    def use(k, slot):
        to = slot_of(nb_ref, box, k, box_count, box_total)
        fold((left[slot, 0], left[slot, 1]), rest[slot], right, pivots, rows, weighted, out_ref,
             to)

    own(0, 0)

    @pl.loop(0, entries // 2)
    def _(pair):
        k = 2 * pair
        own(k + 1, 1)
        other(k)
        use(k, 0)
        own(jnp.minimum(k + 2, entries - 1), 0)
        other(k + 1)
        use(k + 1, 1)


def far_kernel(box_total, col_count, group, nb_ref, buf_ref, high_ref, low_ref, rest_ref, x_ref,
               mine_ref, pivot_ref, out_ref, inter_ref, weighted):
    n = x_ref.shape[1]
    entries, _, _ = rest_ref.shape
    me = lax.axis_index("col")
    box = me // group
    fed = 1 - box
    box_count = pivot_ref.shape[1]
    out_ref[...] = buf_ref[...]
    right = right_side(x_ref)
    pivots = pivot_rows(pivot_ref, fed)
    rows = row_half(col_count, group, n)
    strip = inter_ref.shape[2]
    for p in range(2):
        for ref, where in ((mine_ref, box), (x_ref, fed)):
            block = jnp.transpose(ref[p])
            piece = block[0:strip]
            for c in range(1, block.shape[0] // strip):
                piece = jnp.where(box == c, block[c * strip:(c + 1) * strip], piece)
            inter_ref[where, p] = piece

    @pl.loop(0, entries // 2)
    def _(pair):
        for i in range(2):
            k = 2 * pair + i
            to = slot_of(nb_ref, fed, k, box_count, box_total)
            fold((high_ref[k], low_ref[k]), rest_ref[k], right, pivots, rows, weighted.at[i],
                 out_ref, to)


def reduce_kernel(box_total, buf_ref, out_ref, pair_in, line_out, line_in, side_out, side_in,
                  held, sends, recvs):
    me = lax.axis_index("col")
    place = lax.axis_index("box")
    side = lax.rem(me, 2)
    odd = lax.rem(place, 2)
    near = {"col": me + 1 - 2 * side}
    relay = {"box": lax.rem(place + box_total + 4 * odd - 2, box_total)}
    source = {"box": lax.rem(place + box_total + 2 - 4 * odd, box_total)}
    twin = {"box": place + 1 - 2 * odd}
    meet([near, relay, source, twin])()
    box_count = out_ref.shape[0]
    order = (2 * odd, 2 - 2 * odd, 1)
    chunks = [(d, p) for d in range(box_count) for p in range(2)]
    pairs = {}
    for g, at in enumerate(order):
        for i, (d, p) in enumerate(chunks):
            pairs[g, i] = send(buf_ref.at[at * box_count + d, p, 1 - side], pair_in.at[g, d, p],
                               sends, recvs, len(chunks) * g + i, near)
    base = 3 * len(chunks)
    lines, sides = [], []
    for i, (d, p) in enumerate(chunks):
        pairs[0, i].wait()
        line_out[d, p] = buf_ref[order[0] * box_count + d, p, side] + pair_in[0, d, p]
        lines.append(send(line_out.at[d, p], line_in.at[d, p], sends, recvs, base + i, relay))
    for i, (d, p) in enumerate(chunks):
        pairs[1, i].wait()
        held[d, p] = buf_ref[order[1] * box_count + d, p, side] + pair_in[1, d, p]
    for i, (d, p) in enumerate(chunks):
        lines[i].wait()
        side_out[d, p] = held[d, p] + line_in[d, p]
        sides.append(send(side_out.at[d, p], side_in.at[d, p], sends, recvs,
                          base + len(chunks) + i, twin))
    for i, (d, p) in enumerate(chunks):
        pairs[2, i].wait()
        held[d, p] = buf_ref[box_count + d, p, side] + pair_in[2, d, p]
    for i, (d, p) in enumerate(chunks):
        sides[i].wait()
        out_ref[d, p] = held[d, p] + side_in[d, p]


def ring(count, step):
    return [(i, (i + step) % count) for i in range(count)]


def on_device(
    box_points, proxy_directions, point_order, neighbour_boxes, neighbour_places, pivot_inverse
):
    box_count, _, point_count = box_points.shape
    col_count = lax.axis_size("col")
    box_total = lax.axis_size("box")
    group = col_count // box_count
    listed = neighbour_boxes.shape[1]
    entries = listed // group
    width = pivot_inverse.shape[2]
    rest = width * col_count
    skeleton = point_count - rest
    half = rest // group
    share = proxy_directions.shape[1]
    dma = pltpu.SemaphoreType.DMA

    points, proxies, pivots = pl.pallas_call(
        functools.partial(exchange_kernel, box_total, col_count, group, skeleton),
        out_shape=(
            jax.ShapeDtypeStruct((3, box_count, 8, point_count), F32),
            jax.ShapeDtypeStruct((box_count,) + proxy_directions.shape, F32),
            jax.ShapeDtypeStruct((box_count,) + pivot_inverse.shape, F32),
        ),
        in_specs=[HBM] * 4,
        out_specs=(VMEM,) * 3,
        scratch_shapes=[pltpu.VMEM(box_points.shape, F32),
                        pltpu.VMEM(point_order.shape, jnp.int32),
                        dma((4,)), dma((4,)), dma((4,))],
        compiler_params=params(collective_id=0, has_side_effects=True),
    )(box_points, point_order, proxy_directions, pivot_inverse)

    rows = box_count * share + entries * point_count
    gram, right = pl.pallas_call(
        functools.partial(tile_kernel, box_total, entries, group, skeleton),
        out_shape=(
            jax.ShapeDtypeStruct((2, skeleton, skeleton), F32),
            jax.ShapeDtypeStruct((group, 2, skeleton, half), F32),
        ),
        in_specs=[HBM, HBM, VMEM, VMEM],
        out_specs=(VMEM, VMEM),
        scratch_shapes=[
            pltpu.SMEM(neighbour_boxes.shape, jnp.int32),
            pltpu.SMEM(neighbour_places.shape, jnp.int32),
            pltpu.VMEM((DEPTH, rows), BF16),
            pltpu.VMEM((DEPTH, point_count), BF16),
            pltpu.VMEM((2, 2 * BLOCK, 2 * point_count), BF16),
            pltpu.VMEM((skeleton, 2 * point_count), F32),
            dma((2,)),
        ],
        compiler_params=params(),
    )(neighbour_boxes, neighbour_places, points, proxies)

    gram_in, right_in = pl.pallas_call(
        swap_kernel,
        out_shape=(jax.ShapeDtypeStruct(gram.shape, F32),
                   jax.ShapeDtypeStruct(right.shape[1:], F32)),
        in_specs=[VMEM, VMEM],
        out_specs=(VMEM, VMEM),
        scratch_shapes=[dma((4,)), dma((4,))],
        compiler_params=params(collective_id=2, has_side_effects=True),
    )(gram, right)
    solved = pl.pallas_call(
        functools.partial(solve_kernel, group),
        out_shape=jax.ShapeDtypeStruct((2, skeleton, half), F32),
        in_specs=[VMEM] * 4,
        out_specs=VMEM,
        scratch_shapes=[
            pltpu.VMEM((2, skeleton, skeleton + half), F32),
            pltpu.VMEM((8 * NBLK, 2 * (skeleton + half)), BF16),
            pltpu.VMEM((8 * NBLK, 2 * (skeleton + half)), BF16),
        ],
        compiler_params=params(),
    )(gram, right, gram_in, right_in)
    arrived = lax.ppermute(solved, "col", ring(col_count, group))

    strips = skeleton // box_count
    buffer, high, low, kept = pl.pallas_call(
        functools.partial(near_kernel, box_total, col_count, group),
        out_shape=(
            jax.ShapeDtypeStruct((3 * box_count, 2, strips, skeleton), F32),
            jax.ShapeDtypeStruct((listed, skeleton, 2 * skeleton), BF16),
            jax.ShapeDtypeStruct((listed, skeleton, 2 * skeleton), BF16),
            jax.ShapeDtypeStruct((listed, skeleton, 2 * half), F32),
        ),
        in_specs=[SMEM, SMEM, VMEM, VMEM, VMEM],
        out_specs=(VMEM,) * 4,
        scratch_shapes=[
            pltpu.VMEM((box_count, DEPTH, skeleton + half), BF16),
            pltpu.VMEM((2, 2, skeleton, 2 * skeleton), BF16),
            pltpu.VMEM((2, skeleton, 2 * half), F32),
            pltpu.VMEM((2, skeleton, 2 * half), F32),
        ],
        compiler_params=params(),
        cost_estimate=pl.CostEstimate(flops=4 * 10**9, bytes_accessed=8 * 10**6,
                                      transcendentals=0),
    )(neighbour_boxes, neighbour_places, points, solved, pivots)

    buffer, inter = pl.pallas_call(
        functools.partial(far_kernel, box_total, col_count, group),
        out_shape=(
            jax.ShapeDtypeStruct(buffer.shape, F32),
            jax.ShapeDtypeStruct((box_count, 2, width, skeleton), F32),
        ),
        in_specs=[SMEM] + [VMEM] * 7,
        out_specs=(VMEM, VMEM),
        scratch_shapes=[pltpu.VMEM((2, 2, skeleton, 2 * half), F32)],
        compiler_params=params(),
    )(neighbour_boxes, buffer, high, low, kept, arrived, solved, pivots)
    interpolation = jnp.swapaxes(inter, 2, 3)

    strip = skeleton // col_count
    block = (box_count, 2, strip, skeleton)
    jobs = 5 * 2 * box_count
    skeleton_update = pl.pallas_call(
        functools.partial(reduce_kernel, box_total),
        out_shape=jax.ShapeDtypeStruct(block, F32),
        in_specs=[VMEM],
        out_specs=VMEM,
        scratch_shapes=[
            pltpu.VMEM((3,) + block, F32),
            pltpu.VMEM(block, F32),
            pltpu.VMEM(block, F32),
            pltpu.VMEM(block, F32),
            pltpu.VMEM(block, F32),
            pltpu.VMEM(block, F32),
            dma((jobs,)),
            dma((jobs,)),
        ],
        compiler_params=params(collective_id=1, has_side_effects=True),
    )(buffer.reshape(3 * box_count, 2, group, strip, skeleton))
    return (interpolation, skeleton_update)


def solution(mesh):
    placed = (
        P("box", None, None),
        P(None, "col"),
        P("box", None),
        P("box", None),
        P("box", None),
        P("box", None, "col"),
    )
    return jax.shard_map(
        on_device,
        mesh=mesh,
        in_specs=placed,
        out_specs=(P("box", None, None, "col"), P("box", None, "col", None)),
        check_vma=False,
    )
```

```python
import functools
import math

import jax
import jax.numpy as jnp
from jax import lax
from jax.experimental import pallas as pl
from jax.experimental.pallas import tpu as pltpu
from jax.sharding import PartitionSpec as P

softening = 0.05
proxy_radius = 1.5
ridge_share = 0.05
NBLK = 32
BLOCK = 256
ROWS = 16
DEPTH = 64

SIN = (4.44287959, -7.30781805, 3.59778873, -0.79123822)
COS_TILE = (1.41420408, -6.97764206, 5.7152384, -1.72834866)
COS = (1.4142135381698608, -6.978850841522217, 5.739460468292236, -1.883557915687561, 0.3106880187988281)

HBM = pl.BlockSpec(memory_space=pltpu.HBM)
VMEM = pl.BlockSpec(memory_space=pltpu.VMEM)
SMEM = pl.BlockSpec(memory_space=pltpu.SMEM)
MESH = pl.DeviceIdType.MESH
F32 = jnp.float32
BF16 = jnp.bfloat16


def params(**more):
    return pltpu.CompilerParams(vmem_limit_bytes=24 * 1024 * 1024, **more)


def horner(coefficients, z):
    total = coefficients[-1] * z + coefficients[-2]
    for one in coefficients[-3::-1]:
        total = total * z + one
    return total


def kernel_values(square, cosine):
    inverse = lax.rsqrt(square)
    turns = square * inverse
    part = turns - jnp.floor(turns + 0.5)
    z = part * part
    amplitude = inverse * (1.0 / (2.0 * math.pi))
    sine = part * horner(SIN, z)
    scaled = amplitude * sine
    return amplitude - scaled * sine, scaled * horner(cosine, z)


def three(x):
    high = x.astype(BF16).astype(F32)
    rest = x - high
    mid = rest.astype(BF16).astype(F32)
    return high, mid, rest - mid


def row_three(block, row):
    third = lax.broadcasted_iota(jnp.int32, block.shape, 0) == 3
    return jnp.where(third, row, block)


def norm_of(points):
    return jnp.sum(points * points, axis=0, keepdims=True)


def stacked(groups):
    zero = jnp.zeros_like(groups[0])
    return jnp.concatenate(groups + [zero] * (DEPTH // 8 - len(groups)), axis=0).astype(BF16)


def target_rows(points):
    high, mid, low = three(points)
    n_high, n_mid, n_low = three(norm_of(points))
    return stacked([row_three(high, n_high), row_three(high, n_mid), row_three(mid, n_low),
                    row_three(high, 1.0), row_three(mid, 1.0), row_three(low, 1.0)])


def source_rows(points):
    high, mid, low = three(points)
    norm = norm_of(points) + 4.0 * softening * softening
    n_high, n_mid, n_low = three(norm)
    return stacked([row_three(-2.0 * high, 1.0), row_three(-2.0 * mid, 1.0),
                    row_three(-2.0 * high, 1.0), row_three(-2.0 * low, n_high),
                    row_three(-2.0 * mid, n_mid), row_three(-2.0 * high, n_low)])


def three_rows(points):
    rows = lax.broadcasted_iota(jnp.int32, points.shape, 0)
    return jnp.where(rows < 3, points, 0.0)


def shifted(points, code):
    code = jnp.where(code >= 13, code + 1, code)
    axis_row = lax.broadcasted_iota(jnp.int32, points.shape, 0)
    move = jnp.where(
        axis_row == 0,
        (code // 9 - 1).astype(F32),
        jnp.where(axis_row == 1, ((code // 3) % 3 - 1).astype(F32), (code % 3 - 1).astype(F32)),
    )
    return three_rows(2.0 * (points + (move - 0.5)))


def centred(points):
    return three_rows(2.0 * (points - 0.5))


def slot_of(nb_ref, row, entry, box_count, box_total):
    owner_box = nb_ref[row, entry]
    step = owner_box // box_count - lax.axis_index("box") + 1
    step = jnp.where(step < 0, step + box_total, step)
    step = jnp.where(step >= box_total, step - box_total, step)
    return step * box_count + owner_box % box_count


def dot_tn(a, b):
    return lax.dot_general(a, b, (((0,), (0,)), ((), ())), preferred_element_type=F32)


def meet(peers):
    barrier = pltpu.get_barrier_semaphore()
    for peer in peers:
        pl.semaphore_signal(barrier, inc=1, device_id=peer, device_id_type=MESH)
    return lambda: pl.semaphore_wait(barrier, len(peers))


def send(source, target, sends, recvs, index, peer):
    one = pltpu.make_async_remote_copy(
        src_ref=source, dst_ref=target, send_sem=sends.at[index], recv_sem=recvs.at[index],
        device_id=peer, device_id_type=MESH)
    one.start()
    return one


def exchange_kernel(box_total, col_count, group, skeleton, points_ref, order_ref, proxy_ref,
                    pivot_ref, points_out, proxy_out, pivot_out, points, order, sends, recvs,
                    local):
    me = lax.axis_index("col")
    place = lax.axis_index("box")
    box_count, _, count = points_ref.shape
    after = {"box": lax.rem(place + 1, box_total)}
    before = {"box": lax.rem(place + box_total - 1, box_total)}
    across = {"col": lax.rem(me + group, col_count)}
    mine = me // group
    own = ((points_ref, points), (order_ref, order), (proxy_ref, proxy_out.at[0]),
           (pivot_ref, pivot_out.at[mine]))
    loads = []
    for i, (source, target) in enumerate(own):
        copy = pltpu.make_async_copy(source, target, local.at[i])
        copy.start()
        loads.append(copy)
    arrived = meet([before, after, across])
    for copy in loads:
        copy.wait()
    width = (count - skeleton) // col_count
    for box in range(box_count):
        row = order[box:box + 1, :]
        strips = [row[:, skeleton + s * width:skeleton + (s + 1) * width]
                  for c in range(group) for s in range(c, col_count, group)]
        row = jnp.concatenate([row[:, 0:skeleton]] + strips, axis=1)
        one_hot = (lax.broadcasted_iota(jnp.int32, (count, count), 0) == row).astype(F32)
        whole = jnp.concatenate([points[box], jnp.zeros((5, count), F32)], axis=0)
        rows = jnp.concatenate(list(three(whole)) + [jnp.zeros_like(whole)], axis=0)
        picked = jnp.dot(rows.astype(BF16), one_hot.astype(BF16), preferred_element_type=F32)
        points_out[1, box] = (picked[0:8] + picked[8:16]) + picked[16:24]
    arrived()
    jobs = [
        send(points_out.at[1], points_out.at[0], sends, recvs, 0, after),
        send(points_out.at[1], points_out.at[2], sends, recvs, 1, before),
        send(proxy_ref, proxy_out.at[1], sends, recvs, 2, across),
        send(pivot_ref, pivot_out.at[mine], sends, recvs, 3, across),
    ]
    for copy in jobs:
        copy.wait()


def tile_kernel(box_total, entries, group, skeleton, nb_hbm, place_hbm, points_ref, proxy_ref,
                gram_ref, rest_ref, nb_ref, place_ref, targets, sources, tiles, total, local):
    count = points_ref.shape[3]
    box_count, _, share = proxy_ref.shape
    proxies = box_count * share
    me = lax.axis_index("col")
    box = me // group
    first = lax.rem(me, group) * entries
    loads = [pltpu.make_async_copy(nb_hbm, nb_ref, local.at[0]),
             pltpu.make_async_copy(place_hbm, place_ref, local.at[1])]
    for copy in loads:
        copy.start()
    sources[...] = source_rows(centred(points_ref[1, box]))
    for d in range(box_count):
        directions = jnp.concatenate([proxy_ref[d], jnp.zeros((5, share), F32)], axis=0)
        targets[:, d * share:(d + 1) * share] = target_rows((2.0 * proxy_radius) * directions)
    for copy in loads:
        copy.wait()
    for k in range(entries):
        slot = slot_of(nb_ref, box, first + k, box_count, box_total)
        here = shifted(points_ref[slot // box_count, slot % box_count], place_ref[box, first + k])
        targets[:, proxies + k * count:proxies + (k + 1) * count] = target_rows(here)
    block = tiles.shape[1] // 2

    def evaluate(base, slot):
        squares = dot_tn(targets[:, pl.ds(pl.multiple_of(base, block), block)], sources[...])
        for i in range(block // ROWS):
            inner = slice(i * ROWS, (i + 1) * ROWS)
            lower = slice(block + i * ROWS, block + (i + 1) * ROWS)
            for c in range(0, count, 256):
                here = slice(c, c + 256)
                there = slice(count + c, count + c + 256)
                real, imag = kernel_values(squares[inner, here], COS_TILE)
                real = real.astype(BF16)
                imag = imag.astype(BF16)
                tiles[slot, inner, here] = real
                tiles[slot, inner, there] = imag
                tiles[slot, lower, here] = imag
                tiles[slot, lower, there] = -real

    def gather(slot):
        total[...] += dot_tn(tiles[slot, :, 0:skeleton], tiles[slot])

    total[...] = jnp.zeros_like(total)
    evaluate(0, 0)
    for i in range(1, proxies // block):
        gather((i + 1) % 2)
        evaluate(i * block, i % 2)
    parity = (proxies // block) % 2
    per = count // block

    @pl.loop(0, entries)
    def _(k):
        base = proxies + k * count
        for i in range(per):
            gather((parity + i + 1) % 2)
            evaluate(base + i * block, (parity + i) % 2)

    gather((parity + per - 1) % 2)
    half = (count - skeleton) // group
    for p in range(2):
        gram_ref[p] = total[:, p * count:p * count + skeleton]
        for c in range(group):
            start = p * count + skeleton + c * half
            rest_ref[c, p] = total[:, start:start + half]


def swap_kernel(gram_ref, rest_ref, gram_out, rest_out, sends, recvs):
    me = lax.axis_index("col")
    side = lax.rem(me, 2)
    peer = {"col": me + 1 - 2 * side}
    meet([peer])()
    copies = []
    for i in range(2):
        copies.append(send(gram_ref.at[i], gram_out.at[i], sends, recvs, i, peer))
    for i in range(2):
        copies.append(send(rest_ref.at[1 - side, i], rest_out.at[i], sends, recvs, 2 + i, peer))
    for copy in copies:
        copy.wait()


def lanes(block, k):
    return jnp.take_along_axis(block, jnp.full(block.shape, k, jnp.int32), axis=1)


def across_rows(block, k):
    return jnp.broadcast_to(block[k:k + 1, :], block.shape)


def block_inverse(re, im, start, home):
    count = len(re)
    shape = re[0].shape
    lane = lax.broadcasted_iota(jnp.int32, shape, 1)
    sub = lax.broadcasted_iota(jnp.int32, shape, 0)
    inside = (lane >= start) & (lane < start + 8 * count)
    re = [jnp.where(inside, block, jnp.where(lane - home == sub + 8 * v, 1.0, 0.0))
          for v, block in enumerate(re)]
    im = [jnp.where(inside, block, 0.0) for block in im]
    for r in range(count):
        order = [r] + [v for v in range(count) if v > r] + list(range(r))
        spread = {}
        for v in order:
            for j in range(8):
                k = start + 8 * r + j
                spread[v, j] = (lanes(re[v], k), lanes(im[v], k))
        cols = {j: spread[r, j] for j in range(8)}
        cols["row"] = (re[r], im[r])
        for t in range(0, 8, 2):
            (ar, ai), (cr, ci) = cols.pop(t), cols.pop(t + 1)
            a, d = across_rows(ar, t), across_rows(cr, t + 1)
            br, bi = across_rows(cr, t), across_rows(ci, t)
            scale = 1.0 / (a * d - (br * br + bi * bi))
            a, d, br, bi = a * scale, d * scale, br * scale, bi * scale
            at, on = sub == t, sub == t + 1
            here = at | on
            e0r = jnp.where(at, -d, jnp.where(on, br, ar * d - (cr * br + ci * bi)))
            e0i = jnp.where(at, 0.0, jnp.where(on, -bi, ai * d - (ci * br - cr * bi)))
            e1r = jnp.where(at, br, jnp.where(on, -a, cr * a - (ar * br - ai * bi)))
            e1i = jnp.where(at, bi, jnp.where(on, 0.0, ci * a - (ar * bi + ai * br)))
            for key, (xr, xi) in cols.items():
                x0r, x0i = across_rows(xr, t), across_rows(xi, t)
                x1r, x1i = across_rows(xr, t + 1), across_rows(xi, t + 1)
                lessr = (e0r * x0r - e0i * x0i) + (e1r * x1r - e1i * x1i)
                lessi = (e0r * x0i + e0i * x0r) + (e1r * x1i + e1i * x1r)
                cols[key] = (jnp.where(here, 0.0, xr) - lessr, jnp.where(here, 0.0, xi) - lessi)
            if t < 6:
                yield None
        re[r], im[r] = cols["row"]
        rows = [(across_rows(re[r], j), across_rows(im[r], j)) for j in range(8)]
        for v in order[1:]:
            lessr = [spread[v, j][0] * rows[j][0] - spread[v, j][1] * rows[j][1]
                     for j in range(8)]
            lessi = [spread[v, j][0] * rows[j][1] + spread[v, j][1] * rows[j][0]
                     for j in range(8)]
            re[v] = re[v] - summed(lessr)
            im[v] = im[v] - summed(lessi)
        yield jnp.concatenate(re, axis=0), jnp.concatenate(im, axis=0)


def summed(terms):
    while len(terms) > 1:
        terms = [terms[i] + terms[i + 1] for i in range(0, len(terms), 2)]
    return terms[0]


def plain(a, b):
    return jnp.dot(a, b, preferred_element_type=F32)


def solve_kernel(group, gram_ref, rest_ref, gram_in, rest_in, x_ref, mat, head, tail):
    n = x_ref.shape[1]
    nb = NBLK
    side = lax.rem(lax.axis_index("col"), group)
    diagonal = lax.broadcasted_iota(jnp.int32, (128, 128), 0) == lax.broadcasted_iota(
        jnp.int32, (128, 128), 1
    )
    gram = gram_ref[...] + gram_in[...]
    ridge = 0.0
    for c in range(0, n, 128):
        ridge = ridge + jnp.where(diagonal, gram[0, c:c + 128, c:c + 128], 0.0)
    ridge = ridge_share * jnp.sum(ridge) / n
    mat[:, :, 0:n] = gram
    for c in range(0, n, 128):
        here = slice(c, c + 128)
        mat[0, here, here] = gram[0, here, here] + jnp.where(diagonal, ridge, 0.0)
    mat[:, :, n:] = rest_ref[side] + rest_in[...]
    head[...] = jnp.zeros_like(head)
    tail[...] = jnp.zeros_like(tail)

    def pick(block):
        return [block[8 * v:8 * v + 8] for v in range(nb // 8)]

    def put(ref, at, w, re, im):
        where = slice(256 * w, 256 * w + 256)
        for base, block in ((at, [re, im]), (128 + at, [-im, re])):
            high, rest = split(jnp.concatenate(block, axis=1))
            ref[0, base:base + nb, where] = high
            ref[1, base:base + nb, where] = rest

    def clear(ref, at):
        for base in (at, 128 + at):
            ref[:, base:base + nb, :] = jnp.zeros((2, nb, ref.shape[2]), BF16)

    def doubled(re, im):
        return jnp.concatenate(split(jnp.concatenate([re, im], axis=1)), axis=0)

    def product(left, ref, w):
        where = slice(256 * w, 256 * w + 256)
        half = left.shape[0] // 2
        both = plain(left, ref[0, :, where])
        return both[0:half] + (both[half:] + plain(left[0:half], ref[1, :, where]))

    for step in block_inverse(pick(mat[0, 0:nb, 0:128]), pick(mat[1, 0:nb, 0:128]), 0, nb):
        found = step or None
    for j in range(n // nb):
        rows = slice(j * nb, (j + 1) * nb)
        after = slice((j + 1) * nb, (j + 2) * nb)
        q = (j * nb) // 128 * 128
        at = j * nb - q
        home = (at + nb) % 128
        windows = list(range((j + 1) * nb // 128, mat.shape[2] // 128))
        factor = doubled(*found)
        left = doubled(mat[0, :, q:q + 128], mat[1, :, q:q + 128])
        held = {}

        def solve(w):
            here = slice(128 * w, 128 * w + 128)
            put(head, home, w, mat[0, rows, here], mat[1, rows, here])
            held[w] = product(factor, head, w)
            put(tail, at, w, held[w][:, 0:128], held[w][:, 128:])

        def change(w):
            here = slice(128 * w, 128 * w + 128)
            less = product(left, tail, w)
            mat[0, :, here] = mat[0, :, here] - less[:, 0:128]
            mat[1, :, here] = mat[1, :, here] - less[:, 128:]
            mat[0, rows, here] = held[w][:, 0:128]
            mat[1, rows, here] = held[w][:, 128:]

        first = windows[0]
        solve(first)
        pivots = iter(())
        if (j + 1) * nb < n:
            here = slice(128 * first, 128 * first + 128)
            ahead = jnp.concatenate([left[after], left[n + (j + 1) * nb:n + (j + 2) * nb]], axis=0)
            less = product(ahead, tail, first)
            to = (j + 1) * nb % 128
            pivots = block_inverse(pick(mat[0, after, here] - less[:, 0:128]),
                                   pick(mat[1, after, here] - less[:, 128:]),
                                   to, (to + nb) % 128)
        tasks = [functools.partial(solve, w) for w in windows[1:]]
        tasks += [functools.partial(change, w) for w in windows]
        tasks.append(functools.partial(clear, head, home))
        tasks.append(functools.partial(clear, tail, at))
        steps = nb // 2
        done = 0
        for i, task in enumerate(tasks):
            task()
            upto = (i + 1) * steps // len(tasks)
            for _ in range(upto - done):
                found = next(pivots, None) or found
            done = upto
        for step in pivots:
            found = step or found
    x_ref[...] = mat[:, :, n:]


def split(x):
    high = x.astype(BF16)
    return high, (x - high.astype(F32)).astype(BF16)


def threefold(a, b, dims=((1,), (0,))):
    def one(x, y):
        return lax.dot_general(x, y, (dims, ((), ())), preferred_element_type=F32)

    return one(a[0], b[0]) + (one(a[0], b[1]) + one(a[1], b[0]))


def right_side(x):
    xr, xi = x[0], x[1]
    return split(jnp.concatenate(
        [jnp.concatenate([xr, xi], axis=1), jnp.concatenate([-xi, xr], axis=1)], axis=0))


def pivot_rows(pivot_ref, box):
    pieces = range(pivot_ref.shape[0])
    return [jnp.concatenate([pivot_ref[c, box, p:p + 1, :] for c in pieces], axis=1)
            for p in range(2)]


def fold(left, rest, right, pivots, rows, weighted, out_ref, slot):
    qr, qi = pivots
    width = qr.shape[1]
    held = weighted.shape[1] // 2
    both = rest - threefold(left, right)
    br, bi = both[:, 0:width], both[:, width:]
    wr = br * qr - bi * qi
    wi = br * qi + bi * qr
    weighted[0] = jnp.concatenate([wr, -wi], axis=1)
    weighted[1] = jnp.concatenate([wi, wr], axis=1)
    upper = jnp.concatenate([weighted[0, rows, :], weighted[1, rows, :]], axis=0)
    update = threefold(split(upper), split(both), ((1,), (1,)))
    half = update.shape[0] // 2
    out_ref[slot, 0] = out_ref[slot, 0] - update[0:half]
    out_ref[slot, 1] = out_ref[slot, 1] - update[half:]


def row_half(col_count, group, n):
    count = n // (col_count // group)
    me = lax.axis_index("col")
    return pl.ds(pl.multiple_of((me // group) * count, count), count)


def spread(squares, keep):
    for i in range(0, squares.shape[0], ROWS):
        inner = slice(i, i + ROWS)
        for c in range(0, squares.shape[1], 128):
            real, imag = kernel_values(squares[inner, c:c + 128], COS)
            keep(inner, c, real, imag)


def near_kernel(box_total, col_count, group, nb_ref, place_ref, points_ref, x_ref, pivot_ref,
                out_ref, high_ref, low_ref, rest_ref, sources, left, rest, weighted):
    n = x_ref.shape[1]
    width = x_ref.shape[2]
    box_count, _, count = points_ref.shape[1:]
    entries = nb_ref.shape[1]
    me = lax.axis_index("col")
    side = lax.rem(me, group)
    box = me // group
    fed = 1 - box
    out_ref[...] = jnp.zeros_like(out_ref)
    for i, which in enumerate((box, fed)):
        whole = source_rows(centred(points_ref[1, which]))
        half = whole[:, n:n + width]
        for c in range(1, group):
            half = jnp.where(side == c, whole[:, n + c * width:n + (c + 1) * width], half)
        sources[i, :, 0:n] = whole[:, 0:n]
        sources[i, :, n:] = half
    right = right_side(x_ref)
    pivots = pivot_rows(pivot_ref, box)
    rows = row_half(col_count, group, n)

    def evaluate(i, which, k, high, low, rest_at):
        slot = slot_of(nb_ref, which, k, box_count, box_total)
        here = shifted(points_ref[slot // box_count, slot % box_count], place_ref[which, k])
        squares = dot_tn(target_rows(here[:, 0:n]), sources[i])

        def keep(inner, c, real, imag):
            for p, value in enumerate((real, imag)):
                if c < n:
                    top, bottom = split(value)
                    high[inner, p * n + c:p * n + c + 128] = top
                    low[inner, p * n + c:p * n + c + 128] = bottom
                else:
                    rest_at[inner, p * width + c - n:p * width + c - n + 128] = value

        spread(squares, keep)

    def own(k, slot):
        evaluate(0, box, k, left.at[slot, 0], left.at[slot, 1], rest.at[slot])

    def other(k):
        evaluate(1, fed, k, high_ref.at[k], low_ref.at[k], rest_ref.at[k])

    def use(k, slot):
        to = slot_of(nb_ref, box, k, box_count, box_total)
        fold((left[slot, 0], left[slot, 1]), rest[slot], right, pivots, rows, weighted, out_ref,
             to)

    own(0, 0)

    @pl.loop(0, entries // 2)
    def _(pair):
        k = 2 * pair
        own(k + 1, 1)
        other(k)
        use(k, 0)
        own(jnp.minimum(k + 2, entries - 1), 0)
        other(k + 1)
        use(k + 1, 1)


def far_kernel(box_total, col_count, group, nb_ref, buf_ref, high_ref, low_ref, rest_ref, x_ref,
               mine_ref, pivot_ref, out_ref, inter_ref, weighted):
    n = x_ref.shape[1]
    entries, _, _ = rest_ref.shape
    me = lax.axis_index("col")
    box = me // group
    fed = 1 - box
    box_count = pivot_ref.shape[1]
    out_ref[...] = buf_ref[...]
    right = right_side(x_ref)
    pivots = pivot_rows(pivot_ref, fed)
    rows = row_half(col_count, group, n)
    strip = inter_ref.shape[2]
    for p in range(2):
        for ref, where in ((mine_ref, box), (x_ref, fed)):
            block = jnp.transpose(ref[p])
            piece = block[0:strip]
            for c in range(1, block.shape[0] // strip):
                piece = jnp.where(box == c, block[c * strip:(c + 1) * strip], piece)
            inter_ref[where, p] = piece

    @pl.loop(0, entries // 2)
    def _(pair):
        for i in range(2):
            k = 2 * pair + i
            to = slot_of(nb_ref, fed, k, box_count, box_total)
            fold((high_ref[k], low_ref[k]), rest_ref[k], right, pivots, rows, weighted.at[i],
                 out_ref, to)


def reduce_kernel(box_total, buf_ref, out_ref, pair_in, line_out, line_in, side_out, side_in,
                  held, sends, recvs):
    me = lax.axis_index("col")
    place = lax.axis_index("box")
    side = lax.rem(me, 2)
    odd = lax.rem(place, 2)
    near = {"col": me + 1 - 2 * side}
    relay = {"box": lax.rem(place + box_total + 4 * odd - 2, box_total)}
    source = {"box": lax.rem(place + box_total + 2 - 4 * odd, box_total)}
    twin = {"box": place + 1 - 2 * odd}
    meet([near, relay, source, twin])()
    box_count = out_ref.shape[0]
    order = (2 * odd, 2 - 2 * odd, 1)
    chunks = [(d, p) for d in range(box_count) for p in range(2)]
    pairs = {}
    for g, at in enumerate(order):
        for i, (d, p) in enumerate(chunks):
            pairs[g, i] = send(buf_ref.at[at * box_count + d, p, 1 - side], pair_in.at[g, d, p],
                               sends, recvs, len(chunks) * g + i, near)
    base = 3 * len(chunks)
    lines, sides = [], []
    for i, (d, p) in enumerate(chunks):
        pairs[0, i].wait()
        line_out[d, p] = buf_ref[order[0] * box_count + d, p, side] + pair_in[0, d, p]
        lines.append(send(line_out.at[d, p], line_in.at[d, p], sends, recvs, base + i, relay))
    for i, (d, p) in enumerate(chunks):
        pairs[1, i].wait()
        held[d, p] = buf_ref[order[1] * box_count + d, p, side] + pair_in[1, d, p]
    for i, (d, p) in enumerate(chunks):
        lines[i].wait()
        side_out[d, p] = held[d, p] + line_in[d, p]
        sides.append(send(side_out.at[d, p], side_in.at[d, p], sends, recvs,
                          base + len(chunks) + i, twin))
    for i, (d, p) in enumerate(chunks):
        pairs[2, i].wait()
        held[d, p] = buf_ref[box_count + d, p, side] + pair_in[2, d, p]
    for i, (d, p) in enumerate(chunks):
        sides[i].wait()
        out_ref[d, p] = held[d, p] + side_in[d, p]


def ring(count, step):
    return [(i, (i + step) % count) for i in range(count)]


def on_device(
    box_points, proxy_directions, point_order, neighbour_boxes, neighbour_places, pivot_inverse
):
    box_count, _, point_count = box_points.shape
    col_count = lax.axis_size("col")
    box_total = lax.axis_size("box")
    group = col_count // box_count
    listed = neighbour_boxes.shape[1]
    entries = listed // group
    width = pivot_inverse.shape[2]
    rest = width * col_count
    skeleton = point_count - rest
    half = rest // group
    share = proxy_directions.shape[1]
    dma = pltpu.SemaphoreType.DMA

    points, proxies, pivots = pl.pallas_call(
        functools.partial(exchange_kernel, box_total, col_count, group, skeleton),
        out_shape=(
            jax.ShapeDtypeStruct((3, box_count, 8, point_count), F32),
            jax.ShapeDtypeStruct((box_count,) + proxy_directions.shape, F32),
            jax.ShapeDtypeStruct((box_count,) + pivot_inverse.shape, F32),
        ),
        in_specs=[HBM] * 4,
        out_specs=(VMEM,) * 3,
        scratch_shapes=[pltpu.VMEM(box_points.shape, F32),
                        pltpu.VMEM(point_order.shape, jnp.int32),
                        dma((4,)), dma((4,)), dma((4,))],
        compiler_params=params(collective_id=0, has_side_effects=True),
    )(box_points, point_order, proxy_directions, pivot_inverse)

    rows = box_count * share + entries * point_count
    gram, right = pl.pallas_call(
        functools.partial(tile_kernel, box_total, entries, group, skeleton),
        out_shape=(
            jax.ShapeDtypeStruct((2, skeleton, skeleton), F32),
            jax.ShapeDtypeStruct((group, 2, skeleton, half), F32),
        ),
        in_specs=[HBM, HBM, VMEM, VMEM],
        out_specs=(VMEM, VMEM),
        scratch_shapes=[
            pltpu.SMEM(neighbour_boxes.shape, jnp.int32),
            pltpu.SMEM(neighbour_places.shape, jnp.int32),
            pltpu.VMEM((DEPTH, rows), BF16),
            pltpu.VMEM((DEPTH, point_count), BF16),
            pltpu.VMEM((2, 2 * BLOCK, 2 * point_count), BF16),
            pltpu.VMEM((skeleton, 2 * point_count), F32),
            dma((2,)),
        ],
        compiler_params=params(),
    )(neighbour_boxes, neighbour_places, points, proxies)

    gram_in, right_in = pl.pallas_call(
        swap_kernel,
        out_shape=(jax.ShapeDtypeStruct(gram.shape, F32),
                   jax.ShapeDtypeStruct(right.shape[1:], F32)),
        in_specs=[VMEM, VMEM],
        out_specs=(VMEM, VMEM),
        scratch_shapes=[dma((4,)), dma((4,))],
        compiler_params=params(collective_id=2, has_side_effects=True),
    )(gram, right)
    solved = pl.pallas_call(
        functools.partial(solve_kernel, group),
        out_shape=jax.ShapeDtypeStruct((2, skeleton, half), F32),
        in_specs=[VMEM] * 4,
        out_specs=VMEM,
        scratch_shapes=[
            pltpu.VMEM((2, skeleton, skeleton + half), F32),
            pltpu.VMEM((2, 256, 2 * (skeleton + half)), BF16),
            pltpu.VMEM((2, 256, 2 * (skeleton + half)), BF16),
        ],
        compiler_params=params(),
    )(gram, right, gram_in, right_in)
    arrived = lax.ppermute(solved, "col", ring(col_count, group))

    strips = skeleton // box_count
    buffer, high, low, kept = pl.pallas_call(
        functools.partial(near_kernel, box_total, col_count, group),
        out_shape=(
            jax.ShapeDtypeStruct((3 * box_count, 2, strips, skeleton), F32),
            jax.ShapeDtypeStruct((listed, skeleton, 2 * skeleton), BF16),
            jax.ShapeDtypeStruct((listed, skeleton, 2 * skeleton), BF16),
            jax.ShapeDtypeStruct((listed, skeleton, 2 * half), F32),
        ),
        in_specs=[SMEM, SMEM, VMEM, VMEM, VMEM],
        out_specs=(VMEM,) * 4,
        scratch_shapes=[
            pltpu.VMEM((box_count, DEPTH, skeleton + half), BF16),
            pltpu.VMEM((2, 2, skeleton, 2 * skeleton), BF16),
            pltpu.VMEM((2, skeleton, 2 * half), F32),
            pltpu.VMEM((2, skeleton, 2 * half), F32),
        ],
        compiler_params=params(),
        cost_estimate=pl.CostEstimate(flops=4 * 10**9, bytes_accessed=8 * 10**6,
                                      transcendentals=0),
    )(neighbour_boxes, neighbour_places, points, solved, pivots)

    buffer, inter = pl.pallas_call(
        functools.partial(far_kernel, box_total, col_count, group),
        out_shape=(
            jax.ShapeDtypeStruct(buffer.shape, F32),
            jax.ShapeDtypeStruct((box_count, 2, width, skeleton), F32),
        ),
        in_specs=[SMEM] + [VMEM] * 7,
        out_specs=(VMEM, VMEM),
        scratch_shapes=[pltpu.VMEM((2, 2, skeleton, 2 * half), F32)],
        compiler_params=params(),
    )(neighbour_boxes, buffer, high, low, kept, arrived, solved, pivots)
    interpolation = jnp.swapaxes(inter, 2, 3)

    strip = skeleton // col_count
    block = (box_count, 2, strip, skeleton)
    jobs = 5 * 2 * box_count
    skeleton_update = pl.pallas_call(
        functools.partial(reduce_kernel, box_total),
        out_shape=jax.ShapeDtypeStruct(block, F32),
        in_specs=[VMEM],
        out_specs=VMEM,
        scratch_shapes=[
            pltpu.VMEM((3,) + block, F32),
            pltpu.VMEM(block, F32),
            pltpu.VMEM(block, F32),
            pltpu.VMEM(block, F32),
            pltpu.VMEM(block, F32),
            pltpu.VMEM(block, F32),
            dma((jobs,)),
            dma((jobs,)),
        ],
        compiler_params=params(collective_id=1, has_side_effects=True),
    )(buffer.reshape(3 * box_count, 2, group, strip, skeleton))
    return (interpolation, skeleton_update)


def solution(mesh):
    placed = (
        P("box", None, None),
        P(None, "col"),
        P("box", None),
        P("box", None),
        P("box", None),
        P("box", None, "col"),
    )
    return jax.shard_map(
        on_device,
        mesh=mesh,
        in_specs=placed,
        out_specs=(P("box", None, None, "col"), P("box", None, "col", None)),
        check_vma=False,
    )
```

```python
import functools
import math

import jax
import jax.numpy as jnp
from jax import lax
from jax.experimental import pallas as pl
from jax.experimental.pallas import tpu as pltpu
from jax.sharding import PartitionSpec as P

softening = 0.05
proxy_radius = 1.5
ridge_share = 0.05
NBLK = 32
BLOCK = 256
ROWS = 16
DEPTH = 64

SIN = (4.44287959, -7.30781805, 3.59778873, -0.79123822)
COS_TILE = (1.41420408, -6.97764206, 5.7152384, -1.72834866)
COS = (1.4142135381698608, -6.978850841522217, 5.739460468292236, -1.883557915687561, 0.3106880187988281)

HBM = pl.BlockSpec(memory_space=pltpu.HBM)
VMEM = pl.BlockSpec(memory_space=pltpu.VMEM)
SMEM = pl.BlockSpec(memory_space=pltpu.SMEM)
MESH = pl.DeviceIdType.MESH
F32 = jnp.float32
BF16 = jnp.bfloat16


def params(**more):
    return pltpu.CompilerParams(vmem_limit_bytes=24 * 1024 * 1024, **more)


def horner(coefficients, z):
    total = coefficients[-1] * z + coefficients[-2]
    for one in coefficients[-3::-1]:
        total = total * z + one
    return total


def kernel_values(square, cosine):
    inverse = lax.rsqrt(square)
    turns = square * inverse
    part = turns - jnp.floor(turns + 0.5)
    z = part * part
    amplitude = inverse * (1.0 / (2.0 * math.pi))
    sine = part * horner(SIN, z)
    scaled = amplitude * sine
    return amplitude - scaled * sine, scaled * horner(cosine, z)


def three(x):
    high = x.astype(BF16).astype(F32)
    rest = x - high
    mid = rest.astype(BF16).astype(F32)
    return high, mid, rest - mid


def row_three(block, row):
    third = lax.broadcasted_iota(jnp.int32, block.shape, 0) == 3
    return jnp.where(third, row, block)


def norm_of(points):
    return jnp.sum(points * points, axis=0, keepdims=True)


def stacked(groups):
    zero = jnp.zeros_like(groups[0])
    return jnp.concatenate(groups + [zero] * (DEPTH // 8 - len(groups)), axis=0).astype(BF16)


def target_rows(points):
    high, mid, low = three(points)
    n_high, n_mid, n_low = three(norm_of(points))
    return stacked([row_three(high, n_high), row_three(high, n_mid), row_three(mid, n_low),
                    row_three(high, 1.0), row_three(mid, 1.0), row_three(low, 1.0)])


def source_rows(points):
    high, mid, low = three(points)
    norm = norm_of(points) + 4.0 * softening * softening
    n_high, n_mid, n_low = three(norm)
    return stacked([row_three(-2.0 * high, 1.0), row_three(-2.0 * mid, 1.0),
                    row_three(-2.0 * high, 1.0), row_three(-2.0 * low, n_high),
                    row_three(-2.0 * mid, n_mid), row_three(-2.0 * high, n_low)])


def three_rows(points):
    rows = lax.broadcasted_iota(jnp.int32, points.shape, 0)
    return jnp.where(rows < 3, points, 0.0)


def shifted(points, code):
    code = jnp.where(code >= 13, code + 1, code)
    axis_row = lax.broadcasted_iota(jnp.int32, points.shape, 0)
    move = jnp.where(
        axis_row == 0,
        (code // 9 - 1).astype(F32),
        jnp.where(axis_row == 1, ((code // 3) % 3 - 1).astype(F32), (code % 3 - 1).astype(F32)),
    )
    return three_rows(2.0 * (points + (move - 0.5)))


def centred(points):
    return three_rows(2.0 * (points - 0.5))


def slot_of(nb_ref, row, entry, box_count, box_total):
    owner_box = nb_ref[row, entry]
    step = owner_box // box_count - lax.axis_index("box") + 1
    step = jnp.where(step < 0, step + box_total, step)
    step = jnp.where(step >= box_total, step - box_total, step)
    return step * box_count + owner_box % box_count


def dot_tn(a, b):
    return lax.dot_general(a, b, (((0,), (0,)), ((), ())), preferred_element_type=F32)


def meet(peers):
    barrier = pltpu.get_barrier_semaphore()
    for peer in peers:
        pl.semaphore_signal(barrier, inc=1, device_id=peer, device_id_type=MESH)
    return lambda: pl.semaphore_wait(barrier, len(peers))


def send(source, target, sends, recvs, index, peer):
    one = pltpu.make_async_remote_copy(
        src_ref=source, dst_ref=target, send_sem=sends.at[index], recv_sem=recvs.at[index],
        device_id=peer, device_id_type=MESH)
    one.start()
    return one


def exchange_kernel(box_total, col_count, group, skeleton, points_ref, order_ref, proxy_ref,
                    pivot_ref, points_out, proxy_out, pivot_out, points, order, sends, recvs,
                    local):
    me = lax.axis_index("col")
    place = lax.axis_index("box")
    _, box_count, count = points_ref.shape
    after = {"box": lax.rem(place + 1, box_total)}
    before = {"box": lax.rem(place + box_total - 1, box_total)}
    across = {"col": lax.rem(me + group, col_count)}
    mine = me // group
    own = ((points_ref, points), (order_ref, order), (proxy_ref, proxy_out.at[0]),
           (pivot_ref, pivot_out.at[mine]))
    loads = []
    for i, (source, target) in enumerate(own):
        copy = pltpu.make_async_copy(source, target, local.at[i])
        copy.start()
        loads.append(copy)
    arrived = meet([before, after, across])
    for copy in loads:
        copy.wait()
    width = (count - skeleton) // col_count
    for box in range(box_count):
        row = order[box:box + 1, :]
        strips = [row[:, skeleton + s * width:skeleton + (s + 1) * width]
                  for c in range(group) for s in range(c, col_count, group)]
        row = jnp.concatenate([row[:, 0:skeleton]] + strips, axis=1)
        one_hot = (lax.broadcasted_iota(jnp.int32, (count, count), 0) == row).astype(F32)
        whole = jnp.concatenate([points[axis, box:box + 1, :] for axis in range(3)]
                                + [jnp.zeros((5, count), F32)], axis=0)
        rows = jnp.concatenate(list(three(whole)) + [jnp.zeros_like(whole)], axis=0)
        picked = jnp.dot(rows.astype(BF16), one_hot.astype(BF16), preferred_element_type=F32)
        points_out[1, box] = (picked[0:8] + picked[8:16]) + picked[16:24]
    arrived()
    jobs = [
        send(points_out.at[1], points_out.at[0], sends, recvs, 0, after),
        send(points_out.at[1], points_out.at[2], sends, recvs, 1, before),
        send(proxy_ref, proxy_out.at[1], sends, recvs, 2, across),
        send(pivot_ref, pivot_out.at[mine], sends, recvs, 3, across),
    ]
    for copy in jobs:
        copy.wait()


def tile_kernel(box_total, entries, group, skeleton, nb_ref, place_ref, points_ref, proxy_ref,
                cross_ref, targets, sources, squares, tiles, total):
    count = points_ref.shape[3]
    box_count, _, share = proxy_ref.shape
    proxies = box_count * share
    me = lax.axis_index("col")
    box = me // group
    first = lax.rem(me, group) * entries
    sources[...] = source_rows(centred(points_ref[1, box]))
    for d in range(box_count):
        directions = jnp.concatenate([proxy_ref[d], jnp.zeros((5, share), F32)], axis=0)
        targets[:, d * share:(d + 1) * share] = target_rows((2.0 * proxy_radius) * directions)
    for k in range(entries):
        slot = slot_of(nb_ref, box, first + k, box_count, box_total)
        here = shifted(points_ref[slot // box_count, slot % box_count], place_ref[box, first + k])
        targets[:, proxies + k * count:proxies + (k + 1) * count] = target_rows(here)
    block = tiles.shape[1] // 2

    def measure(base, slot):
        squares[slot] = dot_tn(targets[:, pl.ds(pl.multiple_of(base, block), block)],
                               sources[...])

    def evaluate(slot, i):
        inner = slice(i * ROWS, (i + 1) * ROWS)
        lower = slice(block + i * ROWS, block + (i + 1) * ROWS)
        for c in range(0, count, 256):
            here = slice(c, c + 256)
            there = slice(count + c, count + c + 256)
            real, imag = kernel_values(squares[slot, inner, here], COS_TILE)
            real = real.astype(BF16)
            imag = imag.astype(BF16)
            tiles[slot, inner, here] = real
            tiles[slot, inner, there] = imag
            tiles[slot, lower, here] = imag
            tiles[slot, lower, there] = -real

    def gather(slot, left, c):
        here = slice(c, c + 256)
        total[:, here] += plain(left, tiles[slot, :, here])

    def stage(ahead, now, before):
        measure(*ahead)
        steps = block // ROWS
        pieces = 2 * count // 256
        left = None if before is None else jnp.transpose(tiles[before, :, 0:skeleton])
        for i in range(steps):
            if left is not None and i % (steps // pieces) == 0:
                gather(before, left, i // (steps // pieces) * 256)
            evaluate(now, i)

    total[...] = jnp.zeros_like(total)
    blocks = proxies // block
    measure(0, 0)
    for i in range(blocks):
        stage(((i + 1) * block, (i + 1) % 2), i % 2, (i + 1) % 2 if i else None)
    per = count // block
    last = proxies + (entries * per - 1) * block

    @pl.loop(0, entries)
    def _(k):
        base = proxies + k * count
        for i in range(per):
            now = (blocks + i) % 2
            stage((jnp.minimum(base + (i + 1) * block, last), 1 - now), now, 1 - now)

    end = (blocks + per - 1) % 2
    left = jnp.transpose(tiles[end, :, 0:skeleton])
    for c in range(0, 2 * count, 256):
        gather(end, left, c)
    for p in range(2):
        cross_ref[p] = total[:, p * count:(p + 1) * count]


def lanes(block, k):
    return jnp.take_along_axis(block, jnp.full(block.shape, k, jnp.int32), axis=1)


def across_rows(block, k):
    return jnp.broadcast_to(block[k:k + 1, :], block.shape)


def block_inverse(re, im, start, home):
    count = len(re)
    shape = re[0].shape
    lane = lax.broadcasted_iota(jnp.int32, shape, 1)
    sub = lax.broadcasted_iota(jnp.int32, shape, 0)
    inside = (lane >= start) & (lane < start + 8 * count)
    re = [jnp.where(inside, block, jnp.where(lane - home == sub + 8 * v, 1.0, 0.0))
          for v, block in enumerate(re)]
    im = [jnp.where(inside, block, 0.0) for block in im]
    for r in range(count):
        order = [r] + [v for v in range(count) if v > r] + list(range(r))
        spread = {}
        for v in order:
            for j in range(8):
                k = start + 8 * r + j
                spread[v, j] = (lanes(re[v], k), lanes(im[v], k))
        cols = {j: spread[r, j] for j in range(8)}
        cols["row"] = (re[r], im[r])
        for t in range(0, 8, 2):
            (ar, ai), (cr, ci) = cols.pop(t), cols.pop(t + 1)
            a, d = across_rows(ar, t), across_rows(cr, t + 1)
            br, bi = across_rows(cr, t), across_rows(ci, t)
            scale = 1.0 / (a * d - (br * br + bi * bi))
            a, d, br, bi = a * scale, d * scale, br * scale, bi * scale
            at, on = sub == t, sub == t + 1
            here = at | on
            e0r = jnp.where(at, -d, jnp.where(on, br, ar * d - (cr * br + ci * bi)))
            e0i = jnp.where(at, 0.0, jnp.where(on, -bi, ai * d - (ci * br - cr * bi)))
            e1r = jnp.where(at, br, jnp.where(on, -a, cr * a - (ar * br - ai * bi)))
            e1i = jnp.where(at, bi, jnp.where(on, 0.0, ci * a - (ar * bi + ai * br)))
            for key, (xr, xi) in cols.items():
                x0r, x0i = across_rows(xr, t), across_rows(xi, t)
                x1r, x1i = across_rows(xr, t + 1), across_rows(xi, t + 1)
                lessr = (e0r * x0r - e0i * x0i) + (e1r * x1r - e1i * x1i)
                lessi = (e0r * x0i + e0i * x0r) + (e1r * x1i + e1i * x1r)
                cols[key] = (jnp.where(here, 0.0, xr) - lessr, jnp.where(here, 0.0, xi) - lessi)
            if t < 6:
                yield None
        re[r], im[r] = cols["row"]
        rows = [(across_rows(re[r], j), across_rows(im[r], j)) for j in range(8)]
        for v in order[1:]:
            lessr = [spread[v, j][0] * rows[j][0] - spread[v, j][1] * rows[j][1]
                     for j in range(8)]
            lessi = [spread[v, j][0] * rows[j][1] + spread[v, j][1] * rows[j][0]
                     for j in range(8)]
            re[v] = re[v] - summed(lessr)
            im[v] = im[v] - summed(lessi)
        yield jnp.concatenate(re, axis=0), jnp.concatenate(im, axis=0)


def summed(terms):
    while len(terms) > 1:
        terms = [terms[i] + terms[i + 1] for i in range(0, len(terms), 2)]
    return terms[0]


def plain(a, b):
    return jnp.dot(a, b, preferred_element_type=F32)


def solve_kernel(group, cross_ref, cross_in, x_ref, mat, head, tail):
    n = x_ref.shape[1]
    width = x_ref.shape[2]
    nb = NBLK
    side = lax.rem(lax.axis_index("col"), group)
    diagonal = lax.broadcasted_iota(jnp.int32, (128, 128), 0) == lax.broadcasted_iota(
        jnp.int32, (128, 128), 1
    )
    gram = cross_ref[:, :, 0:n] + cross_in[:, :, 0:n]
    ridge = 0.0
    for c in range(0, n, 128):
        ridge = ridge + jnp.where(diagonal, gram[0, c:c + 128, c:c + 128], 0.0)
    ridge = ridge_share * jnp.sum(ridge) / n
    mat[:, :, 0:n] = gram
    for c in range(0, n, 128):
        here = slice(c, c + 128)
        mat[0, here, here] = gram[0, here, here] + jnp.where(diagonal, ridge, 0.0)
    mine = pl.ds(pl.multiple_of(n + side * width, 128), width)
    mat[:, :, n:] = cross_ref[:, :, mine] + cross_in[:, :, mine]
    head[...] = jnp.zeros_like(head)
    tail[...] = jnp.zeros_like(tail)

    def pick(block):
        return [block[8 * v:8 * v + 8] for v in range(nb // 8)]

    def put(ref, at, w, re, im):
        where = slice(256 * w, 256 * w + 256)
        for base, block in ((at, [re, im]), (128 + at, [-im, re])):
            high, rest = split(jnp.concatenate(block, axis=1))
            ref[0, base:base + nb, where] = high
            ref[1, base:base + nb, where] = rest

    def clear(ref, at):
        for base in (at, 128 + at):
            ref[:, base:base + nb, :] = jnp.zeros((2, nb, ref.shape[2]), BF16)

    def doubled(re, im):
        return jnp.concatenate(split(jnp.concatenate([re, im], axis=1)), axis=0)

    def product(left, ref, w):
        where = slice(256 * w, 256 * w + 256)
        half = left.shape[0] // 2
        both = plain(left, ref[0, :, where])
        return both[0:half] + (both[half:] + plain(left[0:half], ref[1, :, where]))

    for step in block_inverse(pick(mat[0, 0:nb, 0:128]), pick(mat[1, 0:nb, 0:128]), 0, nb):
        found = step or None
    for j in range(n // nb):
        rows = slice(j * nb, (j + 1) * nb)
        after = slice((j + 1) * nb, (j + 2) * nb)
        q = (j * nb) // 128 * 128
        at = j * nb - q
        home = (at + nb) % 128
        windows = list(range((j + 1) * nb // 128, mat.shape[2] // 128))
        factor = doubled(*found)
        left = doubled(mat[0, :, q:q + 128], mat[1, :, q:q + 128])
        held = {}

        def solve(w):
            here = slice(128 * w, 128 * w + 128)
            put(head, home, w, mat[0, rows, here], mat[1, rows, here])
            held[w] = product(factor, head, w)
            put(tail, at, w, held[w][:, 0:128], held[w][:, 128:])

        def change(w):
            here = slice(128 * w, 128 * w + 128)
            less = product(left, tail, w)
            mat[0, :, here] = mat[0, :, here] - less[:, 0:128]
            mat[1, :, here] = mat[1, :, here] - less[:, 128:]
            mat[0, rows, here] = held[w][:, 0:128]
            mat[1, rows, here] = held[w][:, 128:]

        first = windows[0]
        solve(first)
        pivots = iter(())
        if (j + 1) * nb < n:
            here = slice(128 * first, 128 * first + 128)
            ahead = jnp.concatenate([left[after], left[n + (j + 1) * nb:n + (j + 2) * nb]], axis=0)
            less = product(ahead, tail, first)
            to = (j + 1) * nb % 128
            pivots = block_inverse(pick(mat[0, after, here] - less[:, 0:128]),
                                   pick(mat[1, after, here] - less[:, 128:]),
                                   to, (to + nb) % 128)
        tasks = [functools.partial(solve, w) for w in windows[1:]]
        tasks += [functools.partial(change, w) for w in windows]
        tasks.append(functools.partial(clear, head, home))
        tasks.append(functools.partial(clear, tail, at))
        steps = nb // 2
        done = 0
        for i, task in enumerate(tasks):
            task()
            upto = (i + 1) * steps // len(tasks)
            for _ in range(upto - done):
                found = next(pivots, None) or found
            done = upto
        for step in pivots:
            found = step or found
    x_ref[...] = mat[:, :, n:]


def split(x):
    high = x.astype(BF16)
    return high, (x - high.astype(F32)).astype(BF16)


def right_side(x):
    xr, xi = x[0], x[1]
    return jnp.concatenate(split(jnp.concatenate(
        [jnp.concatenate([xr, xi], axis=1), jnp.concatenate([-xi, xr], axis=1)], axis=0)), axis=1)


def pivot_rows(pivot_ref, box):
    pieces = range(pivot_ref.shape[0])
    return [jnp.concatenate([pivot_ref[c, box, p:p + 1, :] for c in pieces], axis=1)
            for p in range(2)]


def quarters(product):
    rows, cols = product.shape[0] // 2, product.shape[1] // 2
    return ((product[:rows, :cols] + product[:rows, cols:])
            + (product[rows:, :cols] + product[rows:, cols:]))


def form(left, rest, right, blocks, slot):
    blocks[slot] = rest - quarters(plain(left, right[...]))


def fold(blocks, slot, rows, pivots, out_ref, to):
    qr, qi = pivots
    width = qr.shape[1]
    mine = blocks[slot, rows, :]
    br, bi = mine[:, 0:width], mine[:, width:]
    wr = br * qr - bi * qi
    wi = br * qi + bi * qr
    upper = jnp.concatenate([jnp.concatenate([wr, -wi], axis=1),
                             jnp.concatenate([wi, wr], axis=1)], axis=0)
    update = quarters(lax.dot_general(
        jnp.concatenate(split(upper), axis=0), jnp.concatenate(split(blocks[slot]), axis=0),
        (((1,), (1,)), ((), ())), preferred_element_type=F32))
    half = update.shape[0] // 2
    out_ref[to, 0] = out_ref[to, 0] - update[0:half]
    out_ref[to, 1] = out_ref[to, 1] - update[half:]


def row_half(col_count, group, n):
    count = n // (col_count // group)
    me = lax.axis_index("col")
    return pl.ds(pl.multiple_of((me // group) * count, count), count)


def entry_squares(box_total, nb_ref, place_ref, points_ref, which, k, n, sources):
    box_count = points_ref.shape[1]
    place = slot_of(nb_ref, which, k, box_count, box_total)
    here = shifted(points_ref[place // box_count, place % box_count], place_ref[which, k])
    return dot_tn(target_rows(here[:, 0:n]), sources[...])


def evaluate(squares, n, width, left_at, rest_at):
    for i in range(0, n, ROWS):
        inner = slice(i, i + ROWS)
        under = slice(n + i, n + i + ROWS)
        for c in range(0, n + width, 128):
            values = kernel_values(squares[inner, c:c + 128], COS)
            for p, value in enumerate(values):
                if c < n:
                    here = slice(p * n + c, p * n + c + 128)
                    left_at[inner, here], left_at[under, here] = split(value)
                else:
                    start = p * width + c - n
                    rest_at[inner, start:start + 128] = value


def half_sources(points, side, group, n, width):
    whole = source_rows(centred(points))
    half = whole[:, n:n + width]
    for c in range(1, group):
        half = jnp.where(side == c, whole[:, n + c * width:n + (c + 1) * width], half)
    return jnp.concatenate([whole[:, 0:n], half], axis=1)


def kernel_kernel(box_total, group, nb_ref, place_ref, points_ref, left_ref, rest_ref, sources,
                  squares):
    entries, n, width = rest_ref.shape
    width //= 2
    me = lax.axis_index("col")
    fed = 1 - me // group
    sources[...] = half_sources(points_ref[1, fed], lax.rem(me, group), group, n, width)

    def measure(k, slot):
        squares[slot] = entry_squares(box_total, nb_ref, place_ref, points_ref, fed, k, n, sources)

    measure(0, 0)

    @pl.loop(0, entries // 2)
    def _(pair):
        for i in range(2):
            k = 2 * pair + i
            measure(jnp.minimum(k + 1, entries - 1), 1 - i)
            evaluate(squares.at[i], n, width, left_ref.at[k], rest_ref.at[k])


def near_kernel(box_total, col_count, group, nb_ref, place_ref, points_ref, x_ref, pivot_ref,
                out_ref, sources, squares, left, rest, right, blocks):
    n = x_ref.shape[1]
    width = x_ref.shape[2]
    box_count = points_ref.shape[1]
    entries = nb_ref.shape[1]
    me = lax.axis_index("col")
    box = me // group
    sources[...] = half_sources(points_ref[1, box], lax.rem(me, group), group, n, width)
    pivots = pivot_rows(pivot_ref, box)
    rows = row_half(col_count, group, n)

    def measure(k, slot):
        squares[slot] = entry_squares(box_total, nb_ref, place_ref, points_ref, box, k, n, sources)

    def finish(k, slot):
        fold(blocks, slot, rows, pivots, out_ref,
             slot_of(nb_ref, box, k, box_count, box_total))

    measure(0, 0)
    measure(1, 1)
    right[...] = right_side(x_ref)
    out_ref[...] = jnp.zeros_like(out_ref)
    evaluate(squares.at[0], n, width, left.at[0], rest.at[0])

    @pl.loop(0, entries // 2)
    def _(pair):
        for i in range(2):
            k = 2 * pair + i
            measure(jnp.minimum(k + 2, entries - 1), i)
            form(left[i], rest[i], right, blocks, i)
            evaluate(squares.at[1 - i], n, width, left.at[1 - i], rest.at[1 - i])
            finish(k, i)


def far_kernel(box_total, col_count, group, nb_ref, buf_ref, left_ref, rest_ref, x_ref,
               mine_ref, pivot_ref, out_ref, inter_ref, right, blocks):
    n = x_ref.shape[1]
    entries, _, _ = rest_ref.shape
    me = lax.axis_index("col")
    box = me // group
    fed = 1 - box
    box_count = pivot_ref.shape[1]
    right[...] = right_side(x_ref)
    pivots = pivot_rows(pivot_ref, fed)
    rows = row_half(col_count, group, n)
    form(left_ref[0], rest_ref[0], right, blocks, 0)
    out_ref[...] = buf_ref[...]
    for k in range(entries):
        if k + 1 < entries:
            form(left_ref[k + 1], rest_ref[k + 1], right, blocks, (k + 1) % 2)
        fold(blocks, k % 2, rows, pivots, out_ref,
             slot_of(nb_ref, fed, k, box_count, box_total))
    strip = inter_ref.shape[2]
    for p in range(2):
        for ref, where in ((mine_ref, box), (x_ref, fed)):
            block = jnp.transpose(ref[p])
            piece = block[0:strip]
            for c in range(1, block.shape[0] // strip):
                piece = jnp.where(box == c, block[c * strip:(c + 1) * strip], piece)
            inter_ref[where, p] = piece


def reduce_kernel(box_total, buf_ref, out_ref, pair_in, line_out, line_in, side_out, side_in,
                  held, sends, recvs):
    me = lax.axis_index("col")
    place = lax.axis_index("box")
    side = lax.rem(me, 2)
    odd = lax.rem(place, 2)
    near = {"col": me + 1 - 2 * side}
    relay = {"box": lax.rem(place + box_total + 4 * odd - 2, box_total)}
    source = {"box": lax.rem(place + box_total + 2 - 4 * odd, box_total)}
    twin = {"box": place + 1 - 2 * odd}
    meet([near, relay, source, twin])()
    box_count = out_ref.shape[0]
    order = (2 * odd, 2 - 2 * odd, 1)
    chunks = [(d, p) for d in range(box_count) for p in range(2)]
    pairs = {}
    for g, at in enumerate(order):
        for i, (d, p) in enumerate(chunks):
            pairs[g, i] = send(buf_ref.at[at * box_count + d, p, 1 - side], pair_in.at[g, d, p],
                               sends, recvs, len(chunks) * g + i, near)
    base = 3 * len(chunks)
    lines, sides = [], []
    for i, (d, p) in enumerate(chunks):
        pairs[0, i].wait()
        line_out[d, p] = buf_ref[order[0] * box_count + d, p, side] + pair_in[0, d, p]
        lines.append(send(line_out.at[d, p], line_in.at[d, p], sends, recvs, base + i, relay))
    for i, (d, p) in enumerate(chunks):
        pairs[1, i].wait()
        held[d, p] = buf_ref[order[1] * box_count + d, p, side] + pair_in[1, d, p]
    for i, (d, p) in enumerate(chunks):
        lines[i].wait()
        side_out[d, p] = held[d, p] + line_in[d, p]
        sides.append(send(side_out.at[d, p], side_in.at[d, p], sends, recvs,
                          base + len(chunks) + i, twin))
    for i, (d, p) in enumerate(chunks):
        pairs[2, i].wait()
        held[d, p] = buf_ref[box_count + d, p, side] + pair_in[2, d, p]
    for i, (d, p) in enumerate(chunks):
        sides[i].wait()
        out_ref[d, p] = held[d, p] + side_in[d, p]


def ring(count, step):
    return [(i, (i + step) % count) for i in range(count)]


def on_device(
    box_points, proxy_directions, point_order, neighbour_boxes, neighbour_places, pivot_inverse
):
    box_count, _, point_count = box_points.shape
    col_count = lax.axis_size("col")
    box_total = lax.axis_size("box")
    group = col_count // box_count
    listed = neighbour_boxes.shape[1]
    entries = listed // group
    width = pivot_inverse.shape[2]
    rest = width * col_count
    skeleton = point_count - rest
    half = rest // group
    share = proxy_directions.shape[1]
    dma = pltpu.SemaphoreType.DMA

    points, proxies, pivots = pl.pallas_call(
        functools.partial(exchange_kernel, box_total, col_count, group, skeleton),
        out_shape=(
            jax.ShapeDtypeStruct((3, box_count, 8, point_count), F32),
            jax.ShapeDtypeStruct((box_count,) + proxy_directions.shape, F32),
            jax.ShapeDtypeStruct((box_count,) + pivot_inverse.shape, F32),
        ),
        in_specs=[HBM] * 4,
        out_specs=(VMEM,) * 3,
        scratch_shapes=[pltpu.VMEM((3, box_count, point_count), F32),
                        pltpu.VMEM(point_order.shape, jnp.int32),
                        dma((4,)), dma((4,)), dma((4,))],
        compiler_params=params(collective_id=0, has_side_effects=True),
        cost_estimate=pl.CostEstimate(flops=4 * 10**9, bytes_accessed=16 * 10**6,
                                      transcendentals=0),
    )(*(pltpu.with_memory_space_constraint(one, pltpu.HBM) for one in (
        jnp.transpose(box_points, (1, 0, 2)), point_order, proxy_directions, pivot_inverse)))

    rows = box_count * share + entries * point_count
    cross = pl.pallas_call(
        functools.partial(tile_kernel, box_total, entries, group, skeleton),
        out_shape=jax.ShapeDtypeStruct((2, skeleton, point_count), F32),
        in_specs=[SMEM, SMEM, VMEM, VMEM],
        out_specs=VMEM,
        scratch_shapes=[
            pltpu.VMEM((DEPTH, rows), BF16),
            pltpu.VMEM((DEPTH, point_count), BF16),
            pltpu.VMEM((2, BLOCK, point_count), F32),
            pltpu.VMEM((2, 2 * BLOCK, 2 * point_count), BF16),
            pltpu.VMEM((skeleton, 2 * point_count), F32),
        ],
        compiler_params=params(),
    )(neighbour_boxes, neighbour_places, points, proxies)
    pairs = [(i, i + 1 - 2 * (i % 2)) for i in range(col_count)]
    cross_in = lax.ppermute(cross, "col", pairs)

    cover = pl.CostEstimate(flops=8 * 10**9, bytes_accessed=16 * 10**6, transcendentals=0)
    left, kept = pl.pallas_call(
        functools.partial(kernel_kernel, box_total, group),
        out_shape=(
            jax.ShapeDtypeStruct((listed, 2 * skeleton, 2 * skeleton), BF16),
            jax.ShapeDtypeStruct((listed, skeleton, 2 * half), F32),
        ),
        in_specs=[SMEM, SMEM, VMEM],
        out_specs=(VMEM, VMEM),
        scratch_shapes=[
            pltpu.VMEM((DEPTH, skeleton + half), BF16),
            pltpu.VMEM((2, skeleton, skeleton + half), F32),
        ],
        compiler_params=params(),
        cost_estimate=cover,
    )(neighbour_boxes, neighbour_places, points)

    solved = pl.pallas_call(
        functools.partial(solve_kernel, group),
        out_shape=jax.ShapeDtypeStruct((2, skeleton, half), F32),
        in_specs=[VMEM] * 2,
        out_specs=VMEM,
        scratch_shapes=[
            pltpu.VMEM((2, skeleton, skeleton + half), F32),
            pltpu.VMEM((2, 256, 2 * (skeleton + half)), BF16),
            pltpu.VMEM((2, 256, 2 * (skeleton + half)), BF16),
        ],
        compiler_params=params(),
    )(cross, cross_in)
    arrived = lax.ppermute(solved, "col", ring(col_count, group))

    strips = skeleton // box_count
    buffer = pl.pallas_call(
        functools.partial(near_kernel, box_total, col_count, group),
        out_shape=jax.ShapeDtypeStruct((3 * box_count, 2, strips, skeleton), F32),
        in_specs=[SMEM, SMEM, VMEM, VMEM, VMEM],
        out_specs=VMEM,
        scratch_shapes=[
            pltpu.VMEM((DEPTH, skeleton + half), BF16),
            pltpu.VMEM((2, skeleton, skeleton + half), F32),
            pltpu.VMEM((2, 2 * skeleton, 2 * skeleton), BF16),
            pltpu.VMEM((2, skeleton, 2 * half), F32),
            pltpu.VMEM((2 * skeleton, 4 * half), BF16),
            pltpu.VMEM((2, skeleton, 2 * half), F32),
        ],
        compiler_params=params(),
        cost_estimate=cover,
    )(neighbour_boxes, neighbour_places, points, solved, pivots)

    buffer, inter = pl.pallas_call(
        functools.partial(far_kernel, box_total, col_count, group),
        out_shape=(
            jax.ShapeDtypeStruct(buffer.shape, F32),
            jax.ShapeDtypeStruct((box_count, 2, width, skeleton), F32),
        ),
        in_specs=[SMEM] + [VMEM] * 6,
        out_specs=(VMEM, VMEM),
        scratch_shapes=[
            pltpu.VMEM((2 * skeleton, 4 * half), BF16),
            pltpu.VMEM((2, skeleton, 2 * half), F32),
        ],
        compiler_params=params(),
    )(neighbour_boxes, buffer, left, kept, arrived, solved, pivots)
    interpolation = jnp.swapaxes(inter, 2, 3)

    strip = skeleton // col_count
    block = (box_count, 2, strip, skeleton)
    jobs = 5 * 2 * box_count
    skeleton_update = pl.pallas_call(
        functools.partial(reduce_kernel, box_total),
        out_shape=jax.ShapeDtypeStruct(block, F32),
        in_specs=[VMEM],
        out_specs=VMEM,
        scratch_shapes=[
            pltpu.VMEM((3,) + block, F32),
            pltpu.VMEM(block, F32),
            pltpu.VMEM(block, F32),
            pltpu.VMEM(block, F32),
            pltpu.VMEM(block, F32),
            pltpu.VMEM(block, F32),
            dma((jobs,)),
            dma((jobs,)),
        ],
        compiler_params=params(collective_id=1, has_side_effects=True),
    )(buffer.reshape(3 * box_count, 2, group, strip, skeleton))
    return (interpolation, skeleton_update)


def solution(mesh):
    placed = (
        P("box", None, None),
        P(None, "col"),
        P("box", None),
        P("box", None),
        P("box", None),
        P("box", None, "col"),
    )
    return jax.shard_map(
        on_device,
        mesh=mesh,
        in_specs=placed,
        out_specs=(P("box", None, None, "col"), P("box", None, "col", None)),
        check_vma=False,
    )
```

```python
import functools
import math

import jax
import jax.numpy as jnp
from jax import lax
from jax.experimental import pallas as pl
from jax.experimental.pallas import tpu as pltpu
from jax.sharding import PartitionSpec as P

softening = 0.05
proxy_radius = 1.5
ridge_share = 0.05
NBLK = 32
BLOCK = 256
ROWS = 16
DEPTH = 64
PIECES = 2

SIN = (4.44287959, -7.30781805, 3.59778873, -0.79123822)
COS = (1.41420408, -6.97764206, 5.7152384, -1.72834866)

HBM = pl.BlockSpec(memory_space=pltpu.HBM)
VMEM = pl.BlockSpec(memory_space=pltpu.VMEM)
SMEM = pl.BlockSpec(memory_space=pltpu.SMEM)
MESH = pl.DeviceIdType.MESH
F32 = jnp.float32
BF16 = jnp.bfloat16


def params(**more):
    return pltpu.CompilerParams(vmem_limit_bytes=24 * 1024 * 1024, **more)


def horner(coefficients, z):
    total = coefficients[-1] * z + coefficients[-2]
    for one in coefficients[-3::-1]:
        total = total * z + one
    return total


def kernel_values(square):
    inverse = lax.rsqrt(square)
    turns = square * inverse
    part = turns - jnp.floor(turns + 0.5)
    z = part * part
    amplitude = inverse * (1.0 / (2.0 * math.pi))
    sine = part * horner(SIN, z)
    scaled = amplitude * sine
    return amplitude - scaled * sine, scaled * horner(COS, z)


def three(x):
    high = x.astype(BF16).astype(F32)
    rest = x - high
    mid = rest.astype(BF16).astype(F32)
    return high, mid, rest - mid


def row_three(block, row):
    third = lax.broadcasted_iota(jnp.int32, block.shape, 0) == 3
    return jnp.where(third, row, block)


def norm_of(points):
    return jnp.sum(points * points, axis=0, keepdims=True)


def stacked(groups):
    zero = jnp.zeros_like(groups[0])
    return jnp.concatenate(groups + [zero] * (DEPTH // 8 - len(groups)), axis=0).astype(BF16)


def target_rows(points):
    high, mid, low = three(points)
    n_high, n_mid, n_low = three(norm_of(points))
    return stacked([row_three(high, n_high), row_three(high, n_mid), row_three(mid, n_low),
                    row_three(high, 1.0), row_three(mid, 1.0), row_three(low, 1.0)])


def source_rows(points):
    high, mid, low = three(points)
    norm = norm_of(points) + 4.0 * softening * softening
    n_high, n_mid, n_low = three(norm)
    return stacked([row_three(-2.0 * high, 1.0), row_three(-2.0 * mid, 1.0),
                    row_three(-2.0 * high, 1.0), row_three(-2.0 * low, n_high),
                    row_three(-2.0 * mid, n_mid), row_three(-2.0 * high, n_low)])


def three_rows(points):
    rows = lax.broadcasted_iota(jnp.int32, points.shape, 0)
    return jnp.where(rows < 3, points, 0.0)


def shifted(points, code):
    code = jnp.where(code >= 13, code + 1, code)
    axis_row = lax.broadcasted_iota(jnp.int32, points.shape, 0)
    move = jnp.where(
        axis_row == 0,
        (code // 9 - 1).astype(F32),
        jnp.where(axis_row == 1, ((code // 3) % 3 - 1).astype(F32), (code % 3 - 1).astype(F32)),
    )
    return three_rows(2.0 * (points + (move - 0.5)))


def centred(points):
    return three_rows(2.0 * (points - 0.5))


def slot_of(nb_ref, row, entry, box_count, box_total):
    owner_box = nb_ref[row, entry]
    step = owner_box // box_count - lax.axis_index("box") + 1
    step = jnp.where(step < 0, step + box_total, step)
    step = jnp.where(step >= box_total, step - box_total, step)
    return step * box_count + owner_box % box_count


def dot_tn(a, b):
    return lax.dot_general(a, b, (((0,), (0,)), ((), ())), preferred_element_type=F32)


def meet(peers):
    barrier = pltpu.get_barrier_semaphore()
    for peer in peers:
        pl.semaphore_signal(barrier, inc=1, device_id=peer, device_id_type=MESH)
    return lambda: pl.semaphore_wait(barrier, len(peers))


def send(source, target, sends, recvs, index, peer):
    one = pltpu.make_async_remote_copy(
        src_ref=source, dst_ref=target, send_sem=sends.at[index], recv_sem=recvs.at[index],
        device_id=peer, device_id_type=MESH)
    one.start()
    return one


def exchange_kernel(box_total, col_count, group, skeleton, points_ref, order_ref, proxy_ref,
                    pivot_ref, points_out, proxy_out, pivot_out, points, order, sends, recvs,
                    local):
    me = lax.axis_index("col")
    place = lax.axis_index("box")
    _, box_count, count = points_ref.shape
    after = {"box": lax.rem(place + 1, box_total)}
    before = {"box": lax.rem(place + box_total - 1, box_total)}
    across = {"col": lax.rem(me + group, col_count)}
    mine = me // group
    own = ((points_ref, points), (order_ref, order), (proxy_ref, proxy_out.at[0]),
           (pivot_ref, pivot_out.at[mine]))
    loads = []
    for i, (source, target) in enumerate(own):
        copy = pltpu.make_async_copy(source, target, local.at[i])
        copy.start()
        loads.append(copy)
    arrived = meet([before, after, across])
    for copy in loads:
        copy.wait()
    width = (count - skeleton) // col_count
    for box in range(box_count):
        row = order[box:box + 1, :]
        strips = [row[:, skeleton + s * width:skeleton + (s + 1) * width]
                  for c in range(group) for s in range(c, col_count, group)]
        row = jnp.concatenate([row[:, 0:skeleton]] + strips, axis=1)
        one_hot = (lax.broadcasted_iota(jnp.int32, (count, count), 0) == row).astype(F32)
        whole = jnp.concatenate([points[axis, box:box + 1, :] for axis in range(3)]
                                + [jnp.zeros((5, count), F32)], axis=0)
        rows = jnp.concatenate(list(three(whole)) + [jnp.zeros_like(whole)], axis=0)
        picked = jnp.dot(rows.astype(BF16), one_hot.astype(BF16), preferred_element_type=F32)
        points_out[1, box] = (picked[0:8] + picked[8:16]) + picked[16:24]
    arrived()
    jobs = [
        send(points_out.at[1], points_out.at[0], sends, recvs, 0, after),
        send(points_out.at[1], points_out.at[2], sends, recvs, 1, before),
        send(proxy_ref, proxy_out.at[1], sends, recvs, 2, across),
        send(pivot_ref, pivot_out.at[mine], sends, recvs, 3, across),
    ]
    for copy in jobs:
        copy.wait()


def tile_kernel(box_total, entries, group, skeleton, nb_ref, place_ref, points_ref, proxy_ref,
                cross_ref, targets, sources, squares, tiles, total):
    count = points_ref.shape[3]
    box_count, _, share = proxy_ref.shape
    proxies = box_count * share
    me = lax.axis_index("col")
    box = me // group
    first = lax.rem(me, group) * entries
    sources[...] = source_rows(centred(points_ref[1, box]))
    for d in range(box_count):
        directions = jnp.concatenate([proxy_ref[d], jnp.zeros((5, share), F32)], axis=0)
        targets[:, d * share:(d + 1) * share] = target_rows((2.0 * proxy_radius) * directions)
    for k in range(entries):
        slot = slot_of(nb_ref, box, first + k, box_count, box_total)
        here = shifted(points_ref[slot // box_count, slot % box_count], place_ref[box, first + k])
        targets[:, proxies + k * count:proxies + (k + 1) * count] = target_rows(here)
    block = tiles.shape[1] // 2

    def measure(base, slot):
        squares[slot] = dot_tn(targets[:, pl.ds(pl.multiple_of(base, block), block)],
                               sources[...])

    def evaluate(slot, i):
        inner = slice(i * ROWS, (i + 1) * ROWS)
        lower = slice(block + i * ROWS, block + (i + 1) * ROWS)
        for c in range(0, count, 256):
            here = slice(c, c + 256)
            there = slice(count + c, count + c + 256)
            real, imag = kernel_values(squares[slot, inner, here])
            real = real.astype(BF16)
            imag = imag.astype(BF16)
            tiles[slot, inner, here] = real
            tiles[slot, inner, there] = imag
            tiles[slot, lower, here] = imag
            tiles[slot, lower, there] = -real

    def gather(slot, left, c):
        here = slice(c, c + 256)
        total[:, here] += plain(left, tiles[slot, :, here])

    def stage(ahead, now, before):
        measure(*ahead)
        steps = block // ROWS
        pieces = 2 * count // 256
        left = None if before is None else jnp.transpose(tiles[before, :, 0:skeleton])
        for i in range(steps):
            if left is not None and i % (steps // pieces) == 0:
                gather(before, left, i // (steps // pieces) * 256)
            evaluate(now, i)

    total[...] = jnp.zeros_like(total)
    blocks = proxies // block
    measure(0, 0)
    for i in range(blocks):
        stage(((i + 1) * block, (i + 1) % 2), i % 2, (i + 1) % 2 if i else None)
    per = count // block
    last = proxies + (entries * per - 1) * block

    @pl.loop(0, entries)
    def _(k):
        base = proxies + k * count
        for i in range(per):
            now = (blocks + i) % 2
            stage((jnp.minimum(base + (i + 1) * block, last), 1 - now), now, 1 - now)

    end = (blocks + per - 1) % 2
    left = jnp.transpose(tiles[end, :, 0:skeleton])
    for c in range(0, 2 * count, 256):
        gather(end, left, c)
    for p in range(2):
        cross_ref[p] = total[:, p * count:(p + 1) * count]


def lanes(block, k):
    return jnp.take_along_axis(block, jnp.full(block.shape, k, jnp.int32), axis=1)


def across_rows(block, k):
    return jnp.broadcast_to(block[k:k + 1, :], block.shape)


def block_inverse(re, im, start, home):
    count = len(re)
    shape = re[0].shape
    lane = lax.broadcasted_iota(jnp.int32, shape, 1)
    sub = lax.broadcasted_iota(jnp.int32, shape, 0)
    inside = (lane >= start) & (lane < start + 8 * count)
    re = [jnp.where(inside, block, jnp.where(lane - home == sub + 8 * v, 1.0, 0.0))
          for v, block in enumerate(re)]
    im = [jnp.where(inside, block, 0.0) for block in im]
    for r in range(count):
        order = [r] + [v for v in range(count) if v > r] + list(range(r))
        spread = {}
        for v in order:
            for j in range(8):
                k = start + 8 * r + j
                spread[v, j] = (lanes(re[v], k), lanes(im[v], k))
        cols = {j: spread[r, j] for j in range(8)}
        cols["row"] = (re[r], im[r])
        for t in range(0, 8, 2):
            (ar, ai), (cr, ci) = cols.pop(t), cols.pop(t + 1)
            a, d = across_rows(ar, t), across_rows(cr, t + 1)
            br, bi = across_rows(cr, t), across_rows(ci, t)
            scale = 1.0 / (a * d - (br * br + bi * bi))
            a, d, br, bi = a * scale, d * scale, br * scale, bi * scale
            at, on = sub == t, sub == t + 1
            here = at | on
            e0r = jnp.where(at, -d, jnp.where(on, br, ar * d - (cr * br + ci * bi)))
            e0i = jnp.where(at, 0.0, jnp.where(on, -bi, ai * d - (ci * br - cr * bi)))
            e1r = jnp.where(at, br, jnp.where(on, -a, cr * a - (ar * br - ai * bi)))
            e1i = jnp.where(at, bi, jnp.where(on, 0.0, ci * a - (ar * bi + ai * br)))
            for key, (xr, xi) in cols.items():
                x0r, x0i = across_rows(xr, t), across_rows(xi, t)
                x1r, x1i = across_rows(xr, t + 1), across_rows(xi, t + 1)
                lessr = (e0r * x0r - e0i * x0i) + (e1r * x1r - e1i * x1i)
                lessi = (e0r * x0i + e0i * x0r) + (e1r * x1i + e1i * x1r)
                cols[key] = (jnp.where(here, 0.0, xr) - lessr, jnp.where(here, 0.0, xi) - lessi)
            if t < 6:
                yield None
        re[r], im[r] = cols["row"]
        rows = [(across_rows(re[r], j), across_rows(im[r], j)) for j in range(8)]
        for v in order[1:]:
            lessr = [spread[v, j][0] * rows[j][0] - spread[v, j][1] * rows[j][1]
                     for j in range(8)]
            lessi = [spread[v, j][0] * rows[j][1] + spread[v, j][1] * rows[j][0]
                     for j in range(8)]
            re[v] = re[v] - summed(lessr)
            im[v] = im[v] - summed(lessi)
        yield jnp.concatenate(re, axis=0), jnp.concatenate(im, axis=0)


def summed(terms):
    while len(terms) > 1:
        terms = [terms[i] + terms[i + 1] for i in range(0, len(terms), 2)]
    return terms[0]


def plain(a, b):
    return jnp.dot(a, b, preferred_element_type=F32)


def solve_kernel(group, cross_ref, cross_in, x_ref, mat, head, tail):
    n = x_ref.shape[1]
    width = x_ref.shape[2]
    nb = NBLK
    side = lax.rem(lax.axis_index("col"), group)
    diagonal = lax.broadcasted_iota(jnp.int32, (128, 128), 0) == lax.broadcasted_iota(
        jnp.int32, (128, 128), 1
    )
    gram = cross_ref[:, :, 0:n] + cross_in[:, :, 0:n]
    ridge = 0.0
    for c in range(0, n, 128):
        ridge = ridge + jnp.where(diagonal, gram[0, c:c + 128, c:c + 128], 0.0)
    ridge = ridge_share * jnp.sum(ridge) / n
    mat[:, :, 0:n] = gram
    for c in range(0, n, 128):
        here = slice(c, c + 128)
        mat[0, here, here] = gram[0, here, here] + jnp.where(diagonal, ridge, 0.0)
    mine = pl.ds(pl.multiple_of(n + side * width, 128), width)
    mat[:, :, n:] = cross_ref[:, :, mine] + cross_in[:, :, mine]
    head[...] = jnp.zeros_like(head)
    tail[...] = jnp.zeros_like(tail)

    def pick(block):
        return [block[8 * v:8 * v + 8] for v in range(nb // 8)]

    def put(ref, at, w, re, im):
        where = slice(256 * w, 256 * w + 256)
        for base, block in ((at, [re, im]), (128 + at, [-im, re])):
            high, rest = split(jnp.concatenate(block, axis=1))
            ref[0, base:base + nb, where] = high
            ref[1, base:base + nb, where] = rest

    def clear(ref, at):
        for base in (at, 128 + at):
            ref[:, base:base + nb, :] = jnp.zeros((2, nb, ref.shape[2]), BF16)

    def doubled(re, im):
        return jnp.concatenate(split(jnp.concatenate([re, im], axis=1)), axis=0)

    def product(left, ref, w):
        where = slice(256 * w, 256 * w + 256)
        half = left.shape[0] // 2
        both = plain(left, ref[0, :, where])
        return both[0:half] + (both[half:] + plain(left[0:half], ref[1, :, where]))

    for step in block_inverse(pick(mat[0, 0:nb, 0:128]), pick(mat[1, 0:nb, 0:128]), 0, nb):
        found = step or None
    for j in range(n // nb):
        rows = slice(j * nb, (j + 1) * nb)
        after = slice((j + 1) * nb, (j + 2) * nb)
        q = (j * nb) // 128 * 128
        at = j * nb - q
        home = (at + nb) % 128
        windows = list(range((j + 1) * nb // 128, mat.shape[2] // 128))
        factor = doubled(*found)
        left = doubled(mat[0, :, q:q + 128], mat[1, :, q:q + 128])
        held = {}

        def solve(w):
            here = slice(128 * w, 128 * w + 128)
            put(head, home, w, mat[0, rows, here], mat[1, rows, here])
            held[w] = product(factor, head, w)
            put(tail, at, w, held[w][:, 0:128], held[w][:, 128:])

        def change(w):
            here = slice(128 * w, 128 * w + 128)
            less = product(left, tail, w)
            mat[0, :, here] = mat[0, :, here] - less[:, 0:128]
            mat[1, :, here] = mat[1, :, here] - less[:, 128:]
            mat[0, rows, here] = held[w][:, 0:128]
            mat[1, rows, here] = held[w][:, 128:]

        first = windows[0]
        solve(first)
        pivots = iter(())
        if (j + 1) * nb < n:
            here = slice(128 * first, 128 * first + 128)
            ahead = jnp.concatenate([left[after], left[n + (j + 1) * nb:n + (j + 2) * nb]], axis=0)
            less = product(ahead, tail, first)
            to = (j + 1) * nb % 128
            pivots = block_inverse(pick(mat[0, after, here] - less[:, 0:128]),
                                   pick(mat[1, after, here] - less[:, 128:]),
                                   to, (to + nb) % 128)
        tasks = [functools.partial(solve, w) for w in windows[1:]]
        tasks += [functools.partial(change, w) for w in windows]
        tasks.append(functools.partial(clear, head, home))
        tasks.append(functools.partial(clear, tail, at))
        steps = nb // 2
        done = 0
        for i, task in enumerate(tasks):
            task()
            upto = (i + 1) * steps // len(tasks)
            for _ in range(upto - done):
                found = next(pivots, None) or found
            done = upto
        for step in pivots:
            found = step or found
    x_ref[...] = mat[:, :, n:]


def split(x):
    high = x.astype(BF16)
    return high, (x - high.astype(F32)).astype(BF16)


def right_side(x):
    xr, xi = x[0], x[1]
    return jnp.concatenate(split(jnp.concatenate(
        [jnp.concatenate([xr, xi], axis=1), jnp.concatenate([-xi, xr], axis=1)], axis=0)), axis=1)


def pivot_rows(pivot_ref, box):
    pieces = range(pivot_ref.shape[0])
    return [jnp.concatenate([pivot_ref[c, box, p:p + 1, :] for c in pieces], axis=1)
            for p in range(2)]


def quarters(product):
    rows, cols = product.shape[0] // 2, product.shape[1] // 2
    return ((product[:rows, :cols] + product[:rows, cols:])
            + (product[rows:, :cols] + product[rows:, cols:]))


def form(left, rest, right, blocks, slot):
    blocks[slot] = rest - quarters(plain(left, right[...]))


def fold(blocks, slot, rows, pivots, out_ref, to):
    qr, qi = pivots
    width = qr.shape[1]
    mine = blocks[slot, rows, :]
    br, bi = mine[:, 0:width], mine[:, width:]
    wr = br * qr - bi * qi
    wi = br * qi + bi * qr
    upper = jnp.concatenate([jnp.concatenate([wr, -wi], axis=1),
                             jnp.concatenate([wi, wr], axis=1)], axis=0)
    update = quarters(lax.dot_general(
        jnp.concatenate(split(upper), axis=0), jnp.concatenate(split(blocks[slot]), axis=0),
        (((1,), (1,)), ((), ())), preferred_element_type=F32))
    half = update.shape[0] // 2
    out_ref[to, 0] = out_ref[to, 0] - update[0:half]
    out_ref[to, 1] = out_ref[to, 1] - update[half:]


def row_half(col_count, group, n):
    count = n // (col_count // group)
    me = lax.axis_index("col")
    return pl.ds(pl.multiple_of((me // group) * count, count), count)


def entry_squares(box_total, nb_ref, place_ref, points_ref, which, k, n, sources):
    box_count = points_ref.shape[1]
    place = slot_of(nb_ref, which, k, box_count, box_total)
    here = shifted(points_ref[place // box_count, place % box_count], place_ref[which, k])
    return dot_tn(target_rows(here[:, 0:n]), sources[...])


def evaluate(squares, n, width, left_at, rest_at, part=0, parts=1):
    for i in range(part * n // parts, (part + 1) * n // parts, ROWS):
        inner = slice(i, i + ROWS)
        under = slice(n + i, n + i + ROWS)
        for c in range(0, n + width, 128):
            values = kernel_values(squares[inner, c:c + 128])
            for p, value in enumerate(values):
                if c < n:
                    here = slice(p * n + c, p * n + c + 128)
                    left_at[inner, here], left_at[under, here] = split(value)
                else:
                    start = p * width + c - n
                    rest_at[inner, start:start + 128] = value


def half_sources(points, side, group, n, width):
    whole = source_rows(centred(points))
    half = whole[:, n:n + width]
    for c in range(1, group):
        half = jnp.where(side == c, whole[:, n + c * width:n + (c + 1) * width], half)
    return jnp.concatenate([whole[:, 0:n], half], axis=1)


def kernel_kernel(box_total, group, nb_ref, place_ref, points_ref, left_ref, rest_ref, sources,
                  squares):
    entries, n, width = rest_ref.shape
    width //= 2
    me = lax.axis_index("col")
    fed = 1 - me // group
    sources[...] = half_sources(points_ref[1, fed], lax.rem(me, group), group, n, width)

    def measure(k, slot):
        squares[slot] = entry_squares(box_total, nb_ref, place_ref, points_ref, fed, k, n, sources)

    measure(0, 0)

    @pl.loop(0, entries // 2)
    def _(pair):
        for i in range(2):
            k = 2 * pair + i
            measure(jnp.minimum(k + 1, entries - 1), 1 - i)
            evaluate(squares.at[i], n, width, left_ref.at[k], rest_ref.at[k])


def near_kernel(box_total, col_count, group, nb_ref, place_ref, points_ref, x_ref, pivot_ref,
                out_ref, sources, squares, left, rest, right, blocks):
    n = x_ref.shape[1]
    width = x_ref.shape[2]
    box_count = points_ref.shape[1]
    entries = nb_ref.shape[1]
    me = lax.axis_index("col")
    box = me // group
    sources[...] = half_sources(points_ref[1, box], lax.rem(me, group), group, n, width)
    pivots = pivot_rows(pivot_ref, box)
    rows = row_half(col_count, group, n)

    def measure(k, slot):
        squares[slot] = entry_squares(box_total, nb_ref, place_ref, points_ref, box, k, n, sources)

    def finish(k, slot):
        fold(blocks, slot, rows, pivots, out_ref,
             slot_of(nb_ref, box, k, box_count, box_total))

    def values(k, part):
        if k < entries:
            evaluate(squares.at[k % 3], n, width, left.at[k % 2], rest.at[k % 2], part, 2)

    measure(0, 0)
    measure(1, 1)
    right[...] = right_side(x_ref)
    out_ref[...] = jnp.zeros_like(out_ref)
    for part in range(2):
        values(0, part)
    for k in range(entries + 1):
        if k + 2 < entries:
            measure(k + 2, (k + 2) % 3)
        if k < entries:
            form(left[k % 2], rest[k % 2], right, blocks, k)
        values(k + 1, 0)
        if k:
            finish(k - 1, k - 1)
        values(k + 1, 1)


def far_kernel(box_total, col_count, group, nb_ref, buf_ref, left_ref, rest_ref, x_ref,
               mine_ref, pivot_ref, out_ref, inter_ref, right, blocks):
    n = x_ref.shape[1]
    entries, _, _ = rest_ref.shape
    me = lax.axis_index("col")
    box = me // group
    fed = 1 - box
    box_count = pivot_ref.shape[1]
    right[...] = right_side(x_ref)
    pivots = pivot_rows(pivot_ref, fed)
    rows = row_half(col_count, group, n)
    out_ref[...] = buf_ref[...]
    for k in range(entries + 2):
        if k < entries:
            form(left_ref[k], rest_ref[k], right, blocks, k)
        if k > 1:
            fold(blocks, k - 2, rows, pivots, out_ref,
                 slot_of(nb_ref, fed, k - 2, box_count, box_total))
    strip = inter_ref.shape[2]
    for p in range(2):
        for ref, where in ((mine_ref, box), (x_ref, fed)):
            block = jnp.transpose(ref[p])
            piece = block[0:strip]
            for c in range(1, block.shape[0] // strip):
                piece = jnp.where(box == c, block[c * strip:(c + 1) * strip], piece)
            inter_ref[where, p] = piece


def reduce_kernel(box_total, buf_ref, out_ref, pair_in, line_out, line_in, side_out, side_in,
                  held, sends, recvs):
    me = lax.axis_index("col")
    place = lax.axis_index("box")
    side = lax.rem(me, 2)
    odd = lax.rem(place, 2)
    near = {"col": me + 1 - 2 * side}
    relay = {"box": lax.rem(place + box_total + 4 * odd - 2, box_total)}
    source = {"box": lax.rem(place + box_total + 2 - 4 * odd, box_total)}
    twin = {"box": place + 1 - 2 * odd}
    meet([near, relay, source, twin])()
    box_count, _, strip, _ = out_ref.shape
    order = (2 * odd, 2 - 2 * odd, 1)
    piece = strip // PIECES
    chunks = [(d, p, pl.ds(i * piece, piece)) for d in range(box_count) for p in range(2)
              for i in range(PIECES)]
    wholes = [(d, p) for d in range(box_count) for p in range(2)]
    pairs = {}
    base = 0
    for g, parts in enumerate((chunks, wholes, wholes)):
        for i, part in enumerate(parts):
            d, p = part[:2]
            source_at = (order[g] * box_count + d, p, 1 - side) + part[2:]
            pairs[g, i] = send(buf_ref.at[source_at], pair_in.at[(g,) + part], sends, recvs,
                               base + i, near)
        base += len(parts)
    lines, sides = [], []
    for i, (d, p, some) in enumerate(chunks):
        pairs[0, i].wait()
        line_out[d, p, some] = (buf_ref[order[0] * box_count + d, p, side, some]
                                + pair_in[0, d, p, some])
        lines.append(send(line_out.at[d, p, some], line_in.at[d, p, some], sends, recvs,
                          base + i, relay))
    base += len(chunks)
    for i, (d, p) in enumerate(wholes):
        pairs[1, i].wait()
        held[d, p] = buf_ref[order[1] * box_count + d, p, side] + pair_in[1, d, p]
    for i, (d, p, some) in enumerate(chunks):
        lines[i].wait()
        side_out[d, p, some] = held[d, p, some] + line_in[d, p, some]
        sides.append(send(side_out.at[d, p, some], side_in.at[d, p, some], sends, recvs,
                          base + i, twin))
    for i, (d, p) in enumerate(wholes):
        pairs[2, i].wait()
        held[d, p] = buf_ref[box_count + d, p, side] + pair_in[2, d, p]
    for i, (d, p, some) in enumerate(chunks):
        sides[i].wait()
        out_ref[d, p, some] = held[d, p, some] + side_in[d, p, some]


def ring(count, step):
    return [(i, (i + step) % count) for i in range(count)]


def on_device(
    box_points, proxy_directions, point_order, neighbour_boxes, neighbour_places, pivot_inverse
):
    box_count, _, point_count = box_points.shape
    col_count = lax.axis_size("col")
    box_total = lax.axis_size("box")
    group = col_count // box_count
    listed = neighbour_boxes.shape[1]
    entries = listed // group
    width = pivot_inverse.shape[2]
    rest = width * col_count
    skeleton = point_count - rest
    half = rest // group
    share = proxy_directions.shape[1]
    dma = pltpu.SemaphoreType.DMA

    points, proxies, pivots = pl.pallas_call(
        functools.partial(exchange_kernel, box_total, col_count, group, skeleton),
        out_shape=(
            jax.ShapeDtypeStruct((3, box_count, 8, point_count), F32),
            jax.ShapeDtypeStruct((box_count,) + proxy_directions.shape, F32),
            jax.ShapeDtypeStruct((box_count,) + pivot_inverse.shape, F32),
        ),
        in_specs=[HBM] * 4,
        out_specs=(VMEM,) * 3,
        scratch_shapes=[pltpu.VMEM((3, box_count, point_count), F32),
                        pltpu.VMEM(point_order.shape, jnp.int32),
                        dma((4,)), dma((4,)), dma((4,))],
        compiler_params=params(collective_id=0, has_side_effects=True),
        cost_estimate=pl.CostEstimate(flops=4 * 10**9, bytes_accessed=16 * 10**6,
                                      transcendentals=0),
    )(*(pltpu.with_memory_space_constraint(one, pltpu.HBM) for one in (
        jnp.transpose(box_points, (1, 0, 2)), point_order, proxy_directions, pivot_inverse)))

    rows = box_count * share + entries * point_count
    cross = pl.pallas_call(
        functools.partial(tile_kernel, box_total, entries, group, skeleton),
        out_shape=jax.ShapeDtypeStruct((2, skeleton, point_count), F32),
        in_specs=[SMEM, SMEM, VMEM, VMEM],
        out_specs=VMEM,
        scratch_shapes=[
            pltpu.VMEM((DEPTH, rows), BF16),
            pltpu.VMEM((DEPTH, point_count), BF16),
            pltpu.VMEM((2, BLOCK, point_count), F32),
            pltpu.VMEM((2, 2 * BLOCK, 2 * point_count), BF16),
            pltpu.VMEM((skeleton, 2 * point_count), F32),
        ],
        compiler_params=params(),
    )(neighbour_boxes, neighbour_places, points, proxies)
    pairs = [(i, i + 1 - 2 * (i % 2)) for i in range(col_count)]
    cross_in = lax.ppermute(cross, "col", pairs)

    cover = pl.CostEstimate(flops=8 * 10**9, bytes_accessed=16 * 10**6, transcendentals=0)
    left, kept = pl.pallas_call(
        functools.partial(kernel_kernel, box_total, group),
        out_shape=(
            jax.ShapeDtypeStruct((listed, 2 * skeleton, 2 * skeleton), BF16),
            jax.ShapeDtypeStruct((listed, skeleton, 2 * half), F32),
        ),
        in_specs=[SMEM, SMEM, VMEM],
        out_specs=(VMEM, VMEM),
        scratch_shapes=[
            pltpu.VMEM((DEPTH, skeleton + half), BF16),
            pltpu.VMEM((2, skeleton, skeleton + half), F32),
        ],
        compiler_params=params(),
        cost_estimate=cover,
    )(neighbour_boxes, neighbour_places, points)

    solved = pl.pallas_call(
        functools.partial(solve_kernel, group),
        out_shape=jax.ShapeDtypeStruct((2, skeleton, half), F32),
        in_specs=[VMEM] * 2,
        out_specs=VMEM,
        scratch_shapes=[
            pltpu.VMEM((2, skeleton, skeleton + half), F32),
            pltpu.VMEM((2, 256, 2 * (skeleton + half)), BF16),
            pltpu.VMEM((2, 256, 2 * (skeleton + half)), BF16),
        ],
        compiler_params=params(),
    )(cross, cross_in)
    arrived = lax.ppermute(solved, "col", ring(col_count, group))

    strips = skeleton // box_count
    buffer = pl.pallas_call(
        functools.partial(near_kernel, box_total, col_count, group),
        out_shape=jax.ShapeDtypeStruct((3 * box_count, 2, strips, skeleton), F32),
        in_specs=[SMEM, SMEM, VMEM, VMEM, VMEM],
        out_specs=VMEM,
        scratch_shapes=[
            pltpu.VMEM((DEPTH, skeleton + half), BF16),
            pltpu.VMEM((3, skeleton, skeleton + half), F32),
            pltpu.VMEM((2, 2 * skeleton, 2 * skeleton), BF16),
            pltpu.VMEM((2, skeleton, 2 * half), F32),
            pltpu.VMEM((2 * skeleton, 4 * half), BF16),
            pltpu.VMEM((listed, skeleton, 2 * half), F32),
        ],
        compiler_params=params(),
        cost_estimate=cover,
    )(neighbour_boxes, neighbour_places, points, solved, pivots)

    buffer, inter = pl.pallas_call(
        functools.partial(far_kernel, box_total, col_count, group),
        out_shape=(
            jax.ShapeDtypeStruct(buffer.shape, F32),
            jax.ShapeDtypeStruct((box_count, 2, width, skeleton), F32),
        ),
        in_specs=[SMEM] + [VMEM] * 6,
        out_specs=(VMEM, VMEM),
        scratch_shapes=[
            pltpu.VMEM((2 * skeleton, 4 * half), BF16),
            pltpu.VMEM((listed, skeleton, 2 * half), F32),
        ],
        compiler_params=params(),
    )(neighbour_boxes, buffer, left, kept, arrived, solved, pivots)
    interpolation = jnp.swapaxes(inter, 2, 3)

    strip = skeleton // col_count
    block = (box_count, 2, strip, skeleton)
    jobs = (2 + 3 * PIECES) * 2 * box_count
    skeleton_update = pl.pallas_call(
        functools.partial(reduce_kernel, box_total),
        out_shape=jax.ShapeDtypeStruct(block, F32),
        in_specs=[VMEM],
        out_specs=VMEM,
        scratch_shapes=[
            pltpu.VMEM((3,) + block, F32),
            pltpu.VMEM(block, F32),
            pltpu.VMEM(block, F32),
            pltpu.VMEM(block, F32),
            pltpu.VMEM(block, F32),
            pltpu.VMEM(block, F32),
            dma((jobs,)),
            dma((jobs,)),
        ],
        compiler_params=params(collective_id=1, has_side_effects=True),
    )(buffer.reshape(3 * box_count, 2, group, strip, skeleton))
    return (interpolation, skeleton_update)


def solution(mesh):
    placed = (
        P("box", None, None),
        P(None, "col"),
        P("box", None),
        P("box", None),
        P("box", None),
        P("box", None, "col"),
    )
    return jax.shard_map(
        on_device,
        mesh=mesh,
        in_specs=placed,
        out_specs=(P("box", None, None, "col"), P("box", None, "col", None)),
        check_vma=False,
    )
```

```python
import functools
import math

import jax
import jax.numpy as jnp
from jax import lax
from jax.experimental import pallas as pl
from jax.experimental.pallas import tpu as pltpu
from jax.sharding import PartitionSpec as P

softening = 0.05
proxy_radius = 1.5
ridge_share = 0.05
NBLK = 32
BLOCK = 256
ROWS = 16
DEPTH = 64
PIECES = 2

SIN = (4.44287959, -7.30781805, 3.59778873, -0.79123822)
COS = (1.41420408, -6.97764206, 5.7152384, -1.72834866)

HBM = pl.BlockSpec(memory_space=pltpu.HBM)
VMEM = pl.BlockSpec(memory_space=pltpu.VMEM)
SMEM = pl.BlockSpec(memory_space=pltpu.SMEM)
MESH = pl.DeviceIdType.MESH
F32 = jnp.float32
BF16 = jnp.bfloat16


def params(**more):
    return pltpu.CompilerParams(vmem_limit_bytes=24 * 1024 * 1024, **more)


def horner(coefficients, z):
    total = coefficients[-1] * z + coefficients[-2]
    for one in coefficients[-3::-1]:
        total = total * z + one
    return total


def kernel_values(square):
    inverse = lax.rsqrt(square)
    turns = square * inverse
    part = turns - jnp.floor(turns + 0.5)
    z = part * part
    amplitude = inverse * (1.0 / (2.0 * math.pi))
    sine = part * horner(SIN, z)
    scaled = amplitude * sine
    return amplitude - scaled * sine, scaled * horner(COS, z)


def three(x):
    high = x.astype(BF16).astype(F32)
    rest = x - high
    mid = rest.astype(BF16).astype(F32)
    return high, mid, rest - mid


def row_three(block, row):
    third = lax.broadcasted_iota(jnp.int32, block.shape, 0) == 3
    return jnp.where(third, row, block)


def norm_of(points):
    return jnp.sum(points * points, axis=0, keepdims=True)


def stacked(groups):
    zero = jnp.zeros_like(groups[0])
    return jnp.concatenate(groups + [zero] * (DEPTH // 8 - len(groups)), axis=0).astype(BF16)


def target_rows(points):
    high, mid, low = three(points)
    n_high, n_mid, n_low = three(norm_of(points))
    return stacked([row_three(high, n_high), row_three(high, n_mid), row_three(mid, n_low),
                    row_three(high, 1.0), row_three(mid, 1.0), row_three(low, 1.0)])


def source_rows(points):
    high, mid, low = three(points)
    norm = norm_of(points) + 4.0 * softening * softening
    n_high, n_mid, n_low = three(norm)
    return stacked([row_three(-2.0 * high, 1.0), row_three(-2.0 * mid, 1.0),
                    row_three(-2.0 * high, 1.0), row_three(-2.0 * low, n_high),
                    row_three(-2.0 * mid, n_mid), row_three(-2.0 * high, n_low)])


def three_rows(points):
    rows = lax.broadcasted_iota(jnp.int32, points.shape, 0)
    return jnp.where(rows < 3, points, 0.0)


def shifted(points, code):
    code = jnp.where(code >= 13, code + 1, code)
    axis_row = lax.broadcasted_iota(jnp.int32, points.shape, 0)
    move = jnp.where(
        axis_row == 0,
        (code // 9 - 1).astype(F32),
        jnp.where(axis_row == 1, ((code // 3) % 3 - 1).astype(F32), (code % 3 - 1).astype(F32)),
    )
    return three_rows(2.0 * (points + (move - 0.5)))


def centred(points):
    return three_rows(2.0 * (points - 0.5))


def slot_of(nb_ref, row, entry, box_count, box_total):
    owner_box = nb_ref[row, entry]
    step = owner_box // box_count - lax.axis_index("box") + 1
    step = jnp.where(step < 0, step + box_total, step)
    step = jnp.where(step >= box_total, step - box_total, step)
    return step * box_count + owner_box % box_count


def dot_tn(a, b):
    return lax.dot_general(a, b, (((0,), (0,)), ((), ())), preferred_element_type=F32)


def meet(peers):
    barrier = pltpu.get_barrier_semaphore()
    for peer in peers:
        pl.semaphore_signal(barrier, inc=1, device_id=peer, device_id_type=MESH)
    return lambda: pl.semaphore_wait(barrier, len(peers))


def send(source, target, sends, recvs, index, peer):
    one = pltpu.make_async_remote_copy(
        src_ref=source, dst_ref=target, send_sem=sends.at[index], recv_sem=recvs.at[index],
        device_id=peer, device_id_type=MESH)
    one.start()
    return one


def exchange_kernel(box_total, col_count, group, skeleton, points_ref, order_ref, proxy_ref,
                    pivot_ref, points_out, proxy_out, pivot_out, points, order, sends, recvs,
                    local):
    me = lax.axis_index("col")
    place = lax.axis_index("box")
    _, box_count, count = points_ref.shape
    after = {"box": lax.rem(place + 1, box_total)}
    before = {"box": lax.rem(place + box_total - 1, box_total)}
    across = {"col": lax.rem(me + group, col_count)}
    mine = me // group
    own = ((points_ref, points), (order_ref, order), (proxy_ref, proxy_out.at[0]),
           (pivot_ref, pivot_out.at[mine]))
    loads = []
    for i, (source, target) in enumerate(own):
        copy = pltpu.make_async_copy(source, target, local.at[i])
        copy.start()
        loads.append(copy)
    arrived = meet([before, after, across])
    for copy in loads:
        copy.wait()
    width = (count - skeleton) // col_count
    for box in range(box_count):
        row = order[box:box + 1, :]
        strips = [row[:, skeleton + s * width:skeleton + (s + 1) * width]
                  for c in range(group) for s in range(c, col_count, group)]
        row = jnp.concatenate([row[:, 0:skeleton]] + strips, axis=1)
        one_hot = (lax.broadcasted_iota(jnp.int32, (count, count), 0) == row).astype(F32)
        whole = jnp.concatenate([points[axis, box:box + 1, :] for axis in range(3)]
                                + [jnp.zeros((5, count), F32)], axis=0)
        rows = jnp.concatenate(list(three(whole)) + [jnp.zeros_like(whole)], axis=0)
        picked = jnp.dot(rows.astype(BF16), one_hot.astype(BF16), preferred_element_type=F32)
        points_out[1, box] = (picked[0:8] + picked[8:16]) + picked[16:24]
    arrived()
    jobs = [
        send(points_out.at[1], points_out.at[0], sends, recvs, 0, after),
        send(points_out.at[1], points_out.at[2], sends, recvs, 1, before),
        send(proxy_ref, proxy_out.at[1], sends, recvs, 2, across),
        send(pivot_ref, pivot_out.at[mine], sends, recvs, 3, across),
    ]
    for copy in jobs:
        copy.wait()


def tile_kernel(box_total, entries, group, skeleton, nb_ref, place_ref, points_ref, proxy_ref,
                cross_ref, targets, sources, squares, tiles, total):
    count = points_ref.shape[3]
    box_count, _, share = proxy_ref.shape
    proxies = box_count * share
    me = lax.axis_index("col")
    box = me // group
    first = lax.rem(me, group) * entries
    sources[...] = source_rows(centred(points_ref[1, box]))
    for d in range(box_count):
        directions = jnp.concatenate([proxy_ref[d], jnp.zeros((5, share), F32)], axis=0)
        targets[:, d * share:(d + 1) * share] = target_rows((2.0 * proxy_radius) * directions)
    for k in range(entries):
        slot = slot_of(nb_ref, box, first + k, box_count, box_total)
        here = shifted(points_ref[slot // box_count, slot % box_count], place_ref[box, first + k])
        targets[:, proxies + k * count:proxies + (k + 1) * count] = target_rows(here)
    block = tiles.shape[1] // 2

    def measure(base, slot):
        squares[slot] = dot_tn(targets[:, pl.ds(pl.multiple_of(base, block), block)],
                               sources[...])

    def evaluate(slot, i):
        inner = slice(i * ROWS, (i + 1) * ROWS)
        lower = slice(block + i * ROWS, block + (i + 1) * ROWS)
        for c in range(0, count, 256):
            here = slice(c, c + 256)
            there = slice(count + c, count + c + 256)
            real, imag = kernel_values(squares[slot, inner, here])
            real = real.astype(BF16)
            imag = imag.astype(BF16)
            tiles[slot, inner, here] = real
            tiles[slot, inner, there] = imag
            tiles[slot, lower, here] = imag
            tiles[slot, lower, there] = -real

    def gather(slot, left, c):
        here = slice(c, c + 256)
        total[:, here] += plain(left, tiles[slot, :, here])

    def stage(ahead, now, before):
        measure(*ahead)
        steps = block // ROWS
        pieces = 2 * count // 256
        left = None if before is None else jnp.transpose(tiles[before, :, 0:skeleton])
        for i in range(steps):
            if left is not None and i % (steps // pieces) == 0:
                gather(before, left, i // (steps // pieces) * 256)
            evaluate(now, i)

    total[...] = jnp.zeros_like(total)
    blocks = proxies // block
    measure(0, 0)
    for i in range(blocks):
        stage(((i + 1) * block, (i + 1) % 2), i % 2, (i + 1) % 2 if i else None)
    per = count // block
    last = proxies + (entries * per - 1) * block

    @pl.loop(0, entries)
    def _(k):
        base = proxies + k * count
        for i in range(per):
            now = (blocks + i) % 2
            stage((jnp.minimum(base + (i + 1) * block, last), 1 - now), now, 1 - now)

    end = (blocks + per - 1) % 2
    left = jnp.transpose(tiles[end, :, 0:skeleton])
    for c in range(0, 2 * count, 256):
        gather(end, left, c)
    for p in range(2):
        cross_ref[p] = total[:, p * count:(p + 1) * count]


def lanes(block, k):
    return jnp.take_along_axis(block, jnp.full(block.shape, k, jnp.int32), axis=1)


def across_rows(block, k):
    return jnp.broadcast_to(block[k:k + 1, :], block.shape)


def block_inverse(re, im, start, home):
    count = len(re)
    shape = re[0].shape
    lane = lax.broadcasted_iota(jnp.int32, shape, 1)
    sub = lax.broadcasted_iota(jnp.int32, shape, 0)
    inside = (lane >= start) & (lane < start + 8 * count)
    re = [jnp.where(inside, block, jnp.where(lane - home == sub + 8 * v, 1.0, 0.0))
          for v, block in enumerate(re)]
    im = [jnp.where(inside, block, 0.0) for block in im]
    for r in range(count):
        order = [r] + [v for v in range(count) if v > r] + list(range(r))
        spread = {}
        for v in order:
            for j in range(8):
                k = start + 8 * r + j
                spread[v, j] = (lanes(re[v], k), lanes(im[v], k))
        cols = {j: spread[r, j] for j in range(8)}
        cols["row"] = (re[r], im[r])
        for t in range(0, 8, 2):
            (ar, ai), (cr, ci) = cols.pop(t), cols.pop(t + 1)
            a, d = across_rows(ar, t), across_rows(cr, t + 1)
            br, bi = across_rows(cr, t), across_rows(ci, t)
            scale = 1.0 / (a * d - (br * br + bi * bi))
            a, d, br, bi = a * scale, d * scale, br * scale, bi * scale
            at, on = sub == t, sub == t + 1
            here = at | on
            e0r = jnp.where(at, -d, jnp.where(on, br, ar * d - (cr * br + ci * bi)))
            e0i = jnp.where(at, 0.0, jnp.where(on, -bi, ai * d - (ci * br - cr * bi)))
            e1r = jnp.where(at, br, jnp.where(on, -a, cr * a - (ar * br - ai * bi)))
            e1i = jnp.where(at, bi, jnp.where(on, 0.0, ci * a - (ar * bi + ai * br)))
            for key, (xr, xi) in cols.items():
                x0r, x0i = across_rows(xr, t), across_rows(xi, t)
                x1r, x1i = across_rows(xr, t + 1), across_rows(xi, t + 1)
                lessr = (e0r * x0r - e0i * x0i) + (e1r * x1r - e1i * x1i)
                lessi = (e0r * x0i + e0i * x0r) + (e1r * x1i + e1i * x1r)
                cols[key] = (jnp.where(here, 0.0, xr) - lessr, jnp.where(here, 0.0, xi) - lessi)
            if t < 6:
                yield None
        re[r], im[r] = cols["row"]
        rows = [(across_rows(re[r], j), across_rows(im[r], j)) for j in range(8)]
        for v in order[1:]:
            lessr = [spread[v, j][0] * rows[j][0] - spread[v, j][1] * rows[j][1]
                     for j in range(8)]
            lessi = [spread[v, j][0] * rows[j][1] + spread[v, j][1] * rows[j][0]
                     for j in range(8)]
            re[v] = re[v] - summed(lessr)
            im[v] = im[v] - summed(lessi)
        yield jnp.concatenate(re, axis=0), jnp.concatenate(im, axis=0)


def summed(terms):
    while len(terms) > 1:
        terms = [terms[i] + terms[i + 1] for i in range(0, len(terms), 2)]
    return terms[0]


def plain(a, b):
    return jnp.dot(a, b, preferred_element_type=F32)


def solve_kernel(group, cross_ref, cross_in, x_ref, mat, head, tail):
    n = x_ref.shape[1]
    width = x_ref.shape[2]
    nb = NBLK
    side = lax.rem(lax.axis_index("col"), group)
    diagonal = lax.broadcasted_iota(jnp.int32, (128, 128), 0) == lax.broadcasted_iota(
        jnp.int32, (128, 128), 1
    )
    gram = cross_ref[:, :, 0:n] + cross_in[:, :, 0:n]
    ridge = 0.0
    for c in range(0, n, 128):
        ridge = ridge + jnp.where(diagonal, gram[0, c:c + 128, c:c + 128], 0.0)
    ridge = ridge_share * jnp.sum(ridge) / n
    mat[:, :, 0:n] = gram
    for c in range(0, n, 128):
        here = slice(c, c + 128)
        mat[0, here, here] = gram[0, here, here] + jnp.where(diagonal, ridge, 0.0)
    mine = pl.ds(pl.multiple_of(n + side * width, 128), width)
    mat[:, :, n:] = cross_ref[:, :, mine] + cross_in[:, :, mine]
    head[...] = jnp.zeros_like(head)
    tail[...] = jnp.zeros_like(tail)

    def pick(block):
        return [block[8 * v:8 * v + 8] for v in range(nb // 8)]

    def put(ref, at, w, re, im):
        where = slice(256 * w, 256 * w + 256)
        for base, block in ((at, [re, im]), (128 + at, [-im, re])):
            high, rest = split(jnp.concatenate(block, axis=1))
            ref[0, base:base + nb, where] = high
            ref[1, base:base + nb, where] = rest

    def clear(ref, at):
        for base in (at, 128 + at):
            ref[:, base:base + nb, :] = jnp.zeros((2, nb, ref.shape[2]), BF16)

    def doubled(re, im):
        return jnp.concatenate(split(jnp.concatenate([re, im], axis=1)), axis=0)

    def product(left, ref, w):
        where = slice(256 * w, 256 * w + 256)
        half = left.shape[0] // 2
        both = plain(left, ref[0, :, where])
        return both[0:half] + (both[half:] + plain(left[0:half], ref[1, :, where]))

    for step in block_inverse(pick(mat[0, 0:nb, 0:128]), pick(mat[1, 0:nb, 0:128]), 0, nb):
        found = step or None
    for j in range(n // nb):
        rows = slice(j * nb, (j + 1) * nb)
        after = slice((j + 1) * nb, (j + 2) * nb)
        q = (j * nb) // 128 * 128
        at = j * nb - q
        home = (at + nb) % 128
        windows = list(range((j + 1) * nb // 128, mat.shape[2] // 128))
        factor = doubled(*found)
        left = doubled(mat[0, :, q:q + 128], mat[1, :, q:q + 128])
        held = {}

        def solve(w):
            here = slice(128 * w, 128 * w + 128)
            put(head, home, w, mat[0, rows, here], mat[1, rows, here])
            held[w] = product(factor, head, w)
            put(tail, at, w, held[w][:, 0:128], held[w][:, 128:])

        def change(w):
            here = slice(128 * w, 128 * w + 128)
            less = product(left, tail, w)
            mat[0, :, here] = mat[0, :, here] - less[:, 0:128]
            mat[1, :, here] = mat[1, :, here] - less[:, 128:]
            mat[0, rows, here] = held[w][:, 0:128]
            mat[1, rows, here] = held[w][:, 128:]

        first = windows[0]
        solve(first)
        pivots = iter(())
        if (j + 1) * nb < n:
            here = slice(128 * first, 128 * first + 128)
            ahead = jnp.concatenate([left[after], left[n + (j + 1) * nb:n + (j + 2) * nb]], axis=0)
            less = product(ahead, tail, first)
            to = (j + 1) * nb % 128
            pivots = block_inverse(pick(mat[0, after, here] - less[:, 0:128]),
                                   pick(mat[1, after, here] - less[:, 128:]),
                                   to, (to + nb) % 128)
        tasks = [functools.partial(solve, w) for w in windows[1:]]
        tasks += [functools.partial(change, w) for w in windows]
        tasks.append(functools.partial(clear, head, home))
        tasks.append(functools.partial(clear, tail, at))
        steps = nb // 2
        done = 0
        for i, task in enumerate(tasks):
            task()
            upto = (i + 1) * steps // len(tasks)
            for _ in range(upto - done):
                found = next(pivots, None) or found
            done = upto
        for step in pivots:
            found = step or found
    x_ref[...] = mat[:, :, n:]


def split(x):
    high = x.astype(BF16)
    return high, (x - high.astype(F32)).astype(BF16)


def left_side(xr, xi):
    return jnp.concatenate(split(jnp.concatenate(
        [jnp.concatenate([xr, -xi], axis=1), jnp.concatenate([xi, xr], axis=1)], axis=0)), axis=0)


def pivot_columns(pivot_ref, box):
    pieces = range(pivot_ref.shape[0])
    rows = [jnp.concatenate([pivot_ref[c, box, p:p + 1, :] for c in pieces], axis=1)
            for p in range(2)]
    return [jnp.transpose(jnp.broadcast_to(row, (128, row.shape[1]))) for row in rows]


def quarters(product):
    rows, cols = product.shape[0] // 2, product.shape[1] // 2
    return ((product[:rows, :cols] + product[:rows, cols:])
            + (product[rows:, :cols] + product[rows:, cols:]))


def form(turned, right, rest, blocks, pair):
    half = turned.shape[0] // 2
    both = plain(turned[...], right[0])
    blocks[pair] = rest - (both[0:half] + (both[half:] + plain(turned[0:half, :], right[1])))


def fold(blocks, pair, i, row, pivots, out_ref, to):
    qr, qi = pivots
    width = qr.shape[0]
    n = blocks.shape[2] // 2
    mine = blocks[pair, :, pl.ds(pl.multiple_of(i * n + row, 128), qr.shape[1])]
    br, bi = mine[0:width], mine[width:]
    wr = jnp.transpose(br * qr - bi * qi)
    wi = jnp.transpose(br * qi + bi * qr)
    upper = jnp.concatenate([jnp.concatenate([wr, -wi], axis=1),
                             jnp.concatenate([wi, wr], axis=1)], axis=0)
    whole = jnp.concatenate(split(blocks[pair, :, i * n:(i + 1) * n]), axis=1)
    update = quarters(plain(jnp.concatenate(split(upper), axis=0), whole))
    half = update.shape[0] // 2
    out_ref[to, 0] = out_ref[to, 0] - update[0:half]
    out_ref[to, 1] = out_ref[to, 1] - update[half:]


def first_row(group, count):
    return lax.axis_index("col") // group * count


def entry_squares(box_total, nb_ref, place_ref, points_ref, which, k, n, sources):
    box_count = points_ref.shape[1]
    place = slot_of(nb_ref, which, k, box_count, box_total)
    here = shifted(points_ref[place // box_count, place % box_count], place_ref[which, k])
    return dot_tn(sources[...], target_rows(here[:, 0:n]))


def evaluate(squares, n, width, right_at, rest_at, i, part=0, parts=1):
    rows = n + width
    for r in range(part * rows // parts, (part + 1) * rows // parts, ROWS):
        for c in range(0, n, 128):
            here = slice(i * n + c, i * n + c + 128)
            for p, value in enumerate(kernel_values(squares[r:r + ROWS, c:c + 128])):
                if r < n:
                    at = slice(p * n + r, p * n + r + ROWS)
                    right_at[0, at, here], right_at[1, at, here] = split(value)
                else:
                    rest_at[p * width + r - n:p * width + r - n + ROWS, here] = value


def half_sources(points, side, group, n, width):
    whole = source_rows(centred(points))
    half = whole[:, n:n + width]
    for c in range(1, group):
        half = jnp.where(side == c, whole[:, n + c * width:n + (c + 1) * width], half)
    return jnp.concatenate([whole[:, 0:n], half], axis=1)


def kernel_kernel(box_total, group, nb_ref, place_ref, points_ref, right_ref, rest_ref, sources,
                  squares):
    pairs, width, n = rest_ref.shape
    width, n = width // 2, n // 2
    me = lax.axis_index("col")
    fed = 1 - me // group
    sources[...] = half_sources(points_ref[1, fed], lax.rem(me, group), group, n, width)

    def measure(k, slot):
        squares[slot] = entry_squares(box_total, nb_ref, place_ref, points_ref, fed, k, n, sources)

    measure(0, 0)

    @pl.loop(0, pairs)
    def _(pair):
        for i in range(2):
            measure(jnp.minimum(2 * pair + i + 1, 2 * pairs - 1), 1 - i)
            evaluate(squares.at[i], n, width, right_ref.at[pair], rest_ref.at[pair], i)


def near_kernel(box_total, group, nb_ref, place_ref, points_ref, x_ref, pivot_ref,
                out_ref, sources, squares, right, rest, turned, blocks):
    n = x_ref.shape[1]
    width = x_ref.shape[2]
    box_count = points_ref.shape[1]
    entries = nb_ref.shape[1]
    me = lax.axis_index("col")
    box = me // group
    sources[...] = half_sources(points_ref[1, box], lax.rem(me, group), group, n, width)

    def measure(k):
        if k < entries:
            squares[k % 4] = entry_squares(box_total, nb_ref, place_ref, points_ref, box, k, n,
                                           sources)

    def values(k, part, parts):
        if k < entries:
            at = k // 2 % 2
            evaluate(squares.at[k % 4], n, width, right.at[at], rest.at[at], k % 2, part, parts)

    for k in range(4):
        measure(k)
    out_ref[...] = jnp.zeros_like(out_ref)
    values(0, 0, 1)
    turned[...] = left_side(jnp.transpose(x_ref[0]), jnp.transpose(x_ref[1]))
    pivots = pivot_columns(pivot_ref, box)
    row = first_row(group, out_ref.shape[2])
    values(1, 0, 1)
    pairs = entries // 2
    for pair in range(pairs + 1):
        if pair < pairs:
            form(turned, right.at[pair % 2], rest[pair % 2], blocks, pair)
        for i in range(2):
            k = 2 * pair + 2 + i
            values(k, 0, 2)
            if pair:
                done = 2 * pair - 2 + i
                fold(blocks, pair - 1, i, row, pivots, out_ref,
                     slot_of(nb_ref, box, done, box_count, box_total))
            values(k, 1, 2)
            measure(k + 2)


def far_kernel(box_total, group, nb_ref, buf_ref, right_ref, rest_ref, x_ref,
               mine_ref, pivot_ref, out_ref, inter_ref, turned, blocks):
    pairs = rest_ref.shape[0]
    me = lax.axis_index("col")
    box = me // group
    fed = 1 - box
    box_count = pivot_ref.shape[1]
    strip = inter_ref.shape[2]
    theirs = [jnp.transpose(x_ref[p]) for p in range(2)]
    turned[...] = left_side(*theirs)
    pivots = pivot_columns(pivot_ref, fed)
    row = first_row(group, out_ref.shape[2])
    for pair in range(pairs + 1):
        if pair < pairs:
            form(turned, right_ref.at[pair], rest_ref[pair], blocks, pair)
        if not pair:
            out_ref[...] = buf_ref[...]
        for i in range(2):
            if pair:
                fold(blocks, pair - 1, i, row, pivots, out_ref,
                     slot_of(nb_ref, fed, 2 * pair - 2 + i, box_count, box_total))
    for p in range(2):
        for block, where in ((jnp.transpose(mine_ref[p]), box), (theirs[p], fed)):
            piece = block[0:strip]
            for c in range(1, block.shape[0] // strip):
                piece = jnp.where(box == c, block[c * strip:(c + 1) * strip], piece)
            inter_ref[where, p] = piece


def reduce_kernel(box_total, buf_ref, out_ref, pair_in, line_out, line_in, side_out, side_in,
                  held, sends, recvs):
    me = lax.axis_index("col")
    place = lax.axis_index("box")
    side = lax.rem(me, 2)
    odd = lax.rem(place, 2)
    near = {"col": me + 1 - 2 * side}
    relay = {"box": lax.rem(place + box_total + 4 * odd - 2, box_total)}
    source = {"box": lax.rem(place + box_total + 2 - 4 * odd, box_total)}
    twin = {"box": place + 1 - 2 * odd}
    meet([near, relay, source, twin])()
    box_count, _, strip, _ = out_ref.shape
    order = (2 * odd, 2 - 2 * odd, 1)
    piece = strip // PIECES
    chunks = [(d, p, pl.ds(i * piece, piece)) for d in range(box_count) for p in range(2)
              for i in range(PIECES)]
    wholes = [(d, p) for d in range(box_count) for p in range(2)]
    pairs = {}
    base = 0
    for g, parts in enumerate((chunks, wholes, wholes)):
        for i, part in enumerate(parts):
            d, p = part[:2]
            source_at = (order[g] * box_count + d, p, 1 - side) + part[2:]
            pairs[g, i] = send(buf_ref.at[source_at], pair_in.at[(g,) + part], sends, recvs,
                               base + i, near)
        base += len(parts)
    lines, sides = [], []
    for i, (d, p, some) in enumerate(chunks):
        pairs[0, i].wait()
        line_out[d, p, some] = (buf_ref[order[0] * box_count + d, p, side, some]
                                + pair_in[0, d, p, some])
        lines.append(send(line_out.at[d, p, some], line_in.at[d, p, some], sends, recvs,
                          base + i, relay))
    base += len(chunks)
    for i, (d, p) in enumerate(wholes):
        pairs[1, i].wait()
        held[d, p] = buf_ref[order[1] * box_count + d, p, side] + pair_in[1, d, p]
    for i, (d, p, some) in enumerate(chunks):
        lines[i].wait()
        side_out[d, p, some] = held[d, p, some] + line_in[d, p, some]
        sides.append(send(side_out.at[d, p, some], side_in.at[d, p, some], sends, recvs,
                          base + i, twin))
    for i, (d, p) in enumerate(wholes):
        pairs[2, i].wait()
        held[d, p] = buf_ref[box_count + d, p, side] + pair_in[2, d, p]
    for i, (d, p, some) in enumerate(chunks):
        sides[i].wait()
        out_ref[d, p, some] = held[d, p, some] + side_in[d, p, some]


def ring(count, step):
    return [(i, (i + step) % count) for i in range(count)]


def on_device(
    box_points, proxy_directions, point_order, neighbour_boxes, neighbour_places, pivot_inverse
):
    box_count, _, point_count = box_points.shape
    col_count = lax.axis_size("col")
    box_total = lax.axis_size("box")
    group = col_count // box_count
    listed = neighbour_boxes.shape[1]
    entries = listed // group
    width = pivot_inverse.shape[2]
    rest = width * col_count
    skeleton = point_count - rest
    half = rest // group
    share = proxy_directions.shape[1]
    dma = pltpu.SemaphoreType.DMA

    points, proxies, pivots = pl.pallas_call(
        functools.partial(exchange_kernel, box_total, col_count, group, skeleton),
        out_shape=(
            jax.ShapeDtypeStruct((3, box_count, 8, point_count), F32),
            jax.ShapeDtypeStruct((box_count,) + proxy_directions.shape, F32),
            jax.ShapeDtypeStruct((box_count,) + pivot_inverse.shape, F32),
        ),
        in_specs=[HBM] * 4,
        out_specs=(VMEM,) * 3,
        scratch_shapes=[pltpu.VMEM((3, box_count, point_count), F32),
                        pltpu.VMEM(point_order.shape, jnp.int32),
                        dma((4,)), dma((4,)), dma((4,))],
        compiler_params=params(collective_id=0, has_side_effects=True),
        cost_estimate=pl.CostEstimate(flops=4 * 10**9, bytes_accessed=16 * 10**6,
                                      transcendentals=0),
    )(*(pltpu.with_memory_space_constraint(one, pltpu.HBM) for one in (
        jnp.transpose(box_points, (1, 0, 2)), point_order, proxy_directions, pivot_inverse)))

    rows = box_count * share + entries * point_count
    cross = pl.pallas_call(
        functools.partial(tile_kernel, box_total, entries, group, skeleton),
        out_shape=jax.ShapeDtypeStruct((2, skeleton, point_count), F32),
        in_specs=[SMEM, SMEM, VMEM, VMEM],
        out_specs=VMEM,
        scratch_shapes=[
            pltpu.VMEM((DEPTH, rows), BF16),
            pltpu.VMEM((DEPTH, point_count), BF16),
            pltpu.VMEM((2, BLOCK, point_count), F32),
            pltpu.VMEM((2, 2 * BLOCK, 2 * point_count), BF16),
            pltpu.VMEM((skeleton, 2 * point_count), F32),
        ],
        compiler_params=params(),
    )(neighbour_boxes, neighbour_places, points, proxies)
    pairs = [(i, i + 1 - 2 * (i % 2)) for i in range(col_count)]
    cross_in = lax.ppermute(cross, "col", pairs)

    cover = pl.CostEstimate(flops=8 * 10**9, bytes_accessed=16 * 10**6, transcendentals=0)
    right, kept = pl.pallas_call(
        functools.partial(kernel_kernel, box_total, group),
        out_shape=(
            jax.ShapeDtypeStruct((listed // 2, 2, 2 * skeleton, 2 * skeleton), BF16),
            jax.ShapeDtypeStruct((listed // 2, 2 * half, 2 * skeleton), F32),
        ),
        in_specs=[SMEM, SMEM, VMEM],
        out_specs=(VMEM, VMEM),
        scratch_shapes=[
            pltpu.VMEM((DEPTH, skeleton + half), BF16),
            pltpu.VMEM((2, skeleton + half, skeleton), F32),
        ],
        compiler_params=params(),
        cost_estimate=cover,
    )(neighbour_boxes, neighbour_places, points)

    solved = pl.pallas_call(
        functools.partial(solve_kernel, group),
        out_shape=jax.ShapeDtypeStruct((2, skeleton, half), F32),
        in_specs=[VMEM] * 2,
        out_specs=VMEM,
        scratch_shapes=[
            pltpu.VMEM((2, skeleton, skeleton + half), F32),
            pltpu.VMEM((2, 256, 2 * (skeleton + half)), BF16),
            pltpu.VMEM((2, 256, 2 * (skeleton + half)), BF16),
        ],
        compiler_params=params(),
    )(cross, cross_in)
    arrived = lax.ppermute(solved, "col", ring(col_count, group))

    strips = skeleton // box_count
    buffer = pl.pallas_call(
        functools.partial(near_kernel, box_total, group),
        out_shape=jax.ShapeDtypeStruct((3 * box_count, 2, strips, skeleton), F32),
        in_specs=[SMEM, SMEM, VMEM, VMEM, VMEM],
        out_specs=VMEM,
        scratch_shapes=[
            pltpu.VMEM((DEPTH, skeleton + half), BF16),
            pltpu.VMEM((4, skeleton + half, skeleton), F32),
            pltpu.VMEM((2, 2, 2 * skeleton, 2 * skeleton), BF16),
            pltpu.VMEM((2, 2 * half, 2 * skeleton), F32),
            pltpu.VMEM((4 * half, 2 * skeleton), BF16),
            pltpu.VMEM((listed // 2, 2 * half, 2 * skeleton), F32),
        ],
        compiler_params=params(),
        cost_estimate=cover,
    )(neighbour_boxes, neighbour_places, points, solved, pivots)

    buffer, inter = pl.pallas_call(
        functools.partial(far_kernel, box_total, group),
        out_shape=(
            jax.ShapeDtypeStruct(buffer.shape, F32),
            jax.ShapeDtypeStruct((box_count, 2, width, skeleton), F32),
        ),
        in_specs=[SMEM] + [VMEM] * 6,
        out_specs=(VMEM, VMEM),
        scratch_shapes=[
            pltpu.VMEM((4 * half, 2 * skeleton), BF16),
            pltpu.VMEM((listed // 2, 2 * half, 2 * skeleton), F32),
        ],
        compiler_params=params(),
    )(neighbour_boxes, buffer, right, kept, arrived, solved, pivots)
    interpolation = jnp.swapaxes(inter, 2, 3)

    strip = skeleton // col_count
    block = (box_count, 2, strip, skeleton)
    jobs = (2 + 3 * PIECES) * 2 * box_count
    skeleton_update = pl.pallas_call(
        functools.partial(reduce_kernel, box_total),
        out_shape=jax.ShapeDtypeStruct(block, F32),
        in_specs=[VMEM],
        out_specs=VMEM,
        scratch_shapes=[
            pltpu.VMEM((3,) + block, F32),
            pltpu.VMEM(block, F32),
            pltpu.VMEM(block, F32),
            pltpu.VMEM(block, F32),
            pltpu.VMEM(block, F32),
            pltpu.VMEM(block, F32),
            dma((jobs,)),
            dma((jobs,)),
        ],
        compiler_params=params(collective_id=1, has_side_effects=True),
    )(buffer.reshape(3 * box_count, 2, group, strip, skeleton))
    return (interpolation, skeleton_update)


def solution(mesh):
    placed = (
        P("box", None, None),
        P(None, "col"),
        P("box", None),
        P("box", None),
        P("box", None),
        P("box", None, "col"),
    )
    return jax.shard_map(
        on_device,
        mesh=mesh,
        in_specs=placed,
        out_specs=(P("box", None, None, "col"), P("box", None, "col", None)),
        check_vma=False,
    )
```

```python
import functools
import math

import jax
import jax.numpy as jnp
from jax import lax
from jax.experimental import pallas as pl
from jax.experimental.pallas import tpu as pltpu
from jax.sharding import PartitionSpec as P

softening = 0.05
proxy_radius = 1.5
ridge_share = 0.05
NBLK = 32
BLOCK = 256
ROWS = 16
DEPTH = 64
PIECES = 2
EARLY = 2

SIN = (4.44287959, -7.30781805, 3.59778873, -0.79123822)
COS = (1.41420408, -6.97764206, 5.7152384, -1.72834866)

HBM = pl.BlockSpec(memory_space=pltpu.HBM)
VMEM = pl.BlockSpec(memory_space=pltpu.VMEM)
SMEM = pl.BlockSpec(memory_space=pltpu.SMEM)
MESH = pl.DeviceIdType.MESH
F32 = jnp.float32
BF16 = jnp.bfloat16


def params(**more):
    return pltpu.CompilerParams(vmem_limit_bytes=24 * 1024 * 1024, **more)


def horner(coefficients, z):
    total = coefficients[-1] * z + coefficients[-2]
    for one in coefficients[-3::-1]:
        total = total * z + one
    return total


def kernel_values(square):
    inverse = lax.rsqrt(square)
    turns = square * inverse
    part = turns - jnp.floor(turns + 0.5)
    z = part * part
    amplitude = inverse * (1.0 / (2.0 * math.pi))
    sine = part * horner(SIN, z)
    scaled = amplitude * sine
    return amplitude - scaled * sine, scaled * horner(COS, z)


def three(x):
    high = x.astype(BF16).astype(F32)
    rest = x - high
    mid = rest.astype(BF16).astype(F32)
    return high, mid, rest - mid


def row_three(block, row):
    third = lax.broadcasted_iota(jnp.int32, block.shape, 0) == 3
    return jnp.where(third, row, block)


def norm_of(points):
    return jnp.sum(points * points, axis=0, keepdims=True)


def stacked(groups):
    zero = jnp.zeros_like(groups[0])
    return jnp.concatenate(groups + [zero] * (DEPTH // 8 - len(groups)), axis=0).astype(BF16)


def target_rows(points):
    high, mid, low = three(points)
    n_high, n_mid, n_low = three(norm_of(points))
    return stacked([row_three(high, n_high), row_three(high, n_mid), row_three(mid, n_low),
                    row_three(high, 1.0), row_three(mid, 1.0), row_three(low, 1.0)])


def source_rows(points):
    high, mid, low = three(points)
    norm = norm_of(points) + 4.0 * softening * softening
    n_high, n_mid, n_low = three(norm)
    return stacked([row_three(-2.0 * high, 1.0), row_three(-2.0 * mid, 1.0),
                    row_three(-2.0 * high, 1.0), row_three(-2.0 * low, n_high),
                    row_three(-2.0 * mid, n_mid), row_three(-2.0 * high, n_low)])


def three_rows(points):
    rows = lax.broadcasted_iota(jnp.int32, points.shape, 0)
    return jnp.where(rows < 3, points, 0.0)


def shifted(points, code):
    code = jnp.where(code >= 13, code + 1, code)
    axis_row = lax.broadcasted_iota(jnp.int32, points.shape, 0)
    move = jnp.where(
        axis_row == 0,
        (code // 9 - 1).astype(F32),
        jnp.where(axis_row == 1, ((code // 3) % 3 - 1).astype(F32), (code % 3 - 1).astype(F32)),
    )
    return three_rows(2.0 * (points + (move - 0.5)))


def centred(points):
    return three_rows(2.0 * (points - 0.5))


def slot_of(nb_ref, row, entry, box_count, box_total):
    owner_box = nb_ref[row, entry]
    step = owner_box // box_count - lax.axis_index("box") + 1
    step = jnp.where(step < 0, step + box_total, step)
    step = jnp.where(step >= box_total, step - box_total, step)
    return step * box_count + owner_box % box_count


def dot_tn(a, b):
    return lax.dot_general(a, b, (((0,), (0,)), ((), ())), preferred_element_type=F32)


def meet(peers):
    barrier = pltpu.get_barrier_semaphore()
    for peer in peers:
        pl.semaphore_signal(barrier, inc=1, device_id=peer, device_id_type=MESH)
    return lambda: pl.semaphore_wait(barrier, len(peers))


def send(source, target, sends, recvs, index, peer):
    one = pltpu.make_async_remote_copy(
        src_ref=source, dst_ref=target, send_sem=sends.at[index], recv_sem=recvs.at[index],
        device_id=peer, device_id_type=MESH)
    one.start()
    return one


def exchange_kernel(box_total, col_count, group, skeleton, points_ref, order_ref, proxy_ref,
                    pivot_ref, points_out, proxy_out, pivot_out, points, order, sends, recvs,
                    local):
    me = lax.axis_index("col")
    place = lax.axis_index("box")
    _, box_count, count = points_ref.shape
    after = {"box": lax.rem(place + 1, box_total)}
    before = {"box": lax.rem(place + box_total - 1, box_total)}
    across = {"col": lax.rem(me + group, col_count)}
    mine = me // group
    own = ((points_ref, points), (order_ref, order), (proxy_ref, proxy_out.at[0]),
           (pivot_ref, pivot_out.at[mine]))
    loads = []
    for i, (source, target) in enumerate(own):
        copy = pltpu.make_async_copy(source, target, local.at[i])
        copy.start()
        loads.append(copy)
    arrived = meet([before, after, across])
    for copy in loads:
        copy.wait()
    width = (count - skeleton) // col_count
    for box in range(box_count):
        row = order[box:box + 1, :]
        strips = [row[:, skeleton + s * width:skeleton + (s + 1) * width]
                  for c in range(group) for s in range(c, col_count, group)]
        row = jnp.concatenate([row[:, 0:skeleton]] + strips, axis=1)
        one_hot = (lax.broadcasted_iota(jnp.int32, (count, count), 0) == row).astype(F32)
        whole = jnp.concatenate([points[axis, box:box + 1, :] for axis in range(3)]
                                + [jnp.zeros((5, count), F32)], axis=0)
        rows = jnp.concatenate(list(three(whole)) + [jnp.zeros_like(whole)], axis=0)
        picked = jnp.dot(rows.astype(BF16), one_hot.astype(BF16), preferred_element_type=F32)
        points_out[1, box] = (picked[0:8] + picked[8:16]) + picked[16:24]
    arrived()
    jobs = [
        send(points_out.at[1], points_out.at[0], sends, recvs, 0, after),
        send(points_out.at[1], points_out.at[2], sends, recvs, 1, before),
        send(proxy_ref, proxy_out.at[1], sends, recvs, 2, across),
        send(pivot_ref, pivot_out.at[mine], sends, recvs, 3, across),
    ]
    for copy in jobs:
        copy.wait()


def tile_kernel(box_total, entries, group, skeleton, nb_ref, place_ref, points_ref, proxy_ref,
                cross_ref, targets, sources, squares, tiles, total):
    count = points_ref.shape[3]
    box_count, _, share = proxy_ref.shape
    proxies = box_count * share
    me = lax.axis_index("col")
    box = me // group
    first = lax.rem(me, group) * entries
    sources[...] = source_rows(centred(points_ref[1, box]))
    for d in range(box_count):
        directions = jnp.concatenate([proxy_ref[d], jnp.zeros((5, share), F32)], axis=0)
        targets[:, d * share:(d + 1) * share] = target_rows((2.0 * proxy_radius) * directions)
    for k in range(entries):
        slot = slot_of(nb_ref, box, first + k, box_count, box_total)
        here = shifted(points_ref[slot // box_count, slot % box_count], place_ref[box, first + k])
        targets[:, proxies + k * count:proxies + (k + 1) * count] = target_rows(here)
    block = tiles.shape[1] // 2

    def measure(base, slot):
        squares[slot] = dot_tn(targets[:, base:base + block], sources[...])

    def evaluate(slot, i):
        inner = slice(i * ROWS, (i + 1) * ROWS)
        lower = slice(block + i * ROWS, block + (i + 1) * ROWS)
        for c in range(0, count, 256):
            here = slice(c, c + 256)
            there = slice(count + c, count + c + 256)
            real, imag = kernel_values(squares[slot, inner, here])
            real = real.astype(BF16)
            imag = imag.astype(BF16)
            tiles[slot, inner, here] = real
            tiles[slot, inner, there] = imag
            tiles[slot, lower, here] = imag
            tiles[slot, lower, there] = -real

    def gather(slot, left, c):
        here = slice(c, c + 256)
        total[:, here] += plain(left, tiles[slot, :, here])

    def stage(ahead, now, before):
        measure(*ahead)
        steps = block // ROWS
        pieces = 2 * count // 256
        left = None if before is None else jnp.transpose(tiles[before, :, 0:skeleton])
        for i in range(steps):
            if left is not None and i % (steps // pieces) == 0:
                gather(before, left, i // (steps // pieces) * 256)
            evaluate(now, i)

    total[...] = jnp.zeros_like(total)
    blocks = proxies // block
    measure(0, 0)
    for i in range(blocks):
        stage(((i + 1) * block, (i + 1) % 2), i % 2, (i + 1) % 2 if i else None)
    last = blocks + entries * (count // block) - 1
    for i in range(blocks, last + 1):
        stage((min(i + 1, last) * block, (i + 1) % 2), i % 2, (i + 1) % 2)
    end = last % 2
    left = jnp.transpose(tiles[end, :, 0:skeleton])
    for c in range(0, 2 * count, 256):
        gather(end, left, c)
    for p in range(2):
        cross_ref[p] = total[:, p * count:(p + 1) * count]


def lanes(block, k):
    return jnp.take_along_axis(block, jnp.full(block.shape, k, jnp.int32), axis=1)


def across_rows(block, k):
    return jnp.broadcast_to(block[k:k + 1, :], block.shape)


def block_inverse(re, im, start, home):
    count = len(re)
    shape = re[0].shape
    lane = lax.broadcasted_iota(jnp.int32, shape, 1)
    sub = lax.broadcasted_iota(jnp.int32, shape, 0)
    inside = (lane >= start) & (lane < start + 8 * count)
    re = [jnp.where(inside, block, jnp.where(lane - home == sub + 8 * v, 1.0, 0.0))
          for v, block in enumerate(re)]
    im = [jnp.where(inside, block, 0.0) for block in im]
    for r in range(count):
        order = [r] + [v for v in range(count) if v > r] + list(range(r))
        spread = {}
        for v in order:
            for j in range(8):
                k = start + 8 * r + j
                spread[v, j] = (lanes(re[v], k), lanes(im[v], k))
        cols = {j: spread[r, j] for j in range(8)}
        cols["row"] = (re[r], im[r])
        for t in range(0, 8, 2):
            (ar, ai), (cr, ci) = cols.pop(t), cols.pop(t + 1)
            a, d = across_rows(ar, t), across_rows(cr, t + 1)
            br, bi = across_rows(cr, t), across_rows(ci, t)
            scale = 1.0 / (a * d - (br * br + bi * bi))
            a, d, br, bi = a * scale, d * scale, br * scale, bi * scale
            at, on = sub == t, sub == t + 1
            here = at | on
            e0r = jnp.where(at, -d, jnp.where(on, br, ar * d - (cr * br + ci * bi)))
            e0i = jnp.where(at, 0.0, jnp.where(on, -bi, ai * d - (ci * br - cr * bi)))
            e1r = jnp.where(at, br, jnp.where(on, -a, cr * a - (ar * br - ai * bi)))
            e1i = jnp.where(at, bi, jnp.where(on, 0.0, ci * a - (ar * bi + ai * br)))
            for key, (xr, xi) in cols.items():
                x0r, x0i = across_rows(xr, t), across_rows(xi, t)
                x1r, x1i = across_rows(xr, t + 1), across_rows(xi, t + 1)
                lessr = (e0r * x0r - e0i * x0i) + (e1r * x1r - e1i * x1i)
                lessi = (e0r * x0i + e0i * x0r) + (e1r * x1i + e1i * x1r)
                cols[key] = (jnp.where(here, 0.0, xr) - lessr, jnp.where(here, 0.0, xi) - lessi)
            if t < 6:
                yield None
        re[r], im[r] = cols["row"]
        rows = [(across_rows(re[r], j), across_rows(im[r], j)) for j in range(8)]
        for v in order[1:]:
            lessr = [spread[v, j][0] * rows[j][0] - spread[v, j][1] * rows[j][1]
                     for j in range(8)]
            lessi = [spread[v, j][0] * rows[j][1] + spread[v, j][1] * rows[j][0]
                     for j in range(8)]
            re[v] = re[v] - summed(lessr)
            im[v] = im[v] - summed(lessi)
        yield jnp.concatenate(re, axis=0), jnp.concatenate(im, axis=0)


def summed(terms):
    while len(terms) > 1:
        terms = [terms[i] + terms[i + 1] for i in range(0, len(terms), 2)]
    return terms[0]


def plain(a, b):
    return jnp.dot(a, b, preferred_element_type=F32)


def solve_kernel(group, cross_ref, cross_in, x_ref, mat, head, tail):
    n = x_ref.shape[1]
    width = x_ref.shape[2]
    nb = NBLK
    side = lax.rem(lax.axis_index("col"), group)
    diagonal = lax.broadcasted_iota(jnp.int32, (128, 128), 0) == lax.broadcasted_iota(
        jnp.int32, (128, 128), 1
    )
    gram = cross_ref[:, :, 0:n] + cross_in[:, :, 0:n]
    ridge = 0.0
    for c in range(0, n, 128):
        ridge = ridge + jnp.where(diagonal, gram[0, c:c + 128, c:c + 128], 0.0)
    ridge = ridge_share * jnp.sum(ridge) / n
    mat[:, :, 0:n] = gram
    for c in range(0, n, 128):
        here = slice(c, c + 128)
        mat[0, here, here] = gram[0, here, here] + jnp.where(diagonal, ridge, 0.0)
    mine = pl.ds(pl.multiple_of(n + side * width, 128), width)
    mat[:, :, n:] = cross_ref[:, :, mine] + cross_in[:, :, mine]
    head[...] = jnp.zeros_like(head)
    tail[...] = jnp.zeros_like(tail)

    def pick(block):
        return [block[8 * v:8 * v + 8] for v in range(nb // 8)]

    def put(ref, at, w, re, im):
        where = slice(256 * w, 256 * w + 256)
        for base, block in ((at, [re, im]), (128 + at, [-im, re])):
            high, rest = split(jnp.concatenate(block, axis=1))
            ref[0, base:base + nb, where] = high
            ref[1, base:base + nb, where] = rest

    def clear(ref, at):
        for base in (at, 128 + at):
            ref[:, base:base + nb, :] = jnp.zeros((2, nb, ref.shape[2]), BF16)

    def doubled(re, im):
        return jnp.concatenate(split(jnp.concatenate([re, im], axis=1)), axis=0)

    def product(left, ref, w):
        where = slice(256 * w, 256 * w + 256)
        half = left.shape[0] // 2
        both = plain(left, ref[0, :, where])
        return both[0:half] + (both[half:] + plain(left[0:half], ref[1, :, where]))

    for step in block_inverse(pick(mat[0, 0:nb, 0:128]), pick(mat[1, 0:nb, 0:128]), 0, nb):
        found = step or None
    for j in range(n // nb):
        rows = slice(j * nb, (j + 1) * nb)
        after = slice((j + 1) * nb, (j + 2) * nb)
        q = (j * nb) // 128 * 128
        at = j * nb - q
        home = (at + nb) % 128
        windows = list(range((j + 1) * nb // 128, mat.shape[2] // 128))
        factor = doubled(*found)
        left = doubled(mat[0, :, q:q + 128], mat[1, :, q:q + 128])
        held = {}

        def solve(w):
            here = slice(128 * w, 128 * w + 128)
            put(head, home, w, mat[0, rows, here], mat[1, rows, here])
            held[w] = product(factor, head, w)
            put(tail, at, w, held[w][:, 0:128], held[w][:, 128:])

        def change(w):
            here = slice(128 * w, 128 * w + 128)
            less = product(left, tail, w)
            mat[0, :, here] = mat[0, :, here] - less[:, 0:128]
            mat[1, :, here] = mat[1, :, here] - less[:, 128:]
            mat[0, rows, here] = held[w][:, 0:128]
            mat[1, rows, here] = held[w][:, 128:]

        first = windows[0]
        solve(first)
        pivots = iter(())
        if (j + 1) * nb < n:
            here = slice(128 * first, 128 * first + 128)
            ahead = jnp.concatenate([left[after], left[n + (j + 1) * nb:n + (j + 2) * nb]], axis=0)
            less = product(ahead, tail, first)
            to = (j + 1) * nb % 128
            pivots = block_inverse(pick(mat[0, after, here] - less[:, 0:128]),
                                   pick(mat[1, after, here] - less[:, 128:]),
                                   to, (to + nb) % 128)
        tasks = [functools.partial(solve, w) for w in windows[1:]]
        tasks += [functools.partial(change, w) for w in windows]
        tasks.append(functools.partial(clear, head, home))
        tasks.append(functools.partial(clear, tail, at))
        steps = nb // 2
        done = 0
        for i, task in enumerate(tasks):
            task()
            upto = (i + 1) * steps // len(tasks)
            for _ in range(upto - done):
                found = next(pivots, None) or found
            done = upto
        for step in pivots:
            found = step or found
    x_ref[...] = mat[:, :, n:]


def split(x):
    high = x.astype(BF16)
    return high, (x - high.astype(F32)).astype(BF16)


def left_side(xr, xi):
    return jnp.concatenate(split(jnp.concatenate(
        [jnp.concatenate([xr, -xi], axis=1), jnp.concatenate([xi, xr], axis=1)], axis=0)), axis=0)


def pivot_columns(pivot_ref, box):
    pieces = range(pivot_ref.shape[0])
    rows = [jnp.concatenate([pivot_ref[c, box, p:p + 1, :] for c in pieces], axis=1)
            for p in range(2)]
    return [jnp.transpose(jnp.broadcast_to(row, (128, row.shape[1]))) for row in rows]


def quarters(product):
    rows, cols = product.shape[0] // 2, product.shape[1] // 2
    return ((product[:rows, :cols] + product[:rows, cols:])
            + (product[rows:, :cols] + product[rows:, cols:]))


def form(turned, right, rest, blocks, pair):
    half = turned.shape[0] // 2
    both = plain(turned[...], right[0])
    blocks[pair] = rest - (both[0:half] + (both[half:] + plain(turned[0:half, :], right[1])))


def fold(blocks, pair, i, row, pivots, out_ref, to):
    qr, qi = pivots
    width = qr.shape[0]
    n = blocks.shape[2] // 2
    mine = blocks[pair, :, pl.ds(pl.multiple_of(i * n + row, 128), qr.shape[1])]
    br, bi = mine[0:width], mine[width:]
    wr = jnp.transpose(br * qr - bi * qi)
    wi = jnp.transpose(br * qi + bi * qr)
    upper = jnp.concatenate([jnp.concatenate([wr, -wi], axis=1),
                             jnp.concatenate([wi, wr], axis=1)], axis=0)
    whole = jnp.concatenate(split(blocks[pair, :, i * n:(i + 1) * n]), axis=1)
    update = quarters(plain(jnp.concatenate(split(upper), axis=0), whole))
    half = update.shape[0] // 2
    out_ref[to, 0] = out_ref[to, 0] - update[0:half]
    out_ref[to, 1] = out_ref[to, 1] - update[half:]


def first_row(group, count):
    return lax.axis_index("col") // group * count


def entry_squares(box_total, nb_ref, place_ref, points_ref, which, k, n, sources):
    box_count = points_ref.shape[1]
    place = slot_of(nb_ref, which, k, box_count, box_total)
    here = shifted(points_ref[place // box_count, place % box_count], place_ref[which, k])
    return dot_tn(sources[...], target_rows(here[:, 0:n]))


def evaluate(squares, n, width, right_at, rest_at, i, part=0, parts=1):
    rows = n + width
    for r in range(part * rows // parts, (part + 1) * rows // parts, ROWS):
        for c in range(0, n, 128):
            here = slice(i * n + c, i * n + c + 128)
            for p, value in enumerate(kernel_values(squares[r:r + ROWS, c:c + 128])):
                if r < n:
                    at = slice(p * n + r, p * n + r + ROWS)
                    right_at[0, at, here], right_at[1, at, here] = split(value)
                else:
                    rest_at[p * width + r - n:p * width + r - n + ROWS, here] = value


def half_sources(points, side, group, n, width):
    whole = source_rows(centred(points))
    half = whole[:, n:n + width]
    for c in range(1, group):
        half = jnp.where(side == c, whole[:, n + c * width:n + (c + 1) * width], half)
    return jnp.concatenate([whole[:, 0:n], half], axis=1)


def kernel_kernel(box_total, group, nb_ref, place_ref, points_ref, right_ref, rest_ref, sources,
                  squares):
    pairs, width, n = rest_ref.shape
    width, n = width // 2, n // 2
    me = lax.axis_index("col")
    fed = 1 - me // group
    sources[...] = half_sources(points_ref[1, fed], lax.rem(me, group), group, n, width)

    def measure(k, slot):
        squares[slot] = entry_squares(box_total, nb_ref, place_ref, points_ref, fed, k, n, sources)

    measure(0, 0)

    @pl.loop(0, pairs)
    def _(pair):
        for i in range(2):
            measure(jnp.minimum(2 * pair + i + 1, 2 * pairs - 1), 1 - i)
            evaluate(squares.at[i], n, width, right_ref.at[pair], rest_ref.at[pair], i)


def near_kernel(box_total, group, nb_ref, place_ref, points_ref, x_ref, pivot_ref,
                out_ref, right_ref, rest_ref, sources, squares, right, rest, turned, blocks):
    n = x_ref.shape[1]
    width = x_ref.shape[2]
    box_count = points_ref.shape[1]
    entries = nb_ref.shape[1]
    me = lax.axis_index("col")
    box = me // group
    for i, which in enumerate((box, 1 - box)):
        sources[i] = half_sources(points_ref[1, which], lax.rem(me, group), group, n, width)

    def measure(k):
        if k < entries + 2:
            other = k >= entries
            squares[k % 4] = entry_squares(box_total, nb_ref, place_ref, points_ref,
                                           1 - box if other else box, k - 2 if other else k, n,
                                           sources.at[int(other)])

    def values(k, part, parts):
        at = k // 2 % 2
        into = (right.at[at], rest.at[at]) if k < entries else (right_ref, rest_ref)
        evaluate(squares.at[k % 4], n, width, *into, k % 2, part, parts)

    for k in range(4):
        measure(k)
    out_ref[...] = jnp.zeros_like(out_ref)
    values(0, 0, 1)
    turned[...] = left_side(jnp.transpose(x_ref[0]), jnp.transpose(x_ref[1]))
    pivots = pivot_columns(pivot_ref, box)
    row = first_row(group, out_ref.shape[2])
    values(1, 0, 1)
    pairs = entries // 2
    for pair in range(pairs + 1):
        if pair < pairs:
            form(turned, right.at[pair % 2], rest[pair % 2], blocks, pair)
        for i in range(2):
            k = 2 * pair + 2 + i
            if k < entries + 2:
                values(k, 0, 2)
            if pair:
                done = 2 * pair - 2 + i
                fold(blocks, pair - 1, i, row, pivots, out_ref,
                     slot_of(nb_ref, box, done, box_count, box_total))
            if k < entries + 2:
                values(k, 1, 2)
            measure(k + 2)


def far_kernel(box_total, group, nb_ref, buf_ref, right_ref, rest_ref, right_last, rest_last,
               x_ref, mine_ref, pivot_ref, out_ref, inter_ref, turned, blocks):
    pairs = rest_ref.shape[0] + 1
    me = lax.axis_index("col")
    box = me // group
    fed = 1 - box
    box_count = pivot_ref.shape[1]
    strip = inter_ref.shape[2]
    theirs = [jnp.transpose(x_ref[p]) for p in range(2)]
    turned[...] = left_side(*theirs)
    pivots = pivot_columns(pivot_ref, fed)
    row = first_row(group, out_ref.shape[2])
    for pair in range(pairs + 1):
        if pair < pairs - 1:
            form(turned, right_ref.at[pair], rest_ref[pair], blocks, pair)
        elif pair < pairs:
            form(turned, right_last, rest_last[...], blocks, pair)
        if not pair:
            out_ref[...] = buf_ref[...]
        for i in range(2):
            if pair:
                fold(blocks, pair - 1, i, row, pivots, out_ref,
                     slot_of(nb_ref, fed, 2 * pair - 2 + i, box_count, box_total))
    for p in range(2):
        for block, where in ((jnp.transpose(mine_ref[p]), box), (theirs[p], fed)):
            piece = block[0:strip]
            for c in range(1, block.shape[0] // strip):
                piece = jnp.where(box == c, block[c * strip:(c + 1) * strip], piece)
            inter_ref[where, p] = piece


def reduce_kernel(box_total, buf_ref, out_ref, pair_in, line_out, line_in, side_out, side_in,
                  last_in, held, sends, recvs):
    me = lax.axis_index("col")
    place = lax.axis_index("box")
    side = lax.rem(me, 2)
    odd = lax.rem(place, 2)
    near = {"col": me + 1 - 2 * side}
    relay = {"box": lax.rem(place + box_total + 4 * odd - 2, box_total)}
    source = {"box": lax.rem(place + box_total + 2 - 4 * odd, box_total)}
    twin = {"box": place + 1 - 2 * odd}
    meet([near, relay, source, twin])()
    box_count, _, strip, _ = out_ref.shape
    order = (2 * odd, 2 - 2 * odd, 1)
    piece = strip // PIECES
    chunks = [(d, p, pl.ds(i * piece, piece)) for d in range(box_count) for p in range(2)
              for i in range(PIECES)]
    late, early = chunks[:-EARLY], chunks[-EARLY:]
    count = iter(range(sends.shape[0]))

    def pair(g, parts):
        return [send(buf_ref.at[(order[g] * box_count + part[0], part[1], 1 - side) + part[2:]],
                     pair_in.at[(g,) + part], sends, recvs, next(count), near) for part in parts]

    def both(g, part):
        return (buf_ref[(order[g] * box_count + part[0], part[1], side) + part[2:]]
                + pair_in[(g,) + part])

    def forward(source_ref, target_ref, part, peer):
        return send(source_ref.at[part], target_ref.at[part], sends, recvs, next(count), peer)

    line_pairs, line_early = pair(0, late), pair(0, early)
    side_early, side_pairs = pair(1, early), pair(1, late)
    own_pairs = pair(2, chunks)
    lines, sides, turns, directs, onward = [], [], [], [], []
    for part, copy in zip(late, line_pairs):
        copy.wait()
        line_out[part] = both(0, part)
        lines.append(forward(line_out, line_in, part, relay))
    for part, copy, other in zip(early, line_early, side_early):
        copy.wait()
        line_out[part] = both(0, part)
        turns.append(forward(line_out, line_in, part, twin))
        other.wait()
        side_out[part] = both(1, part)
        directs.append(forward(side_out, side_in, part, twin))
    for part, copy in zip(late, side_pairs):
        copy.wait()
        held[part] = both(1, part)
    for i, (part, copy) in enumerate(zip(late, lines)):
        copy.wait()
        side_out[part] = held[part] + line_in[part]
        sides.append(forward(side_out, side_in, part, twin))
        if i == 1:
            for some, turn in zip(early, turns):
                turn.wait()
                onward.append(forward(line_in, last_in, some, source))
    for part, copy in zip(chunks, own_pairs):
        copy.wait()
        held[part] = both(2, part)
    for part, direct, copy in zip(early, directs, onward):
        direct.wait()
        copy.wait()
        out_ref[part] = (held[part] + side_in[part]) + last_in[part]
    for part, copy in zip(late, sides):
        copy.wait()
        out_ref[part] = held[part] + side_in[part]


def ring(count, step):
    return [(i, (i + step) % count) for i in range(count)]


def on_device(
    box_points, proxy_directions, point_order, neighbour_boxes, neighbour_places, pivot_inverse
):
    box_count, _, point_count = box_points.shape
    col_count = lax.axis_size("col")
    box_total = lax.axis_size("box")
    group = col_count // box_count
    listed = neighbour_boxes.shape[1]
    entries = listed // group
    width = pivot_inverse.shape[2]
    rest = width * col_count
    skeleton = point_count - rest
    half = rest // group
    share = proxy_directions.shape[1]
    dma = pltpu.SemaphoreType.DMA

    points, proxies, pivots = pl.pallas_call(
        functools.partial(exchange_kernel, box_total, col_count, group, skeleton),
        out_shape=(
            jax.ShapeDtypeStruct((3, box_count, 8, point_count), F32),
            jax.ShapeDtypeStruct((box_count,) + proxy_directions.shape, F32),
            jax.ShapeDtypeStruct((box_count,) + pivot_inverse.shape, F32),
        ),
        in_specs=[HBM] * 4,
        out_specs=(VMEM,) * 3,
        scratch_shapes=[pltpu.VMEM((3, box_count, point_count), F32),
                        pltpu.VMEM(point_order.shape, jnp.int32),
                        dma((4,)), dma((4,)), dma((4,))],
        compiler_params=params(collective_id=0, has_side_effects=True),
        cost_estimate=pl.CostEstimate(flops=4 * 10**9, bytes_accessed=16 * 10**6,
                                      transcendentals=0),
    )(*(pltpu.with_memory_space_constraint(one, pltpu.HBM) for one in (
        jnp.transpose(box_points, (1, 0, 2)), point_order, proxy_directions, pivot_inverse)))

    rows = box_count * share + entries * point_count
    cross = pl.pallas_call(
        functools.partial(tile_kernel, box_total, entries, group, skeleton),
        out_shape=jax.ShapeDtypeStruct((2, skeleton, point_count), F32),
        in_specs=[SMEM, SMEM, VMEM, VMEM],
        out_specs=VMEM,
        scratch_shapes=[
            pltpu.VMEM((DEPTH, rows), BF16),
            pltpu.VMEM((DEPTH, point_count), BF16),
            pltpu.VMEM((2, BLOCK, point_count), F32),
            pltpu.VMEM((2, 2 * BLOCK, 2 * point_count), BF16),
            pltpu.VMEM((skeleton, 2 * point_count), F32),
        ],
        compiler_params=params(),
    )(neighbour_boxes, neighbour_places, points, proxies)
    pairs = [(i, i + 1 - 2 * (i % 2)) for i in range(col_count)]
    cross_in = lax.ppermute(cross, "col", pairs)

    cover = pl.CostEstimate(flops=8 * 10**9, bytes_accessed=16 * 10**6, transcendentals=0)
    right, kept = pl.pallas_call(
        functools.partial(kernel_kernel, box_total, group),
        out_shape=(
            jax.ShapeDtypeStruct((listed // 2 - 1, 2, 2 * skeleton, 2 * skeleton), BF16),
            jax.ShapeDtypeStruct((listed // 2 - 1, 2 * half, 2 * skeleton), F32),
        ),
        in_specs=[SMEM, SMEM, VMEM],
        out_specs=(VMEM, VMEM),
        scratch_shapes=[
            pltpu.VMEM((DEPTH, skeleton + half), BF16),
            pltpu.VMEM((2, skeleton + half, skeleton), F32),
        ],
        compiler_params=params(),
        cost_estimate=cover,
    )(neighbour_boxes, neighbour_places, points)

    solved = pl.pallas_call(
        functools.partial(solve_kernel, group),
        out_shape=jax.ShapeDtypeStruct((2, skeleton, half), F32),
        in_specs=[VMEM] * 2,
        out_specs=VMEM,
        scratch_shapes=[
            pltpu.VMEM((2, skeleton, skeleton + half), F32),
            pltpu.VMEM((2, 256, 2 * (skeleton + half)), BF16),
            pltpu.VMEM((2, 256, 2 * (skeleton + half)), BF16),
        ],
        compiler_params=params(),
    )(cross, cross_in)
    arrived = lax.ppermute(solved, "col", ring(col_count, group))

    strips = skeleton // box_count
    buffer, right_last, kept_last = pl.pallas_call(
        functools.partial(near_kernel, box_total, group),
        out_shape=(
            jax.ShapeDtypeStruct((3 * box_count, 2, strips, skeleton), F32),
            jax.ShapeDtypeStruct((2, 2 * skeleton, 2 * skeleton), BF16),
            jax.ShapeDtypeStruct((2 * half, 2 * skeleton), F32),
        ),
        in_specs=[SMEM, SMEM, VMEM, VMEM, VMEM],
        out_specs=(VMEM,) * 3,
        scratch_shapes=[
            pltpu.VMEM((box_count, DEPTH, skeleton + half), BF16),
            pltpu.VMEM((4, skeleton + half, skeleton), F32),
            pltpu.VMEM((2, 2, 2 * skeleton, 2 * skeleton), BF16),
            pltpu.VMEM((2, 2 * half, 2 * skeleton), F32),
            pltpu.VMEM((4 * half, 2 * skeleton), BF16),
            pltpu.VMEM((listed // 2, 2 * half, 2 * skeleton), F32),
        ],
        compiler_params=params(),
        cost_estimate=cover,
    )(neighbour_boxes, neighbour_places, points, solved, pivots)

    buffer, inter = pl.pallas_call(
        functools.partial(far_kernel, box_total, group),
        out_shape=(
            jax.ShapeDtypeStruct(buffer.shape, F32),
            jax.ShapeDtypeStruct((box_count, 2, width, skeleton), F32),
        ),
        in_specs=[SMEM] + [VMEM] * 8,
        out_specs=(VMEM, VMEM),
        scratch_shapes=[
            pltpu.VMEM((4 * half, 2 * skeleton), BF16),
            pltpu.VMEM((listed // 2, 2 * half, 2 * skeleton), F32),
        ],
        compiler_params=params(),
    )(neighbour_boxes, buffer, right, kept, right_last, kept_last, arrived, solved, pivots)
    interpolation = jnp.swapaxes(inter, 2, 3)

    strip = skeleton // col_count
    block = (box_count, 2, strip, skeleton)
    jobs = 5 * PIECES * 2 * box_count + EARLY
    skeleton_update = pl.pallas_call(
        functools.partial(reduce_kernel, box_total),
        out_shape=jax.ShapeDtypeStruct(block, F32),
        in_specs=[VMEM],
        out_specs=VMEM,
        scratch_shapes=[
            pltpu.VMEM((3,) + block, F32),
            pltpu.VMEM(block, F32),
            pltpu.VMEM(block, F32),
            pltpu.VMEM(block, F32),
            pltpu.VMEM(block, F32),
            pltpu.VMEM(block, F32),
            pltpu.VMEM(block, F32),
            dma((jobs,)),
            dma((jobs,)),
        ],
        compiler_params=params(collective_id=1, has_side_effects=True),
    )(buffer.reshape(3 * box_count, 2, group, strip, skeleton))
    return (interpolation, skeleton_update)


def solution(mesh):
    placed = (
        P("box", None, None),
        P(None, "col"),
        P("box", None),
        P("box", None),
        P("box", None),
        P("box", None, "col"),
    )
    return jax.shard_map(
        on_device,
        mesh=mesh,
        in_specs=placed,
        out_specs=(P("box", None, None, "col"), P("box", None, "col", None)),
        check_vma=False,
    )
```

```python
import functools
import math

import jax
import jax.numpy as jnp
from jax import lax
from jax.experimental import pallas as pl
from jax.experimental.pallas import tpu as pltpu
from jax.sharding import PartitionSpec as P

softening = 0.05
proxy_radius = 1.5
ridge_share = 0.05
NBLK = 32
BLOCK = 256
ROWS = 16
DEPTH = 64
PIECES = 4
EARLY = 6

SIN = (4.44287959, -7.30781805, 3.59778873, -0.79123822)
COS = (1.41420408, -6.97764206, 5.7152384, -1.72834866)

HBM = pl.BlockSpec(memory_space=pltpu.HBM)
VMEM = pl.BlockSpec(memory_space=pltpu.VMEM)
SMEM = pl.BlockSpec(memory_space=pltpu.SMEM)
MESH = pl.DeviceIdType.MESH
F32 = jnp.float32
BF16 = jnp.bfloat16


def params(**more):
    return pltpu.CompilerParams(vmem_limit_bytes=24 * 1024 * 1024, **more)


def horner(coefficients, z):
    total = coefficients[-1] * z + coefficients[-2]
    for one in coefficients[-3::-1]:
        total = total * z + one
    return total


def kernel_values(square):
    inverse = lax.rsqrt(square)
    turns = square * inverse
    part = turns - jnp.floor(turns + 0.5)
    z = part * part
    amplitude = inverse * (1.0 / (2.0 * math.pi))
    sine = part * horner(SIN, z)
    scaled = amplitude * sine
    return amplitude - scaled * sine, scaled * horner(COS, z)


def three(x):
    high = x.astype(BF16).astype(F32)
    rest = x - high
    mid = rest.astype(BF16).astype(F32)
    return high, mid, rest - mid


def row_three(block, row):
    third = lax.broadcasted_iota(jnp.int32, block.shape, 0) == 3
    return jnp.where(third, row, block)


def norm_of(points):
    return jnp.sum(points * points, axis=0, keepdims=True)


def stacked(groups):
    zero = jnp.zeros_like(groups[0])
    return jnp.concatenate(groups + [zero] * (DEPTH // 8 - len(groups)), axis=0).astype(BF16)


def target_rows(points):
    high, mid, low = three(points)
    n_high, n_mid, n_low = three(norm_of(points))
    return stacked([row_three(high, n_high), row_three(high, n_mid), row_three(mid, n_low),
                    row_three(high, 1.0), row_three(mid, 1.0), row_three(low, 1.0)])


def source_rows(points):
    high, mid, low = three(points)
    norm = norm_of(points) + 4.0 * softening * softening
    n_high, n_mid, n_low = three(norm)
    return stacked([row_three(-2.0 * high, 1.0), row_three(-2.0 * mid, 1.0),
                    row_three(-2.0 * high, 1.0), row_three(-2.0 * low, n_high),
                    row_three(-2.0 * mid, n_mid), row_three(-2.0 * high, n_low)])


def padded(points):
    return jnp.concatenate([points, jnp.zeros_like(points)], axis=0)


def three_rows(points):
    rows = lax.broadcasted_iota(jnp.int32, points.shape, 0)
    return jnp.where(rows < 3, points, 0.0)


def shifted(points, code):
    code = jnp.where(code >= 13, code + 1, code)
    axis_row = lax.broadcasted_iota(jnp.int32, points.shape, 0)
    move = jnp.where(
        axis_row == 0,
        (code // 9 - 1).astype(F32),
        jnp.where(axis_row == 1, ((code // 3) % 3 - 1).astype(F32), (code % 3 - 1).astype(F32)),
    )
    return three_rows(2.0 * (points + (move - 0.5)))


def centred(points):
    return three_rows(2.0 * (points - 0.5))


def slot_of(nb_ref, row, entry, box_count, box_total):
    owner_box = nb_ref[row, entry]
    step = owner_box // box_count - lax.axis_index("box") + 1
    step = jnp.where(step < 0, step + box_total, step)
    step = jnp.where(step >= box_total, step - box_total, step)
    return step * box_count + owner_box % box_count


def dot_tn(a, b):
    return lax.dot_general(a, b, (((0,), (0,)), ((), ())), preferred_element_type=F32)


def meet(peers):
    barrier = pltpu.get_barrier_semaphore()
    for peer in peers:
        pl.semaphore_signal(barrier, inc=1, device_id=peer, device_id_type=MESH)
    return lambda: pl.semaphore_wait(barrier, len(peers))


def send(source, target, sends, recvs, index, peer):
    one = pltpu.make_async_remote_copy(
        src_ref=source, dst_ref=target, send_sem=sends.at[index], recv_sem=recvs.at[index],
        device_id=peer, device_id_type=MESH)
    one.start()
    return one


def exchange_kernel(box_total, col_count, group, skeleton, points_ref, order_ref, proxy_ref,
                    pivot_ref, points_out, proxy_out, pivot_out, points, order, sends, recvs,
                    local):
    me = lax.axis_index("col")
    place = lax.axis_index("box")
    _, box_count, count = points_ref.shape
    after = {"box": lax.rem(place + 1, box_total)}
    before = {"box": lax.rem(place + box_total - 1, box_total)}
    across = {"col": lax.rem(me + group, col_count)}
    mine = me // group
    own = ((points_ref, points), (order_ref, order), (proxy_ref, proxy_out.at[0]),
           (pivot_ref, pivot_out.at[mine]))
    loads = []
    for i, (source, target) in enumerate(own):
        copy = pltpu.make_async_copy(source, target, local.at[i])
        copy.start()
        loads.append(copy)
    arrived = meet([before, after, across])
    for copy in loads:
        copy.wait()
    width = (count - skeleton) // col_count
    for box in range(box_count):
        row = order[box:box + 1, :]
        strips = [row[:, skeleton + s * width:skeleton + (s + 1) * width]
                  for c in range(group) for s in range(c, col_count, group)]
        row = jnp.concatenate([row[:, 0:skeleton]] + strips, axis=1)
        one_hot = (lax.broadcasted_iota(jnp.int32, (count, count), 0) == row).astype(F32)
        whole = jnp.concatenate([points[axis, box:box + 1, :] for axis in range(3)]
                                + [jnp.zeros((5, count), F32)], axis=0)
        rows = jnp.concatenate(list(three(whole)) + [jnp.zeros_like(whole)], axis=0)
        picked = jnp.dot(rows.astype(BF16), one_hot.astype(BF16), preferred_element_type=F32)
        points_out[1, box] = ((picked[0:8] + picked[8:16]) + picked[16:24])[0:4]
    arrived()
    jobs = [
        send(points_out.at[1], points_out.at[0], sends, recvs, 0, after),
        send(points_out.at[1], points_out.at[2], sends, recvs, 1, before),
        send(proxy_ref, proxy_out.at[1], sends, recvs, 2, across),
        send(pivot_ref, pivot_out.at[mine], sends, recvs, 3, across),
    ]
    for copy in jobs:
        copy.wait()


def tile_kernel(box_total, entries, group, skeleton, nb_ref, place_ref, points_ref, proxy_ref,
                cross_ref, targets, sources, squares, tiles, total):
    count = points_ref.shape[3]
    box_count, _, share = proxy_ref.shape
    proxies = box_count * share
    me = lax.axis_index("col")
    box = me // group
    first = lax.rem(me, group) * entries
    sources[...] = source_rows(centred(padded(points_ref[1, box])))
    for d in range(box_count):
        directions = jnp.concatenate([proxy_ref[d], jnp.zeros((5, share), F32)], axis=0)
        targets[:, d * share:(d + 1) * share] = target_rows((2.0 * proxy_radius) * directions)
    for k in range(entries):
        slot = slot_of(nb_ref, box, first + k, box_count, box_total)
        here = shifted(padded(points_ref[slot // box_count, slot % box_count]),
                       place_ref[box, first + k])
        targets[:, proxies + k * count:proxies + (k + 1) * count] = target_rows(here)
    block = tiles.shape[1] // 2

    def measure(base, slot):
        squares[slot] = dot_tn(targets[:, base:base + block], sources[...])

    def evaluate(slot, i):
        inner = slice(i * ROWS, (i + 1) * ROWS)
        lower = slice(block + i * ROWS, block + (i + 1) * ROWS)
        for c in range(0, count, 256):
            here = slice(c, c + 256)
            there = slice(count + c, count + c + 256)
            real, imag = kernel_values(squares[slot, inner, here])
            real = real.astype(BF16)
            imag = imag.astype(BF16)
            tiles[slot, inner, here] = real
            tiles[slot, inner, there] = imag
            tiles[slot, lower, here] = imag
            tiles[slot, lower, there] = -real

    def gather(slot, left, c):
        here = slice(c, c + 256)
        total[:, here] += plain(left, tiles[slot, :, here])

    def stage(ahead, now, before):
        measure(*ahead)
        steps = block // ROWS
        pieces = 2 * count // 256
        left = None if before is None else jnp.transpose(tiles[before, :, 0:skeleton])
        for i in range(steps):
            if left is not None and i % (steps // pieces) == 0:
                gather(before, left, i // (steps // pieces) * 256)
            evaluate(now, i)

    total[...] = jnp.zeros_like(total)
    blocks = proxies // block
    measure(0, 0)
    for i in range(blocks):
        stage(((i + 1) * block, (i + 1) % 2), i % 2, (i + 1) % 2 if i else None)
    last = blocks + entries * (count // block) - 1
    for i in range(blocks, last + 1):
        stage((min(i + 1, last) * block, (i + 1) % 2), i % 2, (i + 1) % 2)
    end = last % 2
    left = jnp.transpose(tiles[end, :, 0:skeleton])
    for c in range(0, 2 * count, 256):
        gather(end, left, c)
    for p in range(2):
        cross_ref[p] = total[:, p * count:(p + 1) * count]


def lanes(block, k):
    return jnp.take_along_axis(block, jnp.full(block.shape, k, jnp.int32), axis=1)


def across_rows(block, k):
    return jnp.broadcast_to(block[k:k + 1, :], block.shape)


def block_inverse(re, im, start, home):
    count = len(re)
    shape = re[0].shape
    lane = lax.broadcasted_iota(jnp.int32, shape, 1)
    sub = lax.broadcasted_iota(jnp.int32, shape, 0)
    inside = (lane >= start) & (lane < start + 8 * count)
    re = [jnp.where(inside, block, jnp.where(lane - home == sub + 8 * v, 1.0, 0.0))
          for v, block in enumerate(re)]
    im = [jnp.where(inside, block, 0.0) for block in im]
    for r in range(count):
        order = [r] + [v for v in range(count) if v > r] + list(range(r))
        spread = {}
        for v in order:
            for j in range(8):
                k = start + 8 * r + j
                spread[v, j] = (lanes(re[v], k), lanes(im[v], k))
        cols = {j: spread[r, j] for j in range(8)}
        cols["row"] = (re[r], im[r])
        for t in range(0, 8, 2):
            (ar, ai), (cr, ci) = cols.pop(t), cols.pop(t + 1)
            a, d = across_rows(ar, t), across_rows(cr, t + 1)
            br, bi = across_rows(cr, t), across_rows(ci, t)
            scale = 1.0 / (a * d - (br * br + bi * bi))
            a, d, br, bi = a * scale, d * scale, br * scale, bi * scale
            at, on = sub == t, sub == t + 1
            here = at | on
            e0r = jnp.where(at, -d, jnp.where(on, br, ar * d - (cr * br + ci * bi)))
            e0i = jnp.where(at, 0.0, jnp.where(on, -bi, ai * d - (ci * br - cr * bi)))
            e1r = jnp.where(at, br, jnp.where(on, -a, cr * a - (ar * br - ai * bi)))
            e1i = jnp.where(at, bi, jnp.where(on, 0.0, ci * a - (ar * bi + ai * br)))
            for key, (xr, xi) in cols.items():
                x0r, x0i = across_rows(xr, t), across_rows(xi, t)
                x1r, x1i = across_rows(xr, t + 1), across_rows(xi, t + 1)
                lessr = (e0r * x0r - e0i * x0i) + (e1r * x1r - e1i * x1i)
                lessi = (e0r * x0i + e0i * x0r) + (e1r * x1i + e1i * x1r)
                cols[key] = (jnp.where(here, 0.0, xr) - lessr, jnp.where(here, 0.0, xi) - lessi)
            if t < 6:
                yield None
        re[r], im[r] = cols["row"]
        rows = [(across_rows(re[r], j), across_rows(im[r], j)) for j in range(8)]
        for v in order[1:]:
            lessr = [spread[v, j][0] * rows[j][0] - spread[v, j][1] * rows[j][1]
                     for j in range(8)]
            lessi = [spread[v, j][0] * rows[j][1] + spread[v, j][1] * rows[j][0]
                     for j in range(8)]
            re[v] = re[v] - summed(lessr)
            im[v] = im[v] - summed(lessi)
        yield jnp.concatenate(re, axis=0), jnp.concatenate(im, axis=0)


def summed(terms):
    while len(terms) > 1:
        terms = [terms[i] + terms[i + 1] for i in range(0, len(terms), 2)]
    return terms[0]


def plain(a, b):
    return jnp.dot(a, b, preferred_element_type=F32)


def solve_kernel(group, cross_ref, cross_in, x_ref, mat, head, tail):
    width, n = x_ref.shape[1:]
    nb = NBLK
    side = lax.rem(lax.axis_index("col"), group)
    diagonal = lax.broadcasted_iota(jnp.int32, (128, 128), 0) == lax.broadcasted_iota(
        jnp.int32, (128, 128), 1
    )
    gram = cross_ref[:, :, 0:n] + cross_in[:, :, 0:n]
    ridge = 0.0
    for c in range(0, n, 128):
        ridge = ridge + jnp.where(diagonal, gram[0, c:c + 128, c:c + 128], 0.0)
    ridge = ridge_share * jnp.sum(ridge) / n
    mat[:, :, 0:n] = gram
    for c in range(0, n, 128):
        here = slice(c, c + 128)
        mat[0, here, here] = gram[0, here, here] + jnp.where(diagonal, ridge, 0.0)
    mine = pl.ds(pl.multiple_of(n + side * width, 128), width)
    mat[:, :, n:] = cross_ref[:, :, mine] + cross_in[:, :, mine]
    head[...] = jnp.zeros_like(head)
    tail[...] = jnp.zeros_like(tail)

    def pick(block):
        return [block[8 * v:8 * v + 8] for v in range(nb // 8)]

    def put(ref, at, w, re, im):
        where = slice(256 * w, 256 * w + 256)
        for base, block in ((at, [re, im]), (128 + at, [-im, re])):
            high, rest = split(jnp.concatenate(block, axis=1))
            ref[0, base:base + nb, where] = high
            ref[1, base:base + nb, where] = rest

    def clear(ref, at):
        for base in (at, 128 + at):
            ref[:, base:base + nb, :] = jnp.zeros((2, nb, ref.shape[2]), BF16)

    def doubled(re, im):
        return jnp.concatenate(split(jnp.concatenate([re, im], axis=1)), axis=0)

    def product(left, ref, w):
        where = slice(256 * w, 256 * w + 256)
        half = left.shape[0] // 2
        both = plain(left, ref[0, :, where])
        return both[0:half] + (both[half:] + plain(left[0:half], ref[1, :, where]))

    for step in block_inverse(pick(mat[0, 0:nb, 0:128]), pick(mat[1, 0:nb, 0:128]), 0, nb):
        found = step or None
    for j in range(n // nb):
        rows = slice(j * nb, (j + 1) * nb)
        after = slice((j + 1) * nb, (j + 2) * nb)
        q = (j * nb) // 128 * 128
        at = j * nb - q
        home = (at + nb) % 128
        windows = list(range((j + 1) * nb // 128, mat.shape[2] // 128))
        factor = doubled(*found)
        left = doubled(mat[0, :, q:q + 128], mat[1, :, q:q + 128])
        held = {}

        def solve(w):
            here = slice(128 * w, 128 * w + 128)
            put(head, home, w, mat[0, rows, here], mat[1, rows, here])
            held[w] = product(factor, head, w)
            put(tail, at, w, held[w][:, 0:128], held[w][:, 128:])

        def change(w):
            here = slice(128 * w, 128 * w + 128)
            less = product(left, tail, w)
            mat[0, :, here] = mat[0, :, here] - less[:, 0:128]
            mat[1, :, here] = mat[1, :, here] - less[:, 128:]
            mat[0, rows, here] = held[w][:, 0:128]
            mat[1, rows, here] = held[w][:, 128:]

        first = windows[0]
        solve(first)
        pivots = iter(())
        if (j + 1) * nb < n:
            here = slice(128 * first, 128 * first + 128)
            ahead = jnp.concatenate([left[after], left[n + (j + 1) * nb:n + (j + 2) * nb]], axis=0)
            less = product(ahead, tail, first)
            to = (j + 1) * nb % 128
            pivots = block_inverse(pick(mat[0, after, here] - less[:, 0:128]),
                                   pick(mat[1, after, here] - less[:, 128:]),
                                   to, (to + nb) % 128)
        tasks = [functools.partial(solve, w) for w in windows[1:]]
        tasks += [functools.partial(change, w) for w in windows]
        tasks.append(functools.partial(clear, head, home))
        tasks.append(functools.partial(clear, tail, at))
        steps = nb // 2
        done = 0
        for i, task in enumerate(tasks):
            task()
            upto = (i + 1) * steps // len(tasks)
            for _ in range(upto - done):
                found = next(pivots, None) or found
            done = upto
        for step in pivots:
            found = step or found
    for p in range(2):
        x_ref[p] = jnp.transpose(mat[p, :, n:])


def split(x):
    high = x.astype(BF16)
    return high, (x - high.astype(F32)).astype(BF16)


def left_side(xr, xi):
    return jnp.concatenate(split(jnp.concatenate(
        [jnp.concatenate([xr, -xi], axis=1), jnp.concatenate([xi, xr], axis=1)], axis=0)), axis=0)


def pivot_columns(pivot_ref, box):
    pieces = range(pivot_ref.shape[0])
    rows = [jnp.concatenate([pivot_ref[c, box, p:p + 1, :] for c in pieces], axis=1)
            for p in range(2)]
    return [jnp.transpose(jnp.broadcast_to(row, (128, row.shape[1]))) for row in rows]


def quarters(product):
    rows, cols = product.shape[0] // 2, product.shape[1] // 2
    return ((product[:rows, :cols] + product[:rows, cols:])
            + (product[rows:, :cols] + product[rows:, cols:]))


def form(turned, right, rest, blocks, pair):
    half = turned.shape[0] // 2
    both = plain(turned[...], right[0])
    blocks[pair] = rest - (both[0:half] + (both[half:] + plain(turned[0:half, :], right[1])))


def fold(blocks, pair, i, row, pivots, out_ref, to):
    qr, qi = pivots
    width = qr.shape[0]
    n = blocks.shape[2] // 2
    mine = blocks[pair, :, pl.ds(pl.multiple_of(i * n + row, 128), qr.shape[1])]
    br, bi = mine[0:width], mine[width:]
    wr = jnp.transpose(br * qr - bi * qi)
    wi = jnp.transpose(br * qi + bi * qr)
    upper = jnp.concatenate([jnp.concatenate([wr, -wi], axis=1),
                             jnp.concatenate([wi, wr], axis=1)], axis=0)
    whole = jnp.concatenate(split(blocks[pair, :, i * n:(i + 1) * n]), axis=1)
    update = quarters(plain(jnp.concatenate(split(upper), axis=0), whole))
    half = update.shape[0] // 2
    out_ref[to, 0] = out_ref[to, 0] - update[0:half]
    out_ref[to, 1] = out_ref[to, 1] - update[half:]


def first_row(group, count):
    return lax.axis_index("col") // group * count


def entry_squares(box_total, nb_ref, place_ref, points_ref, which, k, n, sources):
    box_count = points_ref.shape[1]
    place = slot_of(nb_ref, which, k, box_count, box_total)
    here = shifted(padded(points_ref[place // box_count, place % box_count]),
                   place_ref[which, k])
    return dot_tn(sources[...], target_rows(here[:, 0:n]))


def evaluate(squares, n, width, right_at, rest_at, i, part=0, parts=1):
    rows = n + width
    for r in range(part * rows // parts, (part + 1) * rows // parts, ROWS):
        for c in range(0, n, 128):
            here = slice(i * n + c, i * n + c + 128)
            for p, value in enumerate(kernel_values(squares[r:r + ROWS, c:c + 128])):
                if r < n:
                    at = slice(p * n + r, p * n + r + ROWS)
                    right_at[0, at, here], right_at[1, at, here] = split(value)
                else:
                    rest_at[p * width + r - n:p * width + r - n + ROWS, here] = value


def half_sources(points, side, group, n, width):
    whole = source_rows(centred(padded(points)))
    half = whole[:, n:n + width]
    for c in range(1, group):
        half = jnp.where(side == c, whole[:, n + c * width:n + (c + 1) * width], half)
    return jnp.concatenate([whole[:, 0:n], half], axis=1)


def kernel_kernel(box_total, group, nb_ref, place_ref, points_ref, right_ref, rest_ref, sources,
                  squares):
    pairs, width, n = rest_ref.shape
    width, n = width // 2, n // 2
    me = lax.axis_index("col")
    fed = 1 - me // group
    sources[...] = half_sources(points_ref[1, fed], lax.rem(me, group), group, n, width)

    def measure(k, slot):
        squares[slot] = entry_squares(box_total, nb_ref, place_ref, points_ref, fed, k, n, sources)

    measure(0, 0)
    for k in range(2 * pairs):
        if k + 1 < 2 * pairs:
            measure(k + 1, (k + 1) % 2)
        evaluate(squares.at[k % 2], n, width, right_ref.at[k // 2], rest_ref.at[k // 2], k % 2)


def near_kernel(box_total, group, nb_ref, place_ref, points_ref, x_ref, pivot_ref,
                out_ref, right_ref, rest_ref, sources, squares, right, rest, turned, blocks):
    width, n = x_ref.shape[1:]
    box_count = points_ref.shape[1]
    entries = nb_ref.shape[1]
    me = lax.axis_index("col")
    box = me // group
    for i, which in enumerate((box, 1 - box)):
        sources[i] = half_sources(points_ref[1, which], lax.rem(me, group), group, n, width)

    def measure(k):
        if k < entries + 2:
            other = k >= entries
            squares[k % 4] = entry_squares(box_total, nb_ref, place_ref, points_ref,
                                           1 - box if other else box, k - 2 if other else k, n,
                                           sources.at[int(other)])

    def values(k, part, parts):
        at = k // 2 % 2
        into = (right.at[at], rest.at[at]) if k < entries else (right_ref, rest_ref)
        evaluate(squares.at[k % 4], n, width, *into, k % 2, part, parts)

    for k in range(4):
        measure(k)
    out_ref[...] = jnp.zeros_like(out_ref)
    values(0, 0, 1)
    turned[...] = left_side(x_ref[0], x_ref[1])
    pivots = pivot_columns(pivot_ref, box)
    row = first_row(group, out_ref.shape[2])
    values(1, 0, 1)
    pairs = entries // 2
    for pair in range(pairs + 1):
        if pair < pairs:
            form(turned, right.at[pair % 2], rest[pair % 2], blocks, pair)
        for i in range(2):
            k = 2 * pair + 2 + i
            if k < entries + 2:
                values(k, 0, 2)
            if pair:
                done = 2 * pair - 2 + i
                fold(blocks, pair - 1, i, row, pivots, out_ref,
                     slot_of(nb_ref, box, done, box_count, box_total))
            if k < entries + 2:
                values(k, 1, 2)
            measure(k + 2)


def far_kernel(box_total, group, nb_ref, buf_ref, right_ref, rest_ref, right_last, rest_last,
               x_ref, mine_ref, pivot_ref, out_ref, inter_ref, turned, blocks):
    pairs = rest_ref.shape[0] + 1
    me = lax.axis_index("col")
    box = me // group
    fed = 1 - box
    box_count = pivot_ref.shape[1]
    strip = inter_ref.shape[2]
    turned[...] = left_side(x_ref[0], x_ref[1])
    pivots = pivot_columns(pivot_ref, fed)
    row = first_row(group, out_ref.shape[2])
    for pair in range(pairs + 1):
        if pair < pairs - 1:
            form(turned, right_ref.at[pair], rest_ref[pair], blocks, pair)
        elif pair < pairs:
            form(turned, right_last, rest_last[...], blocks, pair)
        if not pair:
            out_ref[...] = buf_ref[...]
        for i in range(2):
            if pair:
                fold(blocks, pair - 1, i, row, pivots, out_ref,
                     slot_of(nb_ref, fed, 2 * pair - 2 + i, box_count, box_total))
    for p in range(2):
        for ref, where in ((mine_ref, box), (x_ref, fed)):
            inter_ref[where, p] = ref[p, pl.ds(pl.multiple_of(box * strip, strip), strip), :]


def reduce_kernel(box_total, buf_ref, out_ref, pair_in, line_out, line_in, side_out, side_in,
                  last_in, held, sends, recvs):
    me = lax.axis_index("col")
    place = lax.axis_index("box")
    side = lax.rem(me, 2)
    odd = lax.rem(place, 2)
    near = {"col": me + 1 - 2 * side}
    relay = {"box": lax.rem(place + box_total + 4 * odd - 2, box_total)}
    source = {"box": lax.rem(place + box_total + 2 - 4 * odd, box_total)}
    twin = {"box": place + 1 - 2 * odd}
    meet([near, relay, source, twin])()
    box_count, _, strip, _ = out_ref.shape
    order = (2 * odd, 2 - 2 * odd, 1)
    piece = strip // PIECES
    chunks = [(d, p, pl.ds(i * piece, piece)) for d in range(box_count) for p in range(2)
              for i in range(PIECES)]
    late, early = chunks[:-EARLY], chunks[-EARLY:]
    count = iter(range(sends.shape[0]))

    def pair(g, parts):
        return [send(buf_ref.at[(order[g] * box_count + part[0], part[1], 1 - side) + part[2:]],
                     pair_in.at[(g,) + part], sends, recvs, next(count), near) for part in parts]

    def both(g, part):
        return (buf_ref[(order[g] * box_count + part[0], part[1], side) + part[2:]]
                + pair_in[(g,) + part])

    def forward(source_ref, target_ref, part, peer):
        return send(source_ref.at[part], target_ref.at[part], sends, recvs, next(count), peer)

    line_pairs, line_early = pair(0, late), pair(0, early)
    side_early, side_pairs = pair(1, early), pair(1, late)
    own_pairs = pair(2, chunks)
    lines, sides, turns, directs, onward = [], [], [], [], []
    for part, copy in zip(late, line_pairs):
        copy.wait()
        line_out[part] = both(0, part)
        lines.append(forward(line_out, line_in, part, relay))
    for part, copy, other in zip(early, line_early, side_early):
        copy.wait()
        line_out[part] = both(0, part)
        turns.append(forward(line_out, line_in, part, twin))
        other.wait()
        side_out[part] = both(1, part)
        directs.append(forward(side_out, side_in, part, twin))
    for part, copy in zip(late, side_pairs):
        copy.wait()
        held[part] = both(1, part)
    for i, (part, copy) in enumerate(zip(late, lines)):
        copy.wait()
        side_out[part] = held[part] + line_in[part]
        sides.append(forward(side_out, side_in, part, twin))
        if i == 3:
            for some, turn in zip(early, turns):
                turn.wait()
                onward.append(forward(line_in, last_in, some, source))
    for part, copy in zip(chunks, own_pairs):
        copy.wait()
        held[part] = both(2, part)
    for part, direct, copy in zip(early, directs, onward):
        direct.wait()
        copy.wait()
        out_ref[part] = (held[part] + side_in[part]) + last_in[part]
    for part, copy in zip(late, sides):
        copy.wait()
        out_ref[part] = held[part] + side_in[part]


def ring(count, step):
    return [(i, (i + step) % count) for i in range(count)]


def on_device(
    box_points, proxy_directions, point_order, neighbour_boxes, neighbour_places, pivot_inverse
):
    box_count, _, point_count = box_points.shape
    col_count = lax.axis_size("col")
    box_total = lax.axis_size("box")
    group = col_count // box_count
    listed = neighbour_boxes.shape[1]
    entries = listed // group
    width = pivot_inverse.shape[2]
    rest = width * col_count
    skeleton = point_count - rest
    half = rest // group
    share = proxy_directions.shape[1]
    dma = pltpu.SemaphoreType.DMA

    points, proxies, pivots = pl.pallas_call(
        functools.partial(exchange_kernel, box_total, col_count, group, skeleton),
        out_shape=(
            jax.ShapeDtypeStruct((3, box_count, 4, point_count), F32),
            jax.ShapeDtypeStruct((box_count,) + proxy_directions.shape, F32),
            jax.ShapeDtypeStruct((box_count,) + pivot_inverse.shape, F32),
        ),
        in_specs=[HBM] * 4,
        out_specs=(VMEM,) * 3,
        scratch_shapes=[pltpu.VMEM((3, box_count, point_count), F32),
                        pltpu.VMEM(point_order.shape, jnp.int32),
                        dma((4,)), dma((4,)), dma((4,))],
        compiler_params=params(collective_id=0, has_side_effects=True),
        cost_estimate=pl.CostEstimate(flops=4 * 10**9, bytes_accessed=16 * 10**6,
                                      transcendentals=0),
    )(*(pltpu.with_memory_space_constraint(one, pltpu.HBM) for one in (
        jnp.transpose(box_points, (1, 0, 2)), point_order, proxy_directions, pivot_inverse)))

    rows = box_count * share + entries * point_count
    cross = pl.pallas_call(
        functools.partial(tile_kernel, box_total, entries, group, skeleton),
        out_shape=jax.ShapeDtypeStruct((2, skeleton, point_count), F32),
        in_specs=[SMEM, SMEM, VMEM, VMEM],
        out_specs=VMEM,
        scratch_shapes=[
            pltpu.VMEM((DEPTH, rows), BF16),
            pltpu.VMEM((DEPTH, point_count), BF16),
            pltpu.VMEM((2, BLOCK, point_count), F32),
            pltpu.VMEM((2, 2 * BLOCK, 2 * point_count), BF16),
            pltpu.VMEM((skeleton, 2 * point_count), F32),
        ],
        compiler_params=params(),
    )(neighbour_boxes, neighbour_places, points, proxies)
    pairs = [(i, i + 1 - 2 * (i % 2)) for i in range(col_count)]
    cross_in = lax.ppermute(cross, "col", pairs)

    cover = pl.CostEstimate(flops=8 * 10**9, bytes_accessed=16 * 10**6, transcendentals=0)
    right, kept = pl.pallas_call(
        functools.partial(kernel_kernel, box_total, group),
        out_shape=(
            jax.ShapeDtypeStruct((listed // 2 - 1, 2, 2 * skeleton, 2 * skeleton), BF16),
            jax.ShapeDtypeStruct((listed // 2 - 1, 2 * half, 2 * skeleton), F32),
        ),
        in_specs=[SMEM, SMEM, VMEM],
        out_specs=(VMEM, VMEM),
        scratch_shapes=[
            pltpu.VMEM((DEPTH, skeleton + half), BF16),
            pltpu.VMEM((2, skeleton + half, skeleton), F32),
        ],
        compiler_params=params(),
        cost_estimate=cover,
    )(neighbour_boxes, neighbour_places, points)

    solved = pl.pallas_call(
        functools.partial(solve_kernel, group),
        out_shape=jax.ShapeDtypeStruct((2, half, skeleton), F32),
        in_specs=[VMEM] * 2,
        out_specs=VMEM,
        scratch_shapes=[
            pltpu.VMEM((2, skeleton, skeleton + half), F32),
            pltpu.VMEM((2, 256, 2 * (skeleton + half)), BF16),
            pltpu.VMEM((2, 256, 2 * (skeleton + half)), BF16),
        ],
        compiler_params=params(),
    )(cross, cross_in)
    arrived = lax.ppermute(solved, "col", ring(col_count, group))

    strips = skeleton // box_count
    buffer, right_last, kept_last = pl.pallas_call(
        functools.partial(near_kernel, box_total, group),
        out_shape=(
            jax.ShapeDtypeStruct((3 * box_count, 2, strips, skeleton), F32),
            jax.ShapeDtypeStruct((2, 2 * skeleton, 2 * skeleton), BF16),
            jax.ShapeDtypeStruct((2 * half, 2 * skeleton), F32),
        ),
        in_specs=[SMEM, SMEM, VMEM, VMEM, VMEM],
        out_specs=(VMEM,) * 3,
        scratch_shapes=[
            pltpu.VMEM((box_count, DEPTH, skeleton + half), BF16),
            pltpu.VMEM((4, skeleton + half, skeleton), F32),
            pltpu.VMEM((2, 2, 2 * skeleton, 2 * skeleton), BF16),
            pltpu.VMEM((2, 2 * half, 2 * skeleton), F32),
            pltpu.VMEM((4 * half, 2 * skeleton), BF16),
            pltpu.VMEM((listed // 2, 2 * half, 2 * skeleton), F32),
        ],
        compiler_params=params(),
        cost_estimate=cover,
    )(neighbour_boxes, neighbour_places, points, solved, pivots)

    buffer, inter = pl.pallas_call(
        functools.partial(far_kernel, box_total, group),
        out_shape=(
            jax.ShapeDtypeStruct(buffer.shape, F32),
            jax.ShapeDtypeStruct((box_count, 2, width, skeleton), F32),
        ),
        in_specs=[SMEM] + [VMEM] * 8,
        out_specs=(VMEM, VMEM),
        scratch_shapes=[
            pltpu.VMEM((4 * half, 2 * skeleton), BF16),
            pltpu.VMEM((listed // 2, 2 * half, 2 * skeleton), F32),
        ],
        compiler_params=params(),
    )(neighbour_boxes, buffer, right, kept, right_last, kept_last, arrived, solved, pivots)
    interpolation = jnp.swapaxes(inter, 2, 3)

    strip = skeleton // col_count
    block = (box_count, 2, strip, skeleton)
    jobs = 5 * PIECES * 2 * box_count + EARLY
    skeleton_update = pl.pallas_call(
        functools.partial(reduce_kernel, box_total),
        out_shape=jax.ShapeDtypeStruct(block, F32),
        in_specs=[VMEM],
        out_specs=VMEM,
        scratch_shapes=[
            pltpu.VMEM((3,) + block, F32),
            pltpu.VMEM(block, F32),
            pltpu.VMEM(block, F32),
            pltpu.VMEM(block, F32),
            pltpu.VMEM(block, F32),
            pltpu.VMEM(block, F32),
            pltpu.VMEM(block, F32),
            dma((jobs,)),
            dma((jobs,)),
        ],
        compiler_params=params(collective_id=1, has_side_effects=True),
    )(buffer.reshape(3 * box_count, 2, group, strip, skeleton))
    return (interpolation, skeleton_update)


def solution(mesh):
    placed = (
        P("box", None, None),
        P(None, "col"),
        P("box", None),
        P("box", None),
        P("box", None),
        P("box", None, "col"),
    )
    return jax.shard_map(
        on_device,
        mesh=mesh,
        in_specs=placed,
        out_specs=(P("box", None, None, "col"), P("box", None, "col", None)),
        check_vma=False,
    )
```

```python
import functools
import math

import jax
import jax.numpy as jnp
from jax import lax
from jax.experimental import pallas as pl
from jax.experimental.pallas import tpu as pltpu
from jax.sharding import PartitionSpec as P

softening = 0.05
proxy_radius = 1.5
ridge_share = 0.05
NBLK = 32
BLOCK = 256
ROWS = 16
DEPTH = 64
PIECES = 2

SIN = (4.44287959, -7.30781805, 3.59778873, -0.79123822)
COS = (1.41420408, -6.97764206, 5.7152384, -1.72834866)

HBM = pl.BlockSpec(memory_space=pltpu.HBM)
VMEM = pl.BlockSpec(memory_space=pltpu.VMEM)
SMEM = pl.BlockSpec(memory_space=pltpu.SMEM)
MESH = pl.DeviceIdType.MESH
F32 = jnp.float32
BF16 = jnp.bfloat16


def params(**more):
    return pltpu.CompilerParams(vmem_limit_bytes=24 * 1024 * 1024, **more)


def horner(coefficients, z):
    total = coefficients[-1] * z + coefficients[-2]
    for one in coefficients[-3::-1]:
        total = total * z + one
    return total


def kernel_values(square):
    inverse = lax.rsqrt(square)
    turns = square * inverse
    part = turns - jnp.floor(turns + 0.5)
    z = part * part
    amplitude = inverse * (1.0 / (2.0 * math.pi))
    sine = part * horner(SIN, z)
    scaled = amplitude * sine
    return amplitude - scaled * sine, scaled * horner(COS, z)


def three(x):
    high = x.astype(BF16).astype(F32)
    rest = x - high
    mid = rest.astype(BF16).astype(F32)
    return high, mid, rest - mid


def row_three(block, row):
    third = lax.broadcasted_iota(jnp.int32, block.shape, 0) == 3
    return jnp.where(third, row, block)


def norm_of(points):
    return jnp.sum(points * points, axis=0, keepdims=True)


def stacked(groups):
    zero = jnp.zeros_like(groups[0])
    return jnp.concatenate(groups + [zero] * (DEPTH // 8 - len(groups)), axis=0).astype(BF16)


def target_rows(points):
    high, mid, low = three(points)
    n_high, n_mid, n_low = three(norm_of(points))
    return stacked([row_three(high, n_high), row_three(high, n_mid), row_three(mid, n_low),
                    row_three(high, 1.0), row_three(mid, 1.0), row_three(low, 1.0)])


def source_rows(points):
    high, mid, low = three(points)
    norm = norm_of(points) + 4.0 * softening * softening
    n_high, n_mid, n_low = three(norm)
    return stacked([row_three(-2.0 * high, 1.0), row_three(-2.0 * mid, 1.0),
                    row_three(-2.0 * high, 1.0), row_three(-2.0 * low, n_high),
                    row_three(-2.0 * mid, n_mid), row_three(-2.0 * high, n_low)])


def padded(points):
    return jnp.concatenate([points, jnp.zeros_like(points)], axis=0)


def three_rows(points):
    rows = lax.broadcasted_iota(jnp.int32, points.shape, 0)
    return jnp.where(rows < 3, points, 0.0)


def shifted(points, code):
    code = jnp.where(code >= 13, code + 1, code)
    axis_row = lax.broadcasted_iota(jnp.int32, points.shape, 0)
    move = jnp.where(
        axis_row == 0,
        (code // 9 - 1).astype(F32),
        jnp.where(axis_row == 1, ((code // 3) % 3 - 1).astype(F32), (code % 3 - 1).astype(F32)),
    )
    return three_rows(2.0 * (points + (move - 0.5)))


def centred(points):
    return three_rows(2.0 * (points - 0.5))


def slot_of(nb_ref, row, entry, box_count, box_total):
    owner_box = nb_ref[row, entry]
    step = owner_box // box_count - lax.axis_index("box") + 1
    step = jnp.where(step < 0, step + box_total, step)
    step = jnp.where(step >= box_total, step - box_total, step)
    return step * box_count + owner_box % box_count


def dot_tn(a, b):
    return lax.dot_general(a, b, (((0,), (0,)), ((), ())), preferred_element_type=F32)


def meet(peers):
    barrier = pltpu.get_barrier_semaphore()
    for peer in peers:
        pl.semaphore_signal(barrier, inc=1, device_id=peer, device_id_type=MESH)
    return lambda: pl.semaphore_wait(barrier, len(peers))


def send(source, target, sends, recvs, index, peer):
    one = pltpu.make_async_remote_copy(
        src_ref=source, dst_ref=target, send_sem=sends.at[index], recv_sem=recvs.at[index],
        device_id=peer, device_id_type=MESH)
    one.start()
    return one


def exchange_kernel(box_total, col_count, group, skeleton, points_ref, order_ref, proxy_ref,
                    pivot_ref, points_out, proxy_out, pivot_out, points, order, sends, recvs,
                    local):
    me = lax.axis_index("col")
    place = lax.axis_index("box")
    _, box_count, count = points_ref.shape
    after = {"box": lax.rem(place + 1, box_total)}
    before = {"box": lax.rem(place + box_total - 1, box_total)}
    across = {"col": lax.rem(me + group, col_count)}
    mine = me // group
    own = ((points_ref, points), (order_ref, order), (proxy_ref, proxy_out.at[0]),
           (pivot_ref, pivot_out.at[mine]))
    loads = []
    for i, (source, target) in enumerate(own):
        copy = pltpu.make_async_copy(source, target, local.at[i])
        copy.start()
        loads.append(copy)
    arrived = meet([before, after, across])
    for copy in loads:
        copy.wait()
    width = (count - skeleton) // col_count
    for box in range(box_count):
        row = order[box:box + 1, :]
        strips = [row[:, skeleton + s * width:skeleton + (s + 1) * width]
                  for c in range(group) for s in range(c, col_count, group)]
        row = jnp.concatenate([row[:, 0:skeleton]] + strips, axis=1)
        one_hot = (lax.broadcasted_iota(jnp.int32, (count, count), 0) == row).astype(F32)
        whole = jnp.concatenate([points[axis, box:box + 1, :] for axis in range(3)]
                                + [jnp.zeros((5, count), F32)], axis=0)
        rows = jnp.concatenate(list(three(whole)) + [jnp.zeros_like(whole)], axis=0)
        picked = jnp.dot(rows.astype(BF16), one_hot.astype(BF16), preferred_element_type=F32)
        points_out[1, box] = ((picked[0:8] + picked[8:16]) + picked[16:24])[0:4]
    arrived()
    jobs = [
        send(points_out.at[1], points_out.at[0], sends, recvs, 0, after),
        send(points_out.at[1], points_out.at[2], sends, recvs, 1, before),
        send(proxy_ref, proxy_out.at[1], sends, recvs, 2, across),
        send(pivot_ref, pivot_out.at[mine], sends, recvs, 3, across),
    ]
    for copy in jobs:
        copy.wait()


def tile_kernel(box_total, entries, group, skeleton, nb_ref, place_ref, points_ref, proxy_ref,
                cross_ref, targets, sources, squares, tiles, total):
    count = points_ref.shape[3]
    box_count, _, share = proxy_ref.shape
    proxies = box_count * share
    me = lax.axis_index("col")
    box = me // group
    first = lax.rem(me, group) * entries
    sources[...] = source_rows(centred(padded(points_ref[1, box])))
    for d in range(box_count):
        directions = jnp.concatenate([proxy_ref[d], jnp.zeros((5, share), F32)], axis=0)
        targets[:, d * share:(d + 1) * share] = target_rows((2.0 * proxy_radius) * directions)
    for k in range(entries):
        slot = slot_of(nb_ref, box, first + k, box_count, box_total)
        here = shifted(padded(points_ref[slot // box_count, slot % box_count]),
                       place_ref[box, first + k])
        targets[:, proxies + k * count:proxies + (k + 1) * count] = target_rows(here)
    block = tiles.shape[1] // 2

    def measure(base, slot):
        squares[slot] = dot_tn(targets[:, base:base + block], sources[...])

    def evaluate(slot, i):
        inner = slice(i * ROWS, (i + 1) * ROWS)
        lower = slice(block + i * ROWS, block + (i + 1) * ROWS)
        for c in range(0, count, 256):
            here = slice(c, c + 256)
            there = slice(count + c, count + c + 256)
            real, imag = kernel_values(squares[slot, inner, here])
            real = real.astype(BF16)
            imag = imag.astype(BF16)
            tiles[slot, inner, here] = real
            tiles[slot, inner, there] = imag
            tiles[slot, lower, here] = imag
            tiles[slot, lower, there] = -real

    def gather(slot, left, c):
        here = slice(c, c + 256)
        total[:, here] += plain(left, tiles[slot, :, here])

    def stage(ahead, now, before):
        measure(*ahead)
        steps = block // ROWS
        pieces = 2 * count // 256
        left = None if before is None else jnp.transpose(tiles[before, :, 0:skeleton])
        for i in range(steps):
            if left is not None and i % (steps // pieces) == 0:
                gather(before, left, i // (steps // pieces) * 256)
            evaluate(now, i)

    total[...] = jnp.zeros_like(total)
    blocks = proxies // block
    measure(0, 0)
    for i in range(blocks):
        stage(((i + 1) * block, (i + 1) % 2), i % 2, (i + 1) % 2 if i else None)
    last = blocks + entries * (count // block) - 1
    for i in range(blocks, last + 1):
        stage((min(i + 1, last) * block, (i + 1) % 2), i % 2, (i + 1) % 2)
    end = last % 2
    left = jnp.transpose(tiles[end, :, 0:skeleton])
    for c in range(0, 2 * count, 256):
        gather(end, left, c)
    for p in range(2):
        cross_ref[p] = total[:, p * count:(p + 1) * count]


def lanes(block, k):
    return jnp.take_along_axis(block, jnp.full(block.shape, k, jnp.int32), axis=1)


def across_rows(block, k):
    return jnp.broadcast_to(block[k:k + 1, :], block.shape)


def block_inverse(re, im, start, home):
    count = len(re)
    shape = re[0].shape
    lane = lax.broadcasted_iota(jnp.int32, shape, 1)
    sub = lax.broadcasted_iota(jnp.int32, shape, 0)
    inside = (lane >= start) & (lane < start + 8 * count)
    re = [jnp.where(inside, block, jnp.where(lane - home == sub + 8 * v, 1.0, 0.0))
          for v, block in enumerate(re)]
    im = [jnp.where(inside, block, 0.0) for block in im]
    for r in range(count):
        order = [r] + [v for v in range(count) if v > r] + list(range(r))
        spread = {}
        for v in order:
            for j in range(8):
                k = start + 8 * r + j
                spread[v, j] = (lanes(re[v], k), lanes(im[v], k))
        cols = {j: spread[r, j] for j in range(8)}
        cols["row"] = (re[r], im[r])
        for t in range(0, 8, 2):
            (ar, ai), (cr, ci) = cols.pop(t), cols.pop(t + 1)
            a, d = across_rows(ar, t), across_rows(cr, t + 1)
            br, bi = across_rows(cr, t), across_rows(ci, t)
            scale = 1.0 / (a * d - (br * br + bi * bi))
            a, d, br, bi = a * scale, d * scale, br * scale, bi * scale
            at, on = sub == t, sub == t + 1
            here = at | on
            e0r = jnp.where(at, -d, jnp.where(on, br, ar * d - (cr * br + ci * bi)))
            e0i = jnp.where(at, 0.0, jnp.where(on, -bi, ai * d - (ci * br - cr * bi)))
            e1r = jnp.where(at, br, jnp.where(on, -a, cr * a - (ar * br - ai * bi)))
            e1i = jnp.where(at, bi, jnp.where(on, 0.0, ci * a - (ar * bi + ai * br)))
            for key, (xr, xi) in cols.items():
                x0r, x0i = across_rows(xr, t), across_rows(xi, t)
                x1r, x1i = across_rows(xr, t + 1), across_rows(xi, t + 1)
                lessr = (e0r * x0r - e0i * x0i) + (e1r * x1r - e1i * x1i)
                lessi = (e0r * x0i + e0i * x0r) + (e1r * x1i + e1i * x1r)
                cols[key] = (jnp.where(here, 0.0, xr) - lessr, jnp.where(here, 0.0, xi) - lessi)
            if t < 6:
                yield None
        re[r], im[r] = cols["row"]
        rows = [(across_rows(re[r], j), across_rows(im[r], j)) for j in range(8)]
        for v in order[1:]:
            lessr = [spread[v, j][0] * rows[j][0] - spread[v, j][1] * rows[j][1]
                     for j in range(8)]
            lessi = [spread[v, j][0] * rows[j][1] + spread[v, j][1] * rows[j][0]
                     for j in range(8)]
            re[v] = re[v] - summed(lessr)
            im[v] = im[v] - summed(lessi)
        yield jnp.concatenate(re, axis=0), jnp.concatenate(im, axis=0)


def summed(terms):
    while len(terms) > 1:
        terms = [terms[i] + terms[i + 1] for i in range(0, len(terms), 2)]
    return terms[0]


def plain(a, b):
    return jnp.dot(a, b, preferred_element_type=F32)


def solve_kernel(group, cross_ref, cross_in, x_ref, mat, head, tail):
    n = x_ref.shape[1]
    width = x_ref.shape[2]
    nb = NBLK
    side = lax.rem(lax.axis_index("col"), group)
    diagonal = lax.broadcasted_iota(jnp.int32, (128, 128), 0) == lax.broadcasted_iota(
        jnp.int32, (128, 128), 1
    )
    gram = cross_ref[:, :, 0:n] + cross_in[:, :, 0:n]
    ridge = 0.0
    for c in range(0, n, 128):
        ridge = ridge + jnp.where(diagonal, gram[0, c:c + 128, c:c + 128], 0.0)
    ridge = ridge_share * jnp.sum(ridge) / n
    mat[:, :, 0:n] = gram
    for c in range(0, n, 128):
        here = slice(c, c + 128)
        mat[0, here, here] = gram[0, here, here] + jnp.where(diagonal, ridge, 0.0)
    mine = pl.ds(pl.multiple_of(n + side * width, 128), width)
    mat[:, :, n:] = cross_ref[:, :, mine] + cross_in[:, :, mine]
    head[...] = jnp.zeros_like(head)
    tail[...] = jnp.zeros_like(tail)

    def pick(block):
        return [block[8 * v:8 * v + 8] for v in range(nb // 8)]

    def put(ref, at, w, re, im):
        where = slice(256 * w, 256 * w + 256)
        for base, block in ((at, [re, im]), (128 + at, [-im, re])):
            high, rest = split(jnp.concatenate(block, axis=1))
            ref[0, base:base + nb, where] = high
            ref[1, base:base + nb, where] = rest

    def clear(ref, at):
        for base in (at, 128 + at):
            ref[:, base:base + nb, :] = jnp.zeros((2, nb, ref.shape[2]), BF16)

    def doubled(re, im):
        return jnp.concatenate(split(jnp.concatenate([re, im], axis=1)), axis=0)

    def product(left, ref, w):
        where = slice(256 * w, 256 * w + 256)
        half = left.shape[0] // 2
        both = plain(left, ref[0, :, where])
        return both[0:half] + (both[half:] + plain(left[0:half], ref[1, :, where]))

    for step in block_inverse(pick(mat[0, 0:nb, 0:128]), pick(mat[1, 0:nb, 0:128]), 0, nb):
        found = step or None
    for j in range(n // nb):
        rows = slice(j * nb, (j + 1) * nb)
        after = slice((j + 1) * nb, (j + 2) * nb)
        q = (j * nb) // 128 * 128
        at = j * nb - q
        home = (at + nb) % 128
        windows = list(range((j + 1) * nb // 128, mat.shape[2] // 128))
        factor = doubled(*found)
        left = doubled(mat[0, :, q:q + 128], mat[1, :, q:q + 128])
        held = {}

        def solve(w):
            here = slice(128 * w, 128 * w + 128)
            put(head, home, w, mat[0, rows, here], mat[1, rows, here])
            held[w] = product(factor, head, w)
            put(tail, at, w, held[w][:, 0:128], held[w][:, 128:])

        def change(w):
            here = slice(128 * w, 128 * w + 128)
            less = product(left, tail, w)
            mat[0, :, here] = mat[0, :, here] - less[:, 0:128]
            mat[1, :, here] = mat[1, :, here] - less[:, 128:]
            mat[0, rows, here] = held[w][:, 0:128]
            mat[1, rows, here] = held[w][:, 128:]

        first = windows[0]
        solve(first)
        pivots = iter(())
        if (j + 1) * nb < n:
            here = slice(128 * first, 128 * first + 128)
            ahead = jnp.concatenate([left[after], left[n + (j + 1) * nb:n + (j + 2) * nb]], axis=0)
            less = product(ahead, tail, first)
            to = (j + 1) * nb % 128
            pivots = block_inverse(pick(mat[0, after, here] - less[:, 0:128]),
                                   pick(mat[1, after, here] - less[:, 128:]),
                                   to, (to + nb) % 128)
        tasks = [functools.partial(solve, w) for w in windows[1:]]
        tasks += [functools.partial(change, w) for w in windows]
        tasks.append(functools.partial(clear, head, home))
        tasks.append(functools.partial(clear, tail, at))
        steps = nb // 2
        done = 0
        for i, task in enumerate(tasks):
            task()
            upto = (i + 1) * steps // len(tasks)
            for _ in range(upto - done):
                found = next(pivots, None) or found
            done = upto
        for step in pivots:
            found = step or found
    x_ref[...] = mat[:, :, n:]


def split(x):
    high = x.astype(BF16)
    return high, (x - high.astype(F32)).astype(BF16)


def left_side(xr, xi):
    return jnp.concatenate(split(jnp.concatenate(
        [jnp.concatenate([xr, -xi], axis=1), jnp.concatenate([xi, xr], axis=1)], axis=0)), axis=0)


def pivot_columns(pivot_ref, box):
    pieces = range(pivot_ref.shape[0])
    rows = [jnp.concatenate([pivot_ref[c, box, p:p + 1, :] for c in pieces], axis=1)
            for p in range(2)]
    return [jnp.transpose(jnp.broadcast_to(row, (128, row.shape[1]))) for row in rows]


def quarters(product):
    rows, cols = product.shape[0] // 2, product.shape[1] // 2
    return ((product[:rows, :cols] + product[:rows, cols:])
            + (product[rows:, :cols] + product[rows:, cols:]))


def form(turned, right, rest, blocks, pair):
    half = turned.shape[0] // 2
    both = plain(turned[...], right[0])
    blocks[pair] = rest - (both[0:half] + (both[half:] + plain(turned[0:half, :], right[1])))


def fold(blocks, pair, i, row, pivots, out_ref, to):
    qr, qi = pivots
    width = qr.shape[0]
    n = blocks.shape[2] // 2
    mine = blocks[pair, :, pl.ds(pl.multiple_of(i * n + row, 128), qr.shape[1])]
    br, bi = mine[0:width], mine[width:]
    wr = jnp.transpose(br * qr - bi * qi)
    wi = jnp.transpose(br * qi + bi * qr)
    upper = jnp.concatenate([jnp.concatenate([wr, -wi], axis=1),
                             jnp.concatenate([wi, wr], axis=1)], axis=0)
    whole = jnp.concatenate(split(blocks[pair, :, i * n:(i + 1) * n]), axis=1)
    update = quarters(plain(jnp.concatenate(split(upper), axis=0), whole))
    half = update.shape[0] // 2
    out_ref[to, 0] = out_ref[to, 0] - update[0:half]
    out_ref[to, 1] = out_ref[to, 1] - update[half:]


def first_row(group, count):
    return lax.axis_index("col") // group * count


def entry_squares(box_total, nb_ref, place_ref, points_ref, which, k, n, sources):
    box_count = points_ref.shape[1]
    place = slot_of(nb_ref, which, k, box_count, box_total)
    here = shifted(padded(points_ref[place // box_count, place % box_count]),
                   place_ref[which, k])
    return dot_tn(sources[...], target_rows(here[:, 0:n]))


def evaluate(squares, n, width, right_at, rest_at, i, part=0, parts=1):
    rows = n + width
    for r in range(part * rows // parts, (part + 1) * rows // parts, ROWS):
        for c in range(0, n, 128):
            here = slice(i * n + c, i * n + c + 128)
            for p, value in enumerate(kernel_values(squares[r:r + ROWS, c:c + 128])):
                if r < n:
                    at = slice(p * n + r, p * n + r + ROWS)
                    right_at[0, at, here], right_at[1, at, here] = split(value)
                else:
                    rest_at[p * width + r - n:p * width + r - n + ROWS, here] = value


def half_sources(points, side, group, n, width):
    whole = source_rows(centred(padded(points)))
    half = whole[:, n:n + width]
    for c in range(1, group):
        half = jnp.where(side == c, whole[:, n + c * width:n + (c + 1) * width], half)
    return jnp.concatenate([whole[:, 0:n], half], axis=1)


def kernel_kernel(box_total, group, nb_ref, place_ref, points_ref, right_ref, rest_ref, sources,
                  squares):
    pairs, width, n = rest_ref.shape
    width, n = width // 2, n // 2
    me = lax.axis_index("col")
    fed = 1 - me // group
    sources[...] = half_sources(points_ref[1, fed], lax.rem(me, group), group, n, width)

    def measure(k, slot):
        squares[slot] = entry_squares(box_total, nb_ref, place_ref, points_ref, fed, k, n, sources)

    measure(0, 0)
    for k in range(2 * pairs):
        if k + 1 < 2 * pairs:
            measure(k + 1, (k + 1) % 2)
        evaluate(squares.at[k % 2], n, width, right_ref.at[k // 2], rest_ref.at[k // 2], k % 2)


def near_kernel(box_total, group, nb_ref, place_ref, points_ref, x_ref, pivot_ref,
                out_ref, right_ref, rest_ref, sources, squares, right, rest, turned, blocks):
    n = x_ref.shape[1]
    width = x_ref.shape[2]
    box_count = points_ref.shape[1]
    entries = nb_ref.shape[1]
    me = lax.axis_index("col")
    box = me // group
    for i, which in enumerate((box, 1 - box)):
        sources[i] = half_sources(points_ref[1, which], lax.rem(me, group), group, n, width)

    def measure(k):
        if k < entries + 2:
            other = k >= entries
            squares[k % 4] = entry_squares(box_total, nb_ref, place_ref, points_ref,
                                           1 - box if other else box, k - 2 if other else k, n,
                                           sources.at[int(other)])

    def values(k, part, parts):
        at = k // 2 % 2
        into = (right.at[at], rest.at[at]) if k < entries else (right_ref, rest_ref)
        evaluate(squares.at[k % 4], n, width, *into, k % 2, part, parts)

    for k in range(4):
        measure(k)
    out_ref[...] = jnp.zeros_like(out_ref)
    values(0, 0, 1)
    turned[...] = left_side(jnp.transpose(x_ref[0]), jnp.transpose(x_ref[1]))
    pivots = pivot_columns(pivot_ref, box)
    row = first_row(group, out_ref.shape[2])
    values(1, 0, 1)
    pairs = entries // 2
    for pair in range(pairs + 1):
        if pair < pairs:
            form(turned, right.at[pair % 2], rest[pair % 2], blocks, pair)
        for i in range(2):
            k = 2 * pair + 2 + i
            if k < entries + 2:
                values(k, 0, 2)
            if pair:
                done = 2 * pair - 2 + i
                fold(blocks, pair - 1, i, row, pivots, out_ref,
                     slot_of(nb_ref, box, done, box_count, box_total))
            if k < entries + 2:
                values(k, 1, 2)
            measure(k + 2)


def far_kernel(box_total, group, nb_ref, buf_ref, right_ref, rest_ref, right_last, rest_last,
               x_ref, mine_ref, pivot_ref, out_ref, inter_ref, turned, blocks):
    pairs = rest_ref.shape[0] + 1
    me = lax.axis_index("col")
    box = me // group
    fed = 1 - box
    box_count = pivot_ref.shape[1]
    strip = inter_ref.shape[2]
    theirs = [jnp.transpose(x_ref[p]) for p in range(2)]
    turned[...] = left_side(*theirs)
    pivots = pivot_columns(pivot_ref, fed)
    row = first_row(group, out_ref.shape[2])
    for pair in range(pairs + 1):
        if pair < pairs - 1:
            form(turned, right_ref.at[pair], rest_ref[pair], blocks, pair)
        elif pair < pairs:
            form(turned, right_last, rest_last[...], blocks, pair)
        if not pair:
            out_ref[...] = buf_ref[...]
        for i in range(2):
            if pair:
                fold(blocks, pair - 1, i, row, pivots, out_ref,
                     slot_of(nb_ref, fed, 2 * pair - 2 + i, box_count, box_total))
    for p in range(2):
        for block, where in ((jnp.transpose(mine_ref[p]), box), (theirs[p], fed)):
            piece = block[0:strip]
            for c in range(1, block.shape[0] // strip):
                piece = jnp.where(box == c, block[c * strip:(c + 1) * strip], piece)
            inter_ref[where, p] = piece


def reduce_kernel(box_total, buf_ref, out_ref, pair_in, line_out, line_in, side_out, side_in,
                  last_in, held, sends, recvs):
    me = lax.axis_index("col")
    place = lax.axis_index("box")
    side = lax.rem(me, 2)
    odd = lax.rem(place, 2)
    near = {"col": me + 1 - 2 * side}
    relay = {"box": lax.rem(place + box_total + 4 * odd - 2, box_total)}
    source = {"box": lax.rem(place + box_total + 2 - 4 * odd, box_total)}
    twin = {"box": place + 1 - 2 * odd}
    meet([near, relay, source, twin])()
    box_count, _, strip, _ = out_ref.shape
    order = (2 * odd, 2 - 2 * odd, 1)
    piece = strip // PIECES
    early = (box_count - 1, 1)
    wholes = [(d, p) for d in range(box_count) for p in range(2) if (d, p) != early]
    late = [part + (pl.ds(i * piece, piece),) for part in wholes for i in range(PIECES)]
    count = iter(range(sends.shape[0]))

    def pair(g, part):
        return send(buf_ref.at[(order[g] * box_count + part[0], part[1], 1 - side) + part[2:]],
                    pair_in.at[(g,) + part], sends, recvs, next(count), near)

    def both(g, part):
        return (buf_ref[(order[g] * box_count + part[0], part[1], side) + part[2:]]
                + pair_in[(g,) + part])

    def forward(source_ref, target_ref, part, peer):
        return send(source_ref.at[part], target_ref.at[part], sends, recvs, next(count), peer)

    line_pairs = [pair(0, part) for part in late]
    line_early, side_early = pair(0, early), pair(1, early)
    side_pairs = [pair(1, part) for part in wholes]
    own_pair = send(buf_ref.at[box_count:2 * box_count, :, 1 - side], pair_in.at[2], sends, recvs,
                    next(count), near)
    lines, sides = [], []
    for part, copy in zip(late, line_pairs):
        copy.wait()
        line_out[part] = both(0, part)
        lines.append(forward(line_out, line_in, part, relay))
    line_early.wait()
    line_out[early] = both(0, early)
    turn = forward(line_out, line_in, early, twin)
    side_early.wait()
    side_out[early] = both(1, early)
    direct = forward(side_out, side_in, early, twin)
    for part, copy in zip(wholes, side_pairs):
        copy.wait()
        held[part] = both(1, part)
    for i, (part, copy) in enumerate(zip(late, lines)):
        copy.wait()
        side_out[part] = held[part] + line_in[part]
        sides.append(forward(side_out, side_in, part, twin))
        if i == 1:
            turn.wait()
            onward = forward(line_in, last_in, early, source)
    own_pair.wait()
    for d in range(box_count):
        for p in range(2):
            held[d, p] = both(2, (d, p))
    direct.wait()
    onward.wait()
    out_ref[early] = (held[early] + side_in[early]) + last_in[early]
    for part, copy in zip(late, sides):
        copy.wait()
        out_ref[part] = held[part] + side_in[part]


def ring(count, step):
    return [(i, (i + step) % count) for i in range(count)]


def on_device(
    box_points, proxy_directions, point_order, neighbour_boxes, neighbour_places, pivot_inverse
):
    box_count, _, point_count = box_points.shape
    col_count = lax.axis_size("col")
    box_total = lax.axis_size("box")
    group = col_count // box_count
    listed = neighbour_boxes.shape[1]
    entries = listed // group
    width = pivot_inverse.shape[2]
    rest = width * col_count
    skeleton = point_count - rest
    half = rest // group
    share = proxy_directions.shape[1]
    dma = pltpu.SemaphoreType.DMA

    points, proxies, pivots = pl.pallas_call(
        functools.partial(exchange_kernel, box_total, col_count, group, skeleton),
        out_shape=(
            jax.ShapeDtypeStruct((3, box_count, 4, point_count), F32),
            jax.ShapeDtypeStruct((box_count,) + proxy_directions.shape, F32),
            jax.ShapeDtypeStruct((box_count,) + pivot_inverse.shape, F32),
        ),
        in_specs=[HBM] * 4,
        out_specs=(VMEM,) * 3,
        scratch_shapes=[pltpu.VMEM((3, box_count, point_count), F32),
                        pltpu.VMEM(point_order.shape, jnp.int32),
                        dma((4,)), dma((4,)), dma((4,))],
        compiler_params=params(collective_id=0, has_side_effects=True),
        cost_estimate=pl.CostEstimate(flops=4 * 10**9, bytes_accessed=16 * 10**6,
                                      transcendentals=0),
    )(*(pltpu.with_memory_space_constraint(one, pltpu.HBM) for one in (
        jnp.transpose(box_points, (1, 0, 2)), point_order, proxy_directions, pivot_inverse)))

    rows = box_count * share + entries * point_count
    cross = pl.pallas_call(
        functools.partial(tile_kernel, box_total, entries, group, skeleton),
        out_shape=jax.ShapeDtypeStruct((2, skeleton, point_count), F32),
        in_specs=[SMEM, SMEM, VMEM, VMEM],
        out_specs=VMEM,
        scratch_shapes=[
            pltpu.VMEM((DEPTH, rows), BF16),
            pltpu.VMEM((DEPTH, point_count), BF16),
            pltpu.VMEM((2, BLOCK, point_count), F32),
            pltpu.VMEM((2, 2 * BLOCK, 2 * point_count), BF16),
            pltpu.VMEM((skeleton, 2 * point_count), F32),
        ],
        compiler_params=params(),
    )(neighbour_boxes, neighbour_places, points, proxies)
    pairs = [(i, i + 1 - 2 * (i % 2)) for i in range(col_count)]
    cross_in = lax.ppermute(cross, "col", pairs)

    cover = pl.CostEstimate(flops=8 * 10**9, bytes_accessed=16 * 10**6, transcendentals=0)
    right, kept = pl.pallas_call(
        functools.partial(kernel_kernel, box_total, group),
        out_shape=(
            jax.ShapeDtypeStruct((listed // 2 - 1, 2, 2 * skeleton, 2 * skeleton), BF16),
            jax.ShapeDtypeStruct((listed // 2 - 1, 2 * half, 2 * skeleton), F32),
        ),
        in_specs=[SMEM, SMEM, VMEM],
        out_specs=(VMEM, VMEM),
        scratch_shapes=[
            pltpu.VMEM((DEPTH, skeleton + half), BF16),
            pltpu.VMEM((2, skeleton + half, skeleton), F32),
        ],
        compiler_params=params(),
        cost_estimate=cover,
    )(neighbour_boxes, neighbour_places, points)

    solved = pl.pallas_call(
        functools.partial(solve_kernel, group),
        out_shape=jax.ShapeDtypeStruct((2, skeleton, half), F32),
        in_specs=[VMEM] * 2,
        out_specs=VMEM,
        scratch_shapes=[
            pltpu.VMEM((2, skeleton, skeleton + half), F32),
            pltpu.VMEM((2, 256, 2 * (skeleton + half)), BF16),
            pltpu.VMEM((2, 256, 2 * (skeleton + half)), BF16),
        ],
        compiler_params=params(),
    )(cross, cross_in)
    arrived = lax.ppermute(solved, "col", ring(col_count, group))

    strips = skeleton // box_count
    buffer, right_last, kept_last = pl.pallas_call(
        functools.partial(near_kernel, box_total, group),
        out_shape=(
            jax.ShapeDtypeStruct((3 * box_count, 2, strips, skeleton), F32),
            jax.ShapeDtypeStruct((2, 2 * skeleton, 2 * skeleton), BF16),
            jax.ShapeDtypeStruct((2 * half, 2 * skeleton), F32),
        ),
        in_specs=[SMEM, SMEM, VMEM, VMEM, VMEM],
        out_specs=(VMEM,) * 3,
        scratch_shapes=[
            pltpu.VMEM((box_count, DEPTH, skeleton + half), BF16),
            pltpu.VMEM((4, skeleton + half, skeleton), F32),
            pltpu.VMEM((2, 2, 2 * skeleton, 2 * skeleton), BF16),
            pltpu.VMEM((2, 2 * half, 2 * skeleton), F32),
            pltpu.VMEM((4 * half, 2 * skeleton), BF16),
            pltpu.VMEM((listed // 2, 2 * half, 2 * skeleton), F32),
        ],
        compiler_params=params(),
        cost_estimate=cover,
    )(neighbour_boxes, neighbour_places, points, solved, pivots)

    buffer, inter = pl.pallas_call(
        functools.partial(far_kernel, box_total, group),
        out_shape=(
            jax.ShapeDtypeStruct(buffer.shape, F32),
            jax.ShapeDtypeStruct((box_count, 2, width, skeleton), F32),
        ),
        in_specs=[SMEM] + [VMEM] * 8,
        out_specs=(VMEM, VMEM),
        scratch_shapes=[
            pltpu.VMEM((4 * half, 2 * skeleton), BF16),
            pltpu.VMEM((listed // 2, 2 * half, 2 * skeleton), F32),
        ],
        compiler_params=params(),
    )(neighbour_boxes, buffer, right, kept, right_last, kept_last, arrived, solved, pivots)
    interpolation = jnp.swapaxes(inter, 2, 3)

    strip = skeleton // col_count
    block = (box_count, 2, strip, skeleton)
    jobs = (3 * PIECES + 1) * (2 * box_count - 1) + 6
    skeleton_update = pl.pallas_call(
        functools.partial(reduce_kernel, box_total),
        out_shape=jax.ShapeDtypeStruct(block, F32),
        in_specs=[VMEM],
        out_specs=VMEM,
        scratch_shapes=[
            pltpu.VMEM((3,) + block, F32),
            pltpu.VMEM(block, F32),
            pltpu.VMEM(block, F32),
            pltpu.VMEM(block, F32),
            pltpu.VMEM(block, F32),
            pltpu.VMEM(block, F32),
            pltpu.VMEM(block, F32),
            dma((jobs,)),
            dma((jobs,)),
        ],
        compiler_params=params(collective_id=1, has_side_effects=True),
    )(buffer.reshape(3 * box_count, 2, group, strip, skeleton))
    return (interpolation, skeleton_update)


def solution(mesh):
    placed = (
        P("box", None, None),
        P(None, "col"),
        P("box", None),
        P("box", None),
        P("box", None),
        P("box", None, "col"),
    )
    return jax.shard_map(
        on_device,
        mesh=mesh,
        in_specs=placed,
        out_specs=(P("box", None, None, "col"), P("box", None, "col", None)),
        check_vma=False,
    )
```

```python
import functools
import math

import jax
import jax.numpy as jnp
from jax import lax
from jax.experimental import pallas as pl
from jax.experimental.pallas import tpu as pltpu
from jax.sharding import PartitionSpec as P

softening = 0.05
proxy_radius = 1.5
ridge_share = 0.05
NBLK = 32
BLOCK = 256
ROWS = 16
DEPTH = 64
PIECES = 2

SIN = (4.44287959, -7.30781805, 3.59778873, -0.79123822)
COS = (1.41420408, -6.97764206, 5.7152384, -1.72834866)

HBM = pl.BlockSpec(memory_space=pltpu.HBM)
VMEM = pl.BlockSpec(memory_space=pltpu.VMEM)
SMEM = pl.BlockSpec(memory_space=pltpu.SMEM)
MESH = pl.DeviceIdType.MESH
F32 = jnp.float32
BF16 = jnp.bfloat16


def params(**more):
    return pltpu.CompilerParams(vmem_limit_bytes=24 * 1024 * 1024, **more)


def horner(coefficients, z):
    total = coefficients[-1] * z + coefficients[-2]
    for one in coefficients[-3::-1]:
        total = total * z + one
    return total


def kernel_values(square):
    inverse = lax.rsqrt(square)
    turns = square * inverse
    part = turns - lax.round(turns, lax.RoundingMethod.TO_NEAREST_EVEN)
    z = part * part
    amplitude = inverse * (1.0 / (2.0 * math.pi))
    sine = part * horner(SIN, z)
    scaled = amplitude * sine
    return amplitude - scaled * sine, scaled * horner(COS, z)


def three(x):
    high = x.astype(BF16).astype(F32)
    rest = x - high
    mid = rest.astype(BF16).astype(F32)
    return high, mid, rest - mid


def row_three(block, row):
    third = lax.broadcasted_iota(jnp.int32, block.shape, 0) == 3
    return jnp.where(third, row, block)


def norm_of(points):
    return jnp.sum(points * points, axis=0, keepdims=True)


def stacked(groups):
    zero = jnp.zeros_like(groups[0])
    return jnp.concatenate(groups + [zero] * (DEPTH // 8 - len(groups)), axis=0).astype(BF16)


def target_rows(points):
    high, mid, low = three(points)
    n_high, n_mid, n_low = three(norm_of(points))
    return stacked([row_three(high, n_high), row_three(high, n_mid), row_three(mid, n_low),
                    row_three(high, 1.0), row_three(mid, 1.0), row_three(low, 1.0)])


def source_rows(points):
    high, mid, low = three(points)
    norm = norm_of(points) + 4.0 * softening * softening
    n_high, n_mid, n_low = three(norm)
    return stacked([row_three(-2.0 * high, 1.0), row_three(-2.0 * mid, 1.0),
                    row_three(-2.0 * high, 1.0), row_three(-2.0 * low, n_high),
                    row_three(-2.0 * mid, n_mid), row_three(-2.0 * high, n_low)])


def padded(points):
    return jnp.concatenate([points, jnp.zeros_like(points)], axis=0)


def three_rows(points):
    rows = lax.broadcasted_iota(jnp.int32, points.shape, 0)
    return jnp.where(rows < 3, points, 0.0)


def shifted(points, code):
    code = jnp.where(code >= 13, code + 1, code)
    axis_row = lax.broadcasted_iota(jnp.int32, points.shape, 0)
    move = jnp.where(
        axis_row == 0,
        (code // 9 - 1).astype(F32),
        jnp.where(axis_row == 1, ((code // 3) % 3 - 1).astype(F32), (code % 3 - 1).astype(F32)),
    )
    return three_rows(2.0 * (points + (move - 0.5)))


def centred(points):
    return three_rows(2.0 * (points - 0.5))


def slot_of(nb_ref, row, entry, box_count, box_total):
    owner_box = nb_ref[row, entry]
    step = owner_box // box_count - lax.axis_index("box") + 1
    step = jnp.where(step < 0, step + box_total, step)
    step = jnp.where(step >= box_total, step - box_total, step)
    return step * box_count + owner_box % box_count


def dot_tn(a, b):
    return lax.dot_general(a, b, (((0,), (0,)), ((), ())), preferred_element_type=F32)


def meet(peers):
    barrier = pltpu.get_barrier_semaphore()
    for peer in peers:
        pl.semaphore_signal(barrier, inc=1, device_id=peer, device_id_type=MESH)
    return lambda: pl.semaphore_wait(barrier, len(peers))


def send(source, target, sends, recvs, index, peer):
    one = pltpu.make_async_remote_copy(
        src_ref=source, dst_ref=target, send_sem=sends.at[index], recv_sem=recvs.at[index],
        device_id=peer, device_id_type=MESH)
    one.start()
    return one


def exchange_kernel(box_total, col_count, group, skeleton, points_ref, order_ref, proxy_ref,
                    pivot_ref, points_out, proxy_out, pivot_out, points, order, sends, recvs,
                    local):
    me = lax.axis_index("col")
    place = lax.axis_index("box")
    _, box_count, count = points_ref.shape
    after = {"box": lax.rem(place + 1, box_total)}
    before = {"box": lax.rem(place + box_total - 1, box_total)}
    across = {"col": lax.rem(me + group, col_count)}
    mine = me // group
    own = ((points_ref, points), (order_ref, order), (proxy_ref, proxy_out.at[0]),
           (pivot_ref, pivot_out.at[mine]))
    loads = []
    for i, (source, target) in enumerate(own):
        copy = pltpu.make_async_copy(source, target, local.at[i])
        copy.start()
        loads.append(copy)
    arrived = meet([before, after, across])
    for copy in loads:
        copy.wait()
    width = (count - skeleton) // col_count
    for box in range(box_count):
        row = order[box:box + 1, :]
        strips = [row[:, skeleton + s * width:skeleton + (s + 1) * width]
                  for c in range(group) for s in range(c, col_count, group)]
        row = jnp.concatenate([row[:, 0:skeleton]] + strips, axis=1)
        one_hot = (lax.broadcasted_iota(jnp.int32, (count, count), 0) == row).astype(F32)
        whole = jnp.concatenate([points[axis, box:box + 1, :] for axis in range(3)]
                                + [jnp.zeros((5, count), F32)], axis=0)
        rows = jnp.concatenate(list(three(whole)) + [jnp.zeros_like(whole)], axis=0)
        picked = jnp.dot(rows.astype(BF16), one_hot.astype(BF16), preferred_element_type=F32)
        points_out[1, box] = ((picked[0:8] + picked[8:16]) + picked[16:24])[0:4]
    arrived()
    jobs = [
        send(points_out.at[1], points_out.at[0], sends, recvs, 0, after),
        send(points_out.at[1], points_out.at[2], sends, recvs, 1, before),
        send(proxy_ref, proxy_out.at[1], sends, recvs, 2, across),
        send(pivot_ref, pivot_out.at[mine], sends, recvs, 3, across),
    ]
    for copy in jobs:
        copy.wait()


def tile_kernel(box_total, entries, group, skeleton, nb_ref, place_ref, points_ref, proxy_ref,
                cross_ref, targets, sources, squares, tiles, total):
    count = points_ref.shape[3]
    box_count, _, share = proxy_ref.shape
    proxies = box_count * share
    me = lax.axis_index("col")
    box = me // group
    first = lax.rem(me, group) * entries
    sources[...] = source_rows(centred(padded(points_ref[1, box])))
    for d in range(box_count):
        directions = jnp.concatenate([proxy_ref[d], jnp.zeros((5, share), F32)], axis=0)
        targets[:, d * share:(d + 1) * share] = target_rows((2.0 * proxy_radius) * directions)
    for k in range(entries):
        slot = slot_of(nb_ref, box, first + k, box_count, box_total)
        here = shifted(padded(points_ref[slot // box_count, slot % box_count]),
                       place_ref[box, first + k])
        targets[:, proxies + k * count:proxies + (k + 1) * count] = target_rows(here)
    block = tiles.shape[1] // 2

    def measure(base, slot):
        squares[slot] = dot_tn(targets[:, base:base + block], sources[...])

    def evaluate(slot, i):
        inner = slice(i * ROWS, (i + 1) * ROWS)
        lower = slice(block + i * ROWS, block + (i + 1) * ROWS)
        for c in range(0, count, 256):
            here = slice(c, c + 256)
            there = slice(count + c, count + c + 256)
            real, imag = kernel_values(squares[slot, inner, here])
            real = real.astype(BF16)
            imag = imag.astype(BF16)
            tiles[slot, inner, here] = real
            tiles[slot, inner, there] = imag
            tiles[slot, lower, here] = imag
            tiles[slot, lower, there] = -real

    def gather(slot, left, c):
        here = slice(c, c + 256)
        total[:, here] += plain(left, tiles[slot, :, here])

    def stage(ahead, now, before):
        measure(*ahead)
        steps = block // ROWS
        pieces = 2 * count // 256
        left = None if before is None else jnp.transpose(tiles[before, :, 0:skeleton])
        for i in range(steps):
            if left is not None and i % (steps // pieces) == 0:
                gather(before, left, i // (steps // pieces) * 256)
            evaluate(now, i)

    total[...] = jnp.zeros_like(total)
    blocks = proxies // block
    measure(0, 0)
    for i in range(blocks):
        stage(((i + 1) * block, (i + 1) % 2), i % 2, (i + 1) % 2 if i else None)
    last = blocks + entries * (count // block) - 1
    for i in range(blocks, last + 1):
        stage((min(i + 1, last) * block, (i + 1) % 2), i % 2, (i + 1) % 2)
    end = last % 2
    left = jnp.transpose(tiles[end, :, 0:skeleton])
    for c in range(0, 2 * count, 256):
        gather(end, left, c)
    for p in range(2):
        cross_ref[p] = total[:, p * count:(p + 1) * count]


def lanes(block, k):
    return jnp.take_along_axis(block, jnp.full(block.shape, k, jnp.int32), axis=1)


def across_rows(block, k):
    return jnp.broadcast_to(block[k:k + 1, :], block.shape)


def block_inverse(re, im, start, home):
    count = len(re)
    shape = re[0].shape
    lane = lax.broadcasted_iota(jnp.int32, shape, 1)
    sub = lax.broadcasted_iota(jnp.int32, shape, 0)
    inside = (lane >= start) & (lane < start + 8 * count)
    re = [jnp.where(inside, block, jnp.where(lane - home == sub + 8 * v, 1.0, 0.0))
          for v, block in enumerate(re)]
    im = [jnp.where(inside, block, 0.0) for block in im]
    for r in range(count):
        order = [r] + [v for v in range(count) if v > r] + list(range(r))
        spread = {}
        for v in order:
            for j in range(8):
                k = start + 8 * r + j
                spread[v, j] = (lanes(re[v], k), lanes(im[v], k))
        cols = {j: spread[r, j] for j in range(8)}
        cols["row"] = (re[r], im[r])
        for t in range(0, 8, 2):
            (ar, ai), (cr, ci) = cols.pop(t), cols.pop(t + 1)
            a, d = across_rows(ar, t), across_rows(cr, t + 1)
            br, bi = across_rows(cr, t), across_rows(ci, t)
            scale = 1.0 / (a * d - (br * br + bi * bi))
            a, d, br, bi = a * scale, d * scale, br * scale, bi * scale
            at, on = sub == t, sub == t + 1
            here = at | on
            e0r = jnp.where(at, -d, jnp.where(on, br, ar * d - (cr * br + ci * bi)))
            e0i = jnp.where(at, 0.0, jnp.where(on, -bi, ai * d - (ci * br - cr * bi)))
            e1r = jnp.where(at, br, jnp.where(on, -a, cr * a - (ar * br - ai * bi)))
            e1i = jnp.where(at, bi, jnp.where(on, 0.0, ci * a - (ar * bi + ai * br)))
            for key, (xr, xi) in cols.items():
                x0r, x0i = across_rows(xr, t), across_rows(xi, t)
                x1r, x1i = across_rows(xr, t + 1), across_rows(xi, t + 1)
                lessr = (e0r * x0r - e0i * x0i) + (e1r * x1r - e1i * x1i)
                lessi = (e0r * x0i + e0i * x0r) + (e1r * x1i + e1i * x1r)
                cols[key] = (jnp.where(here, 0.0, xr) - lessr, jnp.where(here, 0.0, xi) - lessi)
            if t < 6:
                yield None
        re[r], im[r] = cols["row"]
        rows = [(across_rows(re[r], j), across_rows(im[r], j)) for j in range(8)]
        for v in order[1:]:
            lessr = [spread[v, j][0] * rows[j][0] - spread[v, j][1] * rows[j][1]
                     for j in range(8)]
            lessi = [spread[v, j][0] * rows[j][1] + spread[v, j][1] * rows[j][0]
                     for j in range(8)]
            re[v] = re[v] - summed(lessr)
            im[v] = im[v] - summed(lessi)
        yield jnp.concatenate(re, axis=0), jnp.concatenate(im, axis=0)


def summed(terms):
    while len(terms) > 1:
        terms = [terms[i] + terms[i + 1] for i in range(0, len(terms), 2)]
    return terms[0]


def plain(a, b):
    return jnp.dot(a, b, preferred_element_type=F32)


def solve_kernel(group, cross_ref, cross_in, x_ref, mat, head, tail):
    n = x_ref.shape[1]
    width = x_ref.shape[2]
    nb = NBLK
    side = lax.rem(lax.axis_index("col"), group)
    diagonal = lax.broadcasted_iota(jnp.int32, (128, 128), 0) == lax.broadcasted_iota(
        jnp.int32, (128, 128), 1
    )
    gram = cross_ref[:, :, 0:n] + cross_in[:, :, 0:n]
    ridge = 0.0
    for c in range(0, n, 128):
        ridge = ridge + jnp.where(diagonal, gram[0, c:c + 128, c:c + 128], 0.0)
    ridge = ridge_share * jnp.sum(ridge) / n
    mat[:, :, 0:n] = gram
    for c in range(0, n, 128):
        here = slice(c, c + 128)
        mat[0, here, here] = gram[0, here, here] + jnp.where(diagonal, ridge, 0.0)
    mine = pl.ds(pl.multiple_of(n + side * width, 128), width)
    mat[:, :, n:] = cross_ref[:, :, mine] + cross_in[:, :, mine]
    head[...] = jnp.zeros_like(head)
    tail[...] = jnp.zeros_like(tail)

    def pick(block):
        return [block[8 * v:8 * v + 8] for v in range(nb // 8)]

    def put(ref, at, w, re, im):
        where = slice(256 * w, 256 * w + 256)
        for base, block in ((at, [re, im]), (128 + at, [-im, re])):
            high, rest = split(jnp.concatenate(block, axis=1))
            ref[0, base:base + nb, where] = high
            ref[1, base:base + nb, where] = rest

    def clear(ref, at):
        for base in (at, 128 + at):
            ref[:, base:base + nb, :] = jnp.zeros((2, nb, ref.shape[2]), BF16)

    def doubled(re, im):
        return jnp.concatenate(split(jnp.concatenate([re, im], axis=1)), axis=0)

    def product(left, ref, w):
        where = slice(256 * w, 256 * w + 256)
        half = left.shape[0] // 2
        both = plain(left, ref[0, :, where])
        return both[0:half] + (both[half:] + plain(left[0:half], ref[1, :, where]))

    for step in block_inverse(pick(mat[0, 0:nb, 0:128]), pick(mat[1, 0:nb, 0:128]), 0, nb):
        found = step or None
    for j in range(n // nb):
        rows = slice(j * nb, (j + 1) * nb)
        after = slice((j + 1) * nb, (j + 2) * nb)
        q = (j * nb) // 128 * 128
        at = j * nb - q
        home = (at + nb) % 128
        windows = list(range((j + 1) * nb // 128, mat.shape[2] // 128))
        factor = doubled(*found)
        left = doubled(mat[0, :, q:q + 128], mat[1, :, q:q + 128])
        held = {}

        def solve(w):
            here = slice(128 * w, 128 * w + 128)
            put(head, home, w, mat[0, rows, here], mat[1, rows, here])
            held[w] = product(factor, head, w)
            put(tail, at, w, held[w][:, 0:128], held[w][:, 128:])

        def change(w):
            here = slice(128 * w, 128 * w + 128)
            less = product(left, tail, w)
            mat[0, :, here] = mat[0, :, here] - less[:, 0:128]
            mat[1, :, here] = mat[1, :, here] - less[:, 128:]
            mat[0, rows, here] = held[w][:, 0:128]
            mat[1, rows, here] = held[w][:, 128:]

        first = windows[0]
        solve(first)
        pivots = iter(())
        if (j + 1) * nb < n:
            here = slice(128 * first, 128 * first + 128)
            ahead = jnp.concatenate([left[after], left[n + (j + 1) * nb:n + (j + 2) * nb]], axis=0)
            less = product(ahead, tail, first)
            to = (j + 1) * nb % 128
            pivots = block_inverse(pick(mat[0, after, here] - less[:, 0:128]),
                                   pick(mat[1, after, here] - less[:, 128:]),
                                   to, (to + nb) % 128)
        tasks = [functools.partial(solve, w) for w in windows[1:]]
        tasks += [functools.partial(change, w) for w in windows]
        tasks.append(functools.partial(clear, head, home))
        tasks.append(functools.partial(clear, tail, at))
        steps = nb // 2
        done = 0
        for i, task in enumerate(tasks):
            task()
            upto = (i + 1) * steps // len(tasks)
            for _ in range(upto - done):
                found = next(pivots, None) or found
            done = upto
        for step in pivots:
            found = step or found
    x_ref[...] = mat[:, :, n:]


def split(x):
    high = x.astype(BF16)
    return high, (x - high.astype(F32)).astype(BF16)


def left_side(xr, xi):
    return jnp.concatenate(split(jnp.concatenate(
        [jnp.concatenate([xr, -xi], axis=1), jnp.concatenate([xi, xr], axis=1)], axis=0)), axis=0)


def pivot_columns(pivot_ref, box):
    pieces = range(pivot_ref.shape[0])
    rows = [jnp.concatenate([pivot_ref[c, box, p:p + 1, :] for c in pieces], axis=1)
            for p in range(2)]
    return [jnp.transpose(jnp.broadcast_to(row, (128, row.shape[1]))) for row in rows]


def quarters(product):
    rows, cols = product.shape[0] // 2, product.shape[1] // 2
    return ((product[:rows, :cols] + product[:rows, cols:])
            + (product[rows:, :cols] + product[rows:, cols:]))


def form(turned, right, rest, blocks, pair):
    half = turned.shape[0] // 2
    both = plain(turned[...], right[0])
    blocks[pair] = rest - (both[0:half] + (both[half:] + plain(turned[0:half, :], right[1])))


def fold(blocks, pair, i, row, pivots, out_ref, to):
    qr, qi = pivots
    width = qr.shape[0]
    n = blocks.shape[2] // 2
    mine = blocks[pair, :, pl.ds(pl.multiple_of(i * n + row, 128), qr.shape[1])]
    br, bi = mine[0:width], mine[width:]
    wr = jnp.transpose(br * qr - bi * qi)
    wi = jnp.transpose(br * qi + bi * qr)
    upper = jnp.concatenate([jnp.concatenate([wr, -wi], axis=1),
                             jnp.concatenate([wi, wr], axis=1)], axis=0)
    whole = jnp.concatenate(split(blocks[pair, :, i * n:(i + 1) * n]), axis=1)
    update = quarters(plain(jnp.concatenate(split(upper), axis=0), whole))
    half = update.shape[0] // 2
    out_ref[to, 0] = out_ref[to, 0] - update[0:half]
    out_ref[to, 1] = out_ref[to, 1] - update[half:]


def first_row(group, count):
    return lax.axis_index("col") // group * count


def entry_squares(box_total, nb_ref, place_ref, points_ref, which, k, n, sources):
    box_count = points_ref.shape[1]
    place = slot_of(nb_ref, which, k, box_count, box_total)
    here = shifted(padded(points_ref[place // box_count, place % box_count]),
                   place_ref[which, k])
    return dot_tn(sources[...], target_rows(here[:, 0:n]))


def evaluate(squares, n, width, right_at, rest_at, i, part=0, parts=1):
    rows = n + width
    for r in range(part * rows // parts, (part + 1) * rows // parts, ROWS):
        for c in range(0, n, 128):
            here = slice(i * n + c, i * n + c + 128)
            for p, value in enumerate(kernel_values(squares[r:r + ROWS, c:c + 128])):
                if r < n:
                    at = slice(p * n + r, p * n + r + ROWS)
                    right_at[0, at, here], right_at[1, at, here] = split(value)
                else:
                    rest_at[p * width + r - n:p * width + r - n + ROWS, here] = value


def half_sources(points, side, group, n, width):
    whole = source_rows(centred(padded(points)))
    half = whole[:, n:n + width]
    for c in range(1, group):
        half = jnp.where(side == c, whole[:, n + c * width:n + (c + 1) * width], half)
    return jnp.concatenate([whole[:, 0:n], half], axis=1)


def kernel_kernel(box_total, group, nb_ref, place_ref, points_ref, right_ref, rest_ref, sources,
                  squares):
    pairs, width, n = rest_ref.shape
    width, n = width // 2, n // 2
    me = lax.axis_index("col")
    fed = 1 - me // group
    sources[...] = half_sources(points_ref[1, fed], lax.rem(me, group), group, n, width)

    def measure(k, slot):
        squares[slot] = entry_squares(box_total, nb_ref, place_ref, points_ref, fed, k, n, sources)

    measure(0, 0)
    for k in range(2 * pairs):
        if k + 1 < 2 * pairs:
            measure(k + 1, (k + 1) % 2)
        evaluate(squares.at[k % 2], n, width, right_ref.at[k // 2], rest_ref.at[k // 2], k % 2)


def near_kernel(box_total, group, nb_ref, place_ref, points_ref, x_ref, pivot_ref,
                out_ref, right_ref, rest_ref, sources, squares, right, rest, turned, blocks):
    n = x_ref.shape[1]
    width = x_ref.shape[2]
    box_count = points_ref.shape[1]
    entries = nb_ref.shape[1]
    me = lax.axis_index("col")
    box = me // group
    for i, which in enumerate((box, 1 - box)):
        sources[i] = half_sources(points_ref[1, which], lax.rem(me, group), group, n, width)

    def measure(k):
        if k < entries + 2:
            other = k >= entries
            squares[k % 4] = entry_squares(box_total, nb_ref, place_ref, points_ref,
                                           1 - box if other else box, k - 2 if other else k, n,
                                           sources.at[int(other)])

    def values(k, part, parts):
        at = k // 2 % 2
        into = (right.at[at], rest.at[at]) if k < entries else (right_ref, rest_ref)
        evaluate(squares.at[k % 4], n, width, *into, k % 2, part, parts)

    for k in range(4):
        measure(k)
    out_ref[...] = jnp.zeros_like(out_ref)
    values(0, 0, 1)
    turned[...] = left_side(jnp.transpose(x_ref[0]), jnp.transpose(x_ref[1]))
    pivots = pivot_columns(pivot_ref, box)
    row = first_row(group, out_ref.shape[2])
    values(1, 0, 1)
    pairs = entries // 2
    for pair in range(pairs + 1):
        if pair < pairs:
            form(turned, right.at[pair % 2], rest[pair % 2], blocks, pair)
        for i in range(2):
            k = 2 * pair + 2 + i
            if k < entries + 2:
                values(k, 0, 2)
            if pair:
                done = 2 * pair - 2 + i
                fold(blocks, pair - 1, i, row, pivots, out_ref,
                     slot_of(nb_ref, box, done, box_count, box_total))
            if k < entries + 2:
                values(k, 1, 2)
            measure(k + 2)


def far_kernel(box_total, group, nb_ref, buf_ref, right_ref, rest_ref, right_last, rest_last,
               x_ref, mine_ref, pivot_ref, out_ref, inter_hbm, turned, blocks, inter_ref, done):
    pairs = rest_ref.shape[0] + 1
    me = lax.axis_index("col")
    box = me // group
    fed = 1 - box
    box_count = pivot_ref.shape[1]
    strip = inter_ref.shape[2]
    theirs = [jnp.transpose(x_ref[p]) for p in range(2)]
    turned[...] = left_side(*theirs)
    for p in range(2):
        for block, where in ((jnp.transpose(mine_ref[p]), box), (theirs[p], fed)):
            piece = block[0:strip]
            for c in range(1, block.shape[0] // strip):
                piece = jnp.where(box == c, block[c * strip:(c + 1) * strip], piece)
            inter_ref[where, p] = piece
    copy = pltpu.make_async_copy(inter_ref, inter_hbm, done.at[0])
    copy.start()
    pivots = pivot_columns(pivot_ref, fed)
    row = first_row(group, out_ref.shape[2])
    for pair in range(pairs + 1):
        if pair < pairs - 1:
            form(turned, right_ref.at[pair], rest_ref[pair], blocks, pair)
        elif pair < pairs:
            form(turned, right_last, rest_last[...], blocks, pair)
        if not pair:
            out_ref[...] = buf_ref[...]
        for i in range(2):
            if pair:
                fold(blocks, pair - 1, i, row, pivots, out_ref,
                     slot_of(nb_ref, fed, 2 * pair - 2 + i, box_count, box_total))
    copy.wait()


def reduce_kernel(box_total, buf_ref, out_ref, pair_in, line_out, line_in, side_out, side_in,
                  last_in, held, sends, recvs):
    me = lax.axis_index("col")
    place = lax.axis_index("box")
    side = lax.rem(me, 2)
    odd = lax.rem(place, 2)
    near = {"col": me + 1 - 2 * side}
    relay = {"box": lax.rem(place + box_total + 4 * odd - 2, box_total)}
    source = {"box": lax.rem(place + box_total + 2 - 4 * odd, box_total)}
    twin = {"box": place + 1 - 2 * odd}
    meet([near, relay, source, twin])()
    box_count, _, strip, _ = out_ref.shape
    order = (2 * odd, 2 - 2 * odd, 1)
    piece = strip // PIECES
    early = (box_count - 1, 1)
    wholes = [(d, p) for d in range(box_count) for p in range(2) if (d, p) != early]
    late = [part + (pl.ds(i * piece, piece),) for part in wholes for i in range(PIECES)]
    count = iter(range(sends.shape[0]))

    def pair(g, part):
        return send(buf_ref.at[(order[g] * box_count + part[0], part[1], 1 - side) + part[2:]],
                    pair_in.at[(g,) + part], sends, recvs, next(count), near)

    def both(g, part):
        return (buf_ref[(order[g] * box_count + part[0], part[1], side) + part[2:]]
                + pair_in[(g,) + part])

    def forward(source_ref, target_ref, part, peer):
        return send(source_ref.at[part], target_ref.at[part], sends, recvs, next(count), peer)

    line_pairs = [pair(0, part) for part in late]
    line_early, side_early = pair(0, early), pair(1, early)
    side_pairs = [pair(1, part) for part in wholes]
    own_pair = send(buf_ref.at[box_count:2 * box_count, :, 1 - side], pair_in.at[2], sends, recvs,
                    next(count), near)
    lines, sides = [], []
    for part, copy in zip(late, line_pairs):
        copy.wait()
        line_out[part] = both(0, part)
        lines.append(forward(line_out, line_in, part, relay))
    line_early.wait()
    line_out[early] = both(0, early)
    turn = forward(line_out, line_in, early, twin)
    side_early.wait()
    side_out[early] = both(1, early)
    direct = forward(side_out, side_in, early, twin)
    for part, copy in zip(wholes, side_pairs):
        copy.wait()
        held[part] = both(1, part)
    for i, (part, copy) in enumerate(zip(late, lines)):
        copy.wait()
        side_out[part] = held[part] + line_in[part]
        sides.append(forward(side_out, side_in, part, twin))
        if i == 1:
            turn.wait()
            onward = forward(line_in, last_in, early, source)
    own_pair.wait()
    for d in range(box_count):
        for p in range(2):
            held[d, p] = both(2, (d, p))
    direct.wait()
    onward.wait()
    out_ref[early] = (held[early] + side_in[early]) + last_in[early]
    for part, copy in zip(late, sides):
        copy.wait()
        out_ref[part] = held[part] + side_in[part]


def ring(count, step):
    return [(i, (i + step) % count) for i in range(count)]


def on_device(
    box_points, proxy_directions, point_order, neighbour_boxes, neighbour_places, pivot_inverse
):
    box_count, _, point_count = box_points.shape
    col_count = lax.axis_size("col")
    box_total = lax.axis_size("box")
    group = col_count // box_count
    listed = neighbour_boxes.shape[1]
    entries = listed // group
    width = pivot_inverse.shape[2]
    rest = width * col_count
    skeleton = point_count - rest
    half = rest // group
    share = proxy_directions.shape[1]
    dma = pltpu.SemaphoreType.DMA

    points, proxies, pivots = pl.pallas_call(
        functools.partial(exchange_kernel, box_total, col_count, group, skeleton),
        out_shape=(
            jax.ShapeDtypeStruct((3, box_count, 4, point_count), F32),
            jax.ShapeDtypeStruct((box_count,) + proxy_directions.shape, F32),
            jax.ShapeDtypeStruct((box_count,) + pivot_inverse.shape, F32),
        ),
        in_specs=[HBM] * 4,
        out_specs=(VMEM,) * 3,
        scratch_shapes=[pltpu.VMEM((3, box_count, point_count), F32),
                        pltpu.VMEM(point_order.shape, jnp.int32),
                        dma((4,)), dma((4,)), dma((4,))],
        compiler_params=params(collective_id=0, has_side_effects=True),
        cost_estimate=pl.CostEstimate(flops=4 * 10**9, bytes_accessed=16 * 10**6,
                                      transcendentals=0),
    )(*(pltpu.with_memory_space_constraint(one, pltpu.HBM) for one in (
        jnp.transpose(box_points, (1, 0, 2)), point_order, proxy_directions, pivot_inverse)))

    rows = box_count * share + entries * point_count
    cross = pl.pallas_call(
        functools.partial(tile_kernel, box_total, entries, group, skeleton),
        out_shape=jax.ShapeDtypeStruct((2, skeleton, point_count), F32),
        in_specs=[SMEM, SMEM, VMEM, VMEM],
        out_specs=VMEM,
        scratch_shapes=[
            pltpu.VMEM((DEPTH, rows), BF16),
            pltpu.VMEM((DEPTH, point_count), BF16),
            pltpu.VMEM((2, BLOCK, point_count), F32),
            pltpu.VMEM((2, 2 * BLOCK, 2 * point_count), BF16),
            pltpu.VMEM((skeleton, 2 * point_count), F32),
        ],
        compiler_params=params(),
    )(neighbour_boxes, neighbour_places, points, proxies)
    pairs = [(i, i + 1 - 2 * (i % 2)) for i in range(col_count)]
    cross_in = lax.ppermute(cross, "col", pairs)

    cover = pl.CostEstimate(flops=8 * 10**9, bytes_accessed=16 * 10**6, transcendentals=0)
    right, kept = pl.pallas_call(
        functools.partial(kernel_kernel, box_total, group),
        out_shape=(
            jax.ShapeDtypeStruct((listed // 2 - 1, 2, 2 * skeleton, 2 * skeleton), BF16),
            jax.ShapeDtypeStruct((listed // 2 - 1, 2 * half, 2 * skeleton), F32),
        ),
        in_specs=[SMEM, SMEM, VMEM],
        out_specs=(VMEM, VMEM),
        scratch_shapes=[
            pltpu.VMEM((DEPTH, skeleton + half), BF16),
            pltpu.VMEM((2, skeleton + half, skeleton), F32),
        ],
        compiler_params=params(),
        cost_estimate=cover,
    )(neighbour_boxes, neighbour_places, points)

    solved = pl.pallas_call(
        functools.partial(solve_kernel, group),
        out_shape=jax.ShapeDtypeStruct((2, skeleton, half), F32),
        in_specs=[VMEM] * 2,
        out_specs=VMEM,
        scratch_shapes=[
            pltpu.VMEM((2, skeleton, skeleton + half), F32),
            pltpu.VMEM((2, 256, 2 * (skeleton + half)), BF16),
            pltpu.VMEM((2, 256, 2 * (skeleton + half)), BF16),
        ],
        compiler_params=params(),
    )(cross, cross_in)
    arrived = lax.ppermute(solved, "col", ring(col_count, group))

    strips = skeleton // box_count
    buffer, right_last, kept_last = pl.pallas_call(
        functools.partial(near_kernel, box_total, group),
        out_shape=(
            jax.ShapeDtypeStruct((3 * box_count, 2, strips, skeleton), F32),
            jax.ShapeDtypeStruct((2, 2 * skeleton, 2 * skeleton), BF16),
            jax.ShapeDtypeStruct((2 * half, 2 * skeleton), F32),
        ),
        in_specs=[SMEM, SMEM, VMEM, VMEM, VMEM],
        out_specs=(VMEM,) * 3,
        scratch_shapes=[
            pltpu.VMEM((box_count, DEPTH, skeleton + half), BF16),
            pltpu.VMEM((4, skeleton + half, skeleton), F32),
            pltpu.VMEM((2, 2, 2 * skeleton, 2 * skeleton), BF16),
            pltpu.VMEM((2, 2 * half, 2 * skeleton), F32),
            pltpu.VMEM((4 * half, 2 * skeleton), BF16),
            pltpu.VMEM((listed // 2, 2 * half, 2 * skeleton), F32),
        ],
        compiler_params=params(),
        cost_estimate=cover,
    )(neighbour_boxes, neighbour_places, points, solved, pivots)

    buffer, inter = pl.pallas_call(
        functools.partial(far_kernel, box_total, group),
        out_shape=(
            jax.ShapeDtypeStruct(buffer.shape, F32),
            jax.ShapeDtypeStruct((box_count, 2, width, skeleton), F32),
        ),
        in_specs=[SMEM] + [VMEM] * 8,
        out_specs=(VMEM, HBM),
        scratch_shapes=[
            pltpu.VMEM((4 * half, 2 * skeleton), BF16),
            pltpu.VMEM((listed // 2, 2 * half, 2 * skeleton), F32),
            pltpu.VMEM((box_count, 2, width, skeleton), F32),
            dma((1,)),
        ],
        compiler_params=params(),
    )(neighbour_boxes, buffer, right, kept, right_last, kept_last, arrived, solved, pivots)
    interpolation = jnp.swapaxes(inter, 2, 3)

    strip = skeleton // col_count
    block = (box_count, 2, strip, skeleton)
    jobs = (3 * PIECES + 1) * (2 * box_count - 1) + 6
    skeleton_update = pl.pallas_call(
        functools.partial(reduce_kernel, box_total),
        out_shape=jax.ShapeDtypeStruct(block, F32),
        in_specs=[VMEM],
        out_specs=VMEM,
        scratch_shapes=[
            pltpu.VMEM((3,) + block, F32),
            pltpu.VMEM(block, F32),
            pltpu.VMEM(block, F32),
            pltpu.VMEM(block, F32),
            pltpu.VMEM(block, F32),
            pltpu.VMEM(block, F32),
            pltpu.VMEM(block, F32),
            dma((jobs,)),
            dma((jobs,)),
        ],
        compiler_params=params(collective_id=1, has_side_effects=True),
    )(buffer.reshape(3 * box_count, 2, group, strip, skeleton))
    return (interpolation, skeleton_update)


def solution(mesh):
    placed = (
        P("box", None, None),
        P(None, "col"),
        P("box", None),
        P("box", None),
        P("box", None),
        P("box", None, "col"),
    )
    return jax.shard_map(
        on_device,
        mesh=mesh,
        in_specs=placed,
        out_specs=(P("box", None, None, "col"), P("box", None, "col", None)),
        check_vma=False,
    )
```
